32 devices in a mesh: groups: 2 (over y), ctx: 4 (over z), segment: 2 (over x), head: 2 (over core).
Axes of the slice: x: 2, y: 2, z: 4, core: 2. Of those that a mesh axis runs over, the one named last changes fastest.
Arguments:
- queries: bfloat16 [4, 2048, 4096], P(('groups', 'segment'), 'ctx', 'head'), parts along dimension 0, may hold values from -16 to 16
- span_key_values: bfloat16 [4, 2048, 2, 1024], P(('groups', 'segment'), 'ctx', None, 'head'), parts along dimension 0, may hold values from -6 to 6
- key_value_cache: bfloat16 [4, 16384, 2, 1024], P(('groups', 'segment'), 'ctx', None, 'head'), parts along dimension 0, may hold values from -12 to 12
- chosen: int32 [4, 4, 8, 8], P(('groups', 'segment'), None, 'head'), parts along dimension 0, may hold values from 0 to 31, as said below
- offset: int32 [4], P(('groups', 'segment')), parts along dimension 0, may hold values from 8192 to 16384, as said below
Outputs:
- handed: bfloat16 [4, 2048, 4096], P(('groups', 'segment'), 'ctx', 'head'), parts along dimension 0
The draws below stay inside these ranges and needn't reach their ends.
There are 2 independent parts, one for each index of `groups`. The reference program is written for one: setup_inputs(seed, part) draws one part's arguments, and reference() takes and returns one part's arrays. A program takes and returns all parts, laid end to end along the dimension named above; each array names one. Nothing has to cross between parts.
Inputs may be any that keep to these rules, and one draw needn't show every extreme that they name: `offset`: the first section's span starts at 16384; every other section's at 512 times a whole number from 16 to 32. `chosen`: for a section whose span starts at o, each query block and KV head names 8 different cache blocks below o / 512, among them block 0 and block o / 512 - 1.
All inputs are finite; a program needn't handle non-finite values.
Results may differ from the reference program's by a relative error of at most 0.0085.
Values may be sent and summed in bfloat16 or wider, within the bound.
A program may use at most 128 MiB of HBM per device.

```python
import jax
import jax.numpy as jnp
from jax import lax

HEAD_SIZE = 128
QUERY_HEADS = 32
VALUE_HEADS = 8
BLOCK_TOKENS = 512
CHOSEN_BLOCKS = 8
QUERY_BLOCKS = 4
CACHE_BLOCKS = 32
SPAN_TOKENS = 2048
CACHE_SLOTS = 16384
N_SEGMENT = 2


def section_blocks(key):
    drawn = jax.random.randint(jax.random.fold_in(key, 101), (N_SEGMENT,), CACHE_BLOCKS // 2, CACHE_BLOCKS + 1)
    leading = jnp.arange(N_SEGMENT) == 0
    return jnp.where(leading, CACHE_BLOCKS, drawn).astype(jnp.int32)


def draw_offset(key, part):
    return (section_blocks(key) * BLOCK_TOKENS).astype(jnp.int32)


def draw_chosen(key, part):
    valid_mask = section_blocks(key)[:, None, None, None]
    index = jnp.arange(CACHE_BLOCKS, dtype=jnp.int32)
    random_jitter = jax.random.randint(jax.random.fold_in(key, 202), (N_SEGMENT, QUERY_BLOCKS, VALUE_HEADS, CACHE_BLOCKS), 0, 2 ** 20)
    priority = random_jitter * CACHE_BLOCKS + index
    usable = (index >= 1) & (index < valid_mask - 1)
    priority = jnp.where(usable, priority, -1 - index)
    _, picked = lax.top_k(priority, CHOSEN_BLOCKS - 2)
    zero_column = jnp.zeros((N_SEGMENT, QUERY_BLOCKS, VALUE_HEADS, 1), jnp.int32)
    newest_entry = jnp.broadcast_to(valid_mask - 1, (N_SEGMENT, QUERY_BLOCKS, VALUE_HEADS, 1)).astype(jnp.int32)
    joined = jnp.concatenate([zero_column, newest_entry, picked.astype(jnp.int32)], axis=-1)
    ordering_jitter = jax.random.randint(jax.random.fold_in(key, 303), (N_SEGMENT, QUERY_BLOCKS, VALUE_HEADS, CHOSEN_BLOCKS), 0, 2 ** 20) * CHOSEN_BLOCKS + jnp.arange(CHOSEN_BLOCKS, dtype=jnp.int32)
    order = jnp.argsort(ordering_jitter, axis=-1, stable=True)
    return jnp.take_along_axis(joined, order, axis=-1).astype(jnp.int32)


def draw_queries(key, part):
    array_shape = (N_SEGMENT, SPAN_TOKENS, QUERY_HEADS * HEAD_SIZE)
    drawn = jax.random.normal(jax.random.fold_in(key, 1), array_shape, jnp.float32) * 2.5
    drawn = jnp.clip(drawn, -15.0, 15.0)
    return drawn.astype(jnp.bfloat16)


def draw_key_value_cache(key, part):
    array_shape = (N_SEGMENT, CACHE_SLOTS, 2, VALUE_HEADS * HEAD_SIZE)
    drawn = jnp.clip(jax.random.normal(jax.random.fold_in(key, 5), array_shape, jnp.float32), -6.0, 6.0)
    factor = jnp.where(jnp.arange(2) == 0, 1.0, 2.0)[None, None, :, None]
    drawn = drawn * factor
    return drawn.astype(jnp.bfloat16)


def levels(stream_key, extent, shards, least, high):
    level = 1.0
    for axis_at, parts in shards:
        draws = jax.random.uniform(jax.random.fold_in(jax.random.fold_in(stream_key, 6), axis_at), (parts,), jnp.float32, least / len(shards), high / len(shards))
        level = level * jnp.repeat(jnp.exp(draws), extent[axis_at] // parts).reshape((-1,) + (1,) * (len(extent) - 1 - axis_at))
    return level


def bell_draw(rng, dims, width, most, shards=(), kind=jnp.bfloat16):
    result = jax.random.normal(rng, dims, jnp.float32) * width
    if len(shards) > 0:
        result = levels(rng, dims, shards, -0.22, 0.18) * result
    return jnp.clip(result, min=-most, max=most).astype(kind)


def setup_inputs(seed: int = 0, part: int = 0) -> dict:
    key_of = jax.random.split(jax.random.key(seed), 6)
    part_keys = jax.random.split(jax.random.fold_in(key_of[5], part), 6)
    queries = draw_queries(jax.random.fold_in(jax.random.fold_in(key_of[5], part), 71), part)
    span_key_values = bell_draw(part_keys[1], (N_SEGMENT, SPAN_TOKENS, 2, VALUE_HEADS * HEAD_SIZE), 1.0, 6.0, ((0, 2), (1, 4), (3, 2)))
    key_value_cache = draw_key_value_cache(jax.random.fold_in(jax.random.fold_in(key_of[5], part), 71), part)
    chosen = draw_chosen(jax.random.fold_in(jax.random.fold_in(key_of[5], part), 71), part)
    offset = draw_offset(jax.random.fold_in(jax.random.fold_in(key_of[5], part), 71), part)
    return dict(queries=queries, span_key_values=span_key_values, key_value_cache=key_value_cache, chosen=chosen, offset=offset)


ROPE_BASE = 500000.0


def apply_rotary(values, token_positions):
    half_dim = values.shape[-1] // 2
    frequencies = ROPE_BASE ** (-(2.0 * jnp.arange(half_dim, dtype=jnp.float32)) / values.shape[-1])
    angles = token_positions[:, None] * frequencies[None, :]
    cosine = jnp.cos(angles)[:, None, :]
    sine_part = jnp.sin(angles)[:, None, :]
    widened = values.astype(jnp.float32)
    first_half = widened[..., :half_dim]
    second_half = widened[..., half_dim:]
    joined = jnp.concatenate([first_half * cosine - second_half * sine_part, second_half * cosine + first_half * sine_part], axis=-1)
    return joined.astype(jnp.bfloat16)


def reference(queries, span_key_values, key_value_cache, chosen, offset):
    per_value_head = QUERY_HEADS // VALUE_HEADS
    score_scale = HEAD_SIZE ** -0.5
    results = []
    for layer_section in range(N_SEGMENT):
        token_positions = (offset[layer_section] + jnp.arange(SPAN_TOKENS, dtype=jnp.int32)).astype(jnp.float32)
        rot_query = apply_rotary(queries[layer_section].reshape(SPAN_TOKENS, QUERY_HEADS, HEAD_SIZE), token_positions)
        rotated_key_rows = apply_rotary(span_key_values[layer_section, :, 0].reshape(SPAN_TOKENS, VALUE_HEADS, HEAD_SIZE), token_positions)
        fresh_values = span_key_values[layer_section, :, 1].reshape(SPAN_TOKENS, VALUE_HEADS, HEAD_SIZE)
        stored_entries = key_value_cache[layer_section].reshape(CACHE_BLOCKS, BLOCK_TOKENS, 2, VALUE_HEADS, HEAD_SIZE)
        picked_ids = chosen[layer_section]

        def attend_single_item(index_of_item):
            index_of_item = index_of_item.astype(jnp.int32)
            index_of_block = (index_of_item // VALUE_HEADS).astype(jnp.int32)
            index_of_head = (index_of_item % VALUE_HEADS).astype(jnp.int32)
            zero_index = jnp.zeros((), jnp.int32)
            block_ids = picked_ids[index_of_block, index_of_head]
            fetched = jnp.take(stored_entries, block_ids, axis=0)
            fetched = lax.dynamic_index_in_dim(fetched, index_of_head, axis=3, keepdims=False)
            sel_keys = fetched[:, :, 0].reshape(CHOSEN_BLOCKS * BLOCK_TOKENS, HEAD_SIZE)
            sel_values = fetched[:, :, 1].reshape(CHOSEN_BLOCKS * BLOCK_TOKENS, HEAD_SIZE)
            row_start = (index_of_block * BLOCK_TOKENS).astype(jnp.int32)
            head_start = (index_of_head * per_value_head).astype(jnp.int32)
            own_keys = lax.dynamic_slice(rotated_key_rows, (row_start, index_of_head, zero_index), (BLOCK_TOKENS, 1, HEAD_SIZE)).reshape(BLOCK_TOKENS, HEAD_SIZE)
            own_values = lax.dynamic_slice(fresh_values, (row_start, index_of_head, zero_index), (BLOCK_TOKENS, 1, HEAD_SIZE)).reshape(BLOCK_TOKENS, HEAD_SIZE)
            query_rows = lax.dynamic_slice(rot_query, (row_start, head_start, zero_index), (BLOCK_TOKENS, per_value_head, HEAD_SIZE)).reshape(BLOCK_TOKENS * per_value_head, HEAD_SIZE)
            sel_scores = jnp.dot(query_rows, sel_keys.T, preferred_element_type=jnp.float32) * score_scale
            own_scores = jnp.dot(query_rows, own_keys.T, preferred_element_type=jnp.float32) * score_scale
            query_token = jnp.arange(BLOCK_TOKENS * per_value_head, dtype=jnp.int32) // per_value_head
            key_token = jnp.arange(BLOCK_TOKENS, dtype=jnp.int32)
            causal = key_token[None, :] <= query_token[:, None]
            own_scores = jnp.where(causal, own_scores, -jnp.inf)
            maxima = jnp.maximum(jnp.max(sel_scores, axis=1), jnp.max(own_scores, axis=1))
            sel_weights = jnp.exp(sel_scores - maxima[:, None])
            own_weights = jnp.exp(own_scores - maxima[:, None])
            totals = jnp.sum(sel_weights, axis=1) + jnp.sum(own_weights, axis=1)
            weighted = jnp.dot(sel_weights, sel_values.astype(jnp.float32), precision=lax.Precision.HIGHEST)
            weighted = weighted + jnp.dot(own_weights, own_values.astype(jnp.float32), precision=lax.Precision.HIGHEST)
            context = (weighted / totals[:, None]).astype(jnp.bfloat16)
            return context.reshape(BLOCK_TOKENS, per_value_head, HEAD_SIZE)

        work_items = lax.map(attend_single_item, jnp.arange(QUERY_BLOCKS * VALUE_HEADS, dtype=jnp.int32))
        arranged_rows = work_items.reshape(QUERY_BLOCKS, VALUE_HEADS, BLOCK_TOKENS, per_value_head, HEAD_SIZE).transpose(0, 2, 1, 3, 4)
        results.append(arranged_rows.reshape(SPAN_TOKENS, QUERY_HEADS * HEAD_SIZE))
    stacked = jnp.stack(results)
    return jnp.roll(stacked, 1, axis=0)
```

```python
import functools

import jax
import jax.numpy as jnp
from jax import lax
from jax.experimental import pallas as pl
from jax.experimental.pallas import tpu as pltpu
from jax.sharding import PartitionSpec as P

HEAD_SIZE = 128
BLOCK_TOKENS = 512
CHOSEN_BLOCKS = 8


ROPE_BASE = 500000.0


def swapped(x, axis, stride):
    return lax.ppermute(x, axis, [(i, i ^ 1 << stride) for i in range(lax.axis_size(axis))])


def passed_along(block, axis, distance):
    devices = range(lax.axis_size(axis))
    route = [((i - distance) % len(devices), i) for i in devices]
    return lax.ppermute(block, axis, route)


def apply_rotary(values, token_positions):
    half_dim = values.shape[-1] // 2
    frequencies = ROPE_BASE ** (-(2.0 * jnp.arange(half_dim, dtype=jnp.float32)) / values.shape[-1])
    angles = token_positions[:, None] * frequencies[None, :]
    cosine = jnp.cos(angles)[:, None, :]
    sine_part = jnp.sin(angles)[:, None, :]
    widened = values.astype(jnp.float32)
    first_half = widened[..., :half_dim]
    second_half = widened[..., half_dim:]
    joined = jnp.concatenate(
        [
            first_half * cosine - second_half * sine_part,
            second_half * cosine + first_half * sine_part,
        ],
        axis=-1,
    )
    return joined.astype(jnp.bfloat16)


def combine(earlier, later):
    maxima = jnp.maximum(earlier[0], later[0])
    first_factor = jnp.exp(earlier[0] - maxima)
    second_factor = jnp.exp(later[0] - maxima)
    totals = earlier[1] * first_factor + later[1] * second_factor
    weighted = earlier[2] * first_factor[..., None] + later[2] * second_factor[..., None]
    return (maxima, totals, weighted)


def general(queries, span_key_values, key_value_cache, chosen, offset):
    ctx_size = lax.axis_size("ctx")
    my_index = lax.axis_index("ctx")
    tok_rows = queries.shape[1]
    kv_heads = key_value_cache.shape[3] // HEAD_SIZE
    q_heads = queries.shape[2] // HEAD_SIZE
    per_value_head = q_heads // kv_heads
    members = ctx_size // kv_heads
    blocks_here = key_value_cache.shape[1] // BLOCK_TOKENS
    blocks_total = blocks_here * ctx_size
    q_blocks = chosen.shape[1]
    per_block = BLOCK_TOKENS // tok_rows
    key_rows = BLOCK_TOKENS // members
    own_rows = tok_rows // members
    my_head = my_index // members
    my_rank = my_index % members
    score_scale = HEAD_SIZE ** (-0.5)
    token_start = offset[0] + my_index * tok_rows
    token_positions = (token_start + jnp.arange(tok_rows, dtype=jnp.int32)).astype(jnp.float32)
    rot_query = apply_rotary(queries[0].reshape(tok_rows, q_heads, HEAD_SIZE), token_positions)
    rotated_key_rows = apply_rotary(
        span_key_values[0, :, 0].reshape(tok_rows, kv_heads, HEAD_SIZE), token_positions
    )
    fresh_values = span_key_values[0, :, 1].reshape(tok_rows, kv_heads, HEAD_SIZE)
    query_send = jnp.broadcast_to(
        rot_query.reshape(tok_rows, kv_heads, 1, per_value_head * HEAD_SIZE),
        (tok_rows, kv_heads, members, per_value_head * HEAD_SIZE),
    )
    query_send = query_send.reshape(tok_rows, ctx_size, per_value_head * HEAD_SIZE)
    pair_rows = jnp.concatenate([rotated_key_rows, fresh_values], axis=-1)
    pair_send = (
        pair_rows.reshape(members, own_rows, kv_heads, 2 * HEAD_SIZE)
        .transpose(1, 2, 0, 3)
        .reshape(own_rows, ctx_size, 2 * HEAD_SIZE)
    )
    query_recv, pair_recv = (
        lax.all_to_all(query_send, "ctx", split_axis=1, concat_axis=1, tiled=True),
        lax.all_to_all(pair_send, "ctx", split_axis=1, concat_axis=1, tiled=True),
    )
    picks_here = chosen[0]
    needed = jnp.any(
        picks_here[..., None] == jnp.arange(blocks_total, dtype=jnp.int32), axis=(0, 2)
    )
    needed_here = lax.dynamic_slice_in_dim(needed, my_index * blocks_here, blocks_here, axis=1)
    needed_here = needed_here.T.reshape(blocks_here, 1, kv_heads, 1, 1, 1)
    arranged_rows = (
        key_value_cache[0]
        .reshape(blocks_here, members, key_rows, 2, kv_heads, HEAD_SIZE)
        .transpose(0, 2, 4, 1, 3, 5)
    )
    arranged_rows = jnp.where(needed_here, arranged_rows, jnp.zeros((), jnp.bfloat16))
    tile_send = arranged_rows.reshape(blocks_here * key_rows, ctx_size, 2 * HEAD_SIZE)
    fetched = lax.all_to_all(tile_send, "ctx", split_axis=1, concat_axis=1, tiled=True)
    fetched = fetched.reshape(blocks_here, key_rows, ctx_size, 2 * HEAD_SIZE)
    maxima_parts = []
    totals_parts = []
    weighted_parts = []
    for index_of_block in range(q_blocks):
        block_ids = picks_here[index_of_block][my_head]
        owner_rank = block_ids // blocks_here
        slot_index = block_ids % blocks_here
        picked = jnp.stack(
            [
                lax.dynamic_slice(
                    fetched,
                    (slot_index[n], 0, owner_rank[n], 0),
                    (1, key_rows, 1, 2 * HEAD_SIZE),
                )[0, :, 0]
                for n in range(CHOSEN_BLOCKS)
            ]
        )
        sel_keys = picked[..., :HEAD_SIZE].reshape(CHOSEN_BLOCKS * key_rows, HEAD_SIZE)
        sel_values = picked[..., HEAD_SIZE:].reshape(CHOSEN_BLOCKS * key_rows, HEAD_SIZE)
        first_source = index_of_block * per_block
        own_pairs = pair_recv[:, first_source : first_source + per_block]
        own_keys = own_pairs[..., :HEAD_SIZE].reshape(own_rows * per_block, HEAD_SIZE)
        own_values = own_pairs[..., HEAD_SIZE:].reshape(own_rows * per_block, HEAD_SIZE)
        query_rows = query_recv[:, first_source : first_source + per_block].reshape(
            tok_rows * per_block * per_value_head, HEAD_SIZE
        )
        sources = first_source + jnp.arange(per_block, dtype=jnp.int32)
        query_token = sources[None, :] * tok_rows + jnp.arange(tok_rows, dtype=jnp.int32)[:, None]
        query_token = jnp.broadcast_to(
            query_token[:, :, None], (tok_rows, per_block, per_value_head)
        ).reshape(-1)
        key_token = (
            sources[None, :] * tok_rows
            + my_rank * own_rows
            + jnp.arange(own_rows, dtype=jnp.int32)[:, None]
        )
        key_token = key_token.reshape(-1)
        sel_scores = (
            jnp.dot(query_rows, sel_keys.T, preferred_element_type=jnp.float32) * score_scale
        )
        own_scores = (
            jnp.dot(query_rows, own_keys.T, preferred_element_type=jnp.float32) * score_scale
        )
        causal = key_token[None, :] <= query_token[:, None]
        own_scores = jnp.where(causal, own_scores, -jnp.inf)
        maxima = jnp.maximum(jnp.max(sel_scores, axis=1), jnp.max(own_scores, axis=1))
        sel_weights = jnp.exp(sel_scores - maxima[:, None])
        own_weights = jnp.exp(own_scores - maxima[:, None])
        totals = jnp.sum(sel_weights, axis=1) + jnp.sum(own_weights, axis=1)
        weighted = jnp.dot(
            sel_weights, sel_values.astype(jnp.float32), precision=lax.Precision.HIGHEST
        )
        weighted = weighted + jnp.dot(
            own_weights, own_values.astype(jnp.float32), precision=lax.Precision.HIGHEST
        )
        maxima_parts.append(maxima.reshape(tok_rows, per_block, per_value_head))
        totals_parts.append(totals.reshape(tok_rows, per_block, per_value_head))
        weighted_parts.append(weighted.reshape(tok_rows, per_block, per_value_head, HEAD_SIZE))
    maxima_all = jnp.concatenate(maxima_parts, axis=1)
    totals_all = jnp.concatenate(totals_parts, axis=1)
    weighted_all = jnp.concatenate(weighted_parts, axis=1)
    current = (maxima_all, totals_all, weighted_all)
    bit_count = members.bit_length() - 1
    for bit_index in reversed(range(bit_count)):
        half_rows = current[0].shape[0] // 2
        my_bit = my_index // 2**bit_index % 2
        kept = tuple(
            (
                lax.dynamic_slice_in_dim(part_array, my_bit * half_rows, half_rows, 0)
                for part_array in current
            )
        )
        given = tuple(
            (
                lax.dynamic_slice_in_dim(part_array, (1 - my_bit) * half_rows, half_rows, 0)
                for part_array in current
            )
        )
        partner = swapped((given[0], given[1], given[2]), "ctx", bit_index)
        current = combine(kept, partner)
    finished = (
        (current[2] / current[1][..., None])
        .astype(jnp.bfloat16)
        .reshape(own_rows, ctx_size, per_value_head * HEAD_SIZE)
    )
    returned = lax.all_to_all(finished, "ctx", split_axis=1, concat_axis=1, tiled=True)
    context = (
        returned.reshape(own_rows, kv_heads, members, per_value_head * HEAD_SIZE)
        .transpose(2, 0, 1, 3)
        .reshape(tok_rows, q_heads * HEAD_SIZE)
    )
    handed = passed_along(context, "segment", 1)
    return handed[None]


LOG2E = 1.4426950408889634
MESH = pl.DeviceIdType.MESH
PAIR = 2
NOTHING = -1e29
HIDDEN = 1e30
SCALE2 = LOG2E * HEAD_SIZE ** (-0.5)


def turned(block, cosine, sine):
    wide = block.astype(jnp.float32)
    other = pltpu.roll(wide, HEAD_SIZE // 2, 1)
    return (wide * cosine + other * sine).astype(jnp.bfloat16)


def widened(column, count):
    return jnp.concatenate([column] * count, axis=1)


def fold(query, keys, values, shift, causal, first, acc, top):
    scores = lax.dot_general(
        query, keys, (((1,), (1,)), ((), ())), preferred_element_type=jnp.float32
    )
    if causal is not None:
        scores = jnp.where(causal, scores, -jnp.inf)
    new = jnp.max(scores, axis=1, keepdims=True) * SCALE2
    if shift is not None:
        new = new - shift
    new = jnp.broadcast_to(new, (scores.shape[0], HEAD_SIZE))
    if first:
        new = jnp.maximum(new, NOTHING)
    else:
        held = top[...]
        new = jnp.maximum(new, held)
    taken = new if shift is None else new + shift
    weights = jnp.exp2(scores * SCALE2 - widened(taken, scores.shape[1] // HEAD_SIZE))
    part = jnp.dot(weights.astype(jnp.bfloat16), values, preferred_element_type=jnp.float32)
    if first:
        acc[...] = part
    else:
        acc[...] = acc[...] * widened(jnp.exp2(held - new), 2) + part
    top[...] = new


def diagonal():
    rows = lax.broadcasted_iota(jnp.int32, (HEAD_SIZE, HEAD_SIZE), 0)
    columns = lax.broadcasted_iota(jnp.int32, (HEAD_SIZE, HEAD_SIZE), 1)
    return rows == columns


def closed(acc, top):
    totals = jnp.maximum(acc[:, HEAD_SIZE:], 1e-30)
    context = acc[:, :HEAD_SIZE] / totals
    logs = top[...] + jnp.log2(totals)
    eye = diagonal()
    lines = [
        jnp.sum(
            jnp.where(eye, logs[r : r + HEAD_SIZE], 0.0), axis=0, keepdims=True
        )
        for r in range(0, logs.shape[0], HEAD_SIZE)
    ]
    return context, jnp.concatenate(lines, axis=0)


def merged(own, own_logs, other, other_logs):
    most = jnp.maximum(own_logs, other_logs)
    mine = jnp.exp2(own_logs - most)
    total = mine + jnp.exp2(other_logs - most)
    share = mine / total
    eye = diagonal()
    columns = [
        jnp.broadcast_to(
            jnp.sum(
                jnp.where(eye, share[r : r + 1], 0.0), axis=1, keepdims=True
            ),
            (HEAD_SIZE, HEAD_SIZE),
        )
        for r in range(share.shape[0])
    ]
    other = other.astype(jnp.float32)
    return other + jnp.concatenate(columns, axis=0) * (own - other), most + jnp.log2(total)


def turn_kernel(q_ref, cos_ref, sin_ref, out_ref):
    tokens = q_ref.shape[1]
    for h in range(q_ref.shape[2] // HEAD_SIZE):
        spot = slice(h % PAIR * tokens, (h % PAIR + 1) * tokens)
        out_ref[h // PAIR, spot] = turned(
            q_ref[0, :, h * HEAD_SIZE : (h + 1) * HEAD_SIZE], cos_ref[...], sin_ref[...]
        )


def home_kernel(
    picks_ref, q_ref, sk_ref, sv_ref, cos_ref, sin_ref, k_ref, v_ref, out_ref, logs_ref,
    acc, top, values,
):
    tokens = cos_ref.shape[0]
    kv_heads = k_ref.shape[1] // HEAD_SIZE
    halves = q_ref.shape[0] // kv_heads
    blocks_here = k_ref.shape[0] // BLOCK_TOKENS
    values[:, HEAD_SIZE:] = jnp.ones((tokens, HEAD_SIZE), values.dtype)

    @pl.loop(0, kv_heads)
    def _(g):
        spot = pl.ds(pl.multiple_of(g * HEAD_SIZE, HEAD_SIZE), HEAD_SIZE)
        values[:, :HEAD_SIZE] = sv_ref[:, spot]
        own_keys = turned(sk_ref[:, spot], cos_ref[...], sin_ref[...])
        rows = lax.broadcasted_iota(jnp.int32, (tokens, tokens), 0)
        columns = lax.broadcasted_iota(jnp.int32, (tokens, tokens), 1)
        causal = jnp.concatenate([columns <= rows] * PAIR, axis=0)
        for i in range(halves):
            fold(q_ref[g * halves + i], own_keys, values[...], None, causal, True, acc.at[i], top.at[i])

        @pl.loop(0, CHOSEN_BLOCKS)
        def _(n):
            block = picks_ref[g * CHOSEN_BLOCKS + n]

            @pl.when((block >= 0) & (block < blocks_here))
            def _():
                lines = pl.ds(pl.multiple_of(block * BLOCK_TOKENS, BLOCK_TOKENS), BLOCK_TOKENS)
                values[:, :HEAD_SIZE] = v_ref[lines, spot]
                for i in range(halves):
                    fold(
                        q_ref[g * halves + i], k_ref[lines, spot], values[...], None, None, False,
                        acc.at[i], top.at[i],
                    )

        for i in range(halves):
            out_ref[g * halves + i], logs_ref[g * halves + i] = closed(acc[i], top[i])


def relay_kernel(
    n_seg, shift_ref, own_ref, own_logs_ref, k_ref, v_ref, ql_ref, qr_ref, out_ref,
    q_buf, k_buf, v_buf, buf, logs, stash, stash_logs, acc, top,
    load_sem, q_send, q_recv, p_send, p_recv, l_send, l_recv, o_send, o_recv,
):
    me = lax.axis_index("ctx")
    seg = lax.axis_index("segment")
    side = me // 2
    ahead = 1 - 2 * side
    is_mid = (me == 1) | (me == 2)
    is_end = (me == 0) | (me == 3)
    forth, back = side, 1 - side
    kv_heads, slots = k_buf.shape[0], k_buf.shape[1]
    chunks, rows = ql_ref.shape[0], ql_ref.shape[1]
    tokens = rows // PAIR
    halves = chunks // kv_heads
    blocks_here = slots // BLOCK_TOKENS
    after = lax.rem(seg + 1, n_seg)
    before = lax.rem(seg + n_seg - 1, n_seg)

    def seen(b):
        return b * ahead + 3 * side

    def load(i, source, target):
        return pltpu.make_async_copy(source, target, load_sem.at[i])

    loads = []
    for g in range(kv_heads):
        spot = pl.ds(g * HEAD_SIZE, HEAD_SIZE)
        loads.append(load(2 * g, k_ref.at[:, spot], k_buf.at[g]))
        loads.append(load(2 * g + 1, v_ref.at[:, spot], v_buf.at[g, :, pl.ds(0, HEAD_SIZE)]))
    from_left = load(2 * kv_heads, ql_ref, q_buf.at[lax.max(me - 1, 0)])
    from_right = load(2 * kv_heads + 1, qr_ref, q_buf.at[lax.min(me + 1, 3)])
    for copy in loads:
        copy.start()

    @pl.when(me > 0)
    def _():
        from_left.start()

    @pl.when(me < 3)
    def _():
        from_right.start()

    barrier = pltpu.get_barrier_semaphore()

    def greet(**place):
        pl.semaphore_signal(barrier, inc=1, device_id=place, device_id_type=MESH)

    @pl.when(me > 0)
    def _():
        greet(ctx=me - 1)

    @pl.when(me < 3)
    def _():
        greet(ctx=me + 1)

    others = (after,) if n_seg == 2 else (after, before)
    for other in others:
        greet(segment=other)

    @pl.when(is_mid)
    def _():
        pl.semaphore_wait(barrier, 2 + len(others))

    @pl.when(is_end)
    def _():
        pl.semaphore_wait(barrier, 1 + len(others))

    def q_copy(source, b, k, target):
        return pltpu.make_async_remote_copy(
            src_ref=source,
            dst_ref=q_buf.at[b, k],
            send_sem=q_send.at[b, k],
            recv_sem=q_recv.at[b, k],
            device_id={"ctx": target},
            device_id_type=MESH,
        )

    def second_hops(k):
        left = q_copy(qr_ref.at[k], lax.min(me + 1, 3), k, lax.max(me - 1, 0))
        right = q_copy(ql_ref.at[k], lax.max(me - 1, 0), k, lax.min(me + 1, 3))
        return left, right

    def third_hop(k):
        b = seen(3)
        return q_copy(q_buf.at[b, k], b, k, me - ahead)

    def part_copies(way, p, k, target):
        return (
            pltpu.make_async_remote_copy(
                src_ref=buf.at[way, p, k],
                dst_ref=buf.at[way, p, k],
                send_sem=p_send.at[way, p, k],
                recv_sem=p_recv.at[way, p, k],
                device_id={"ctx": target},
                device_id_type=MESH,
            ),
            pltpu.make_async_remote_copy(
                src_ref=logs.at[way, p, k],
                dst_ref=logs.at[way, p, k],
                send_sem=l_send.at[way, p, k],
                recv_sem=l_recv.at[way, p, k],
                device_id={"ctx": target},
                device_id_type=MESH,
            ),
        )

    def arrived(way, p, k):
        for copy in part_copies(way, p, k, me + ahead):
            copy.wait_recv()

    def send(way, p, k, target):
        for copy in part_copies(way, p, k, target):
            copy.start()

    def out_copies(way, p, k):
        return [
            pltpu.make_async_remote_copy(
                src_ref=buf.at[way, p, k, pl.ds(i * tokens, tokens)],
                dst_ref=out_ref.at[
                    0,
                    :,
                    pl.ds(pl.multiple_of((k * PAIR + i) * HEAD_SIZE, HEAD_SIZE), HEAD_SIZE),
                ],
                send_sem=o_send.at[k, i],
                recv_sem=o_recv.at[k, i],
                device_id={"segment": after},
                device_id_type=MESH,
            )
            for i in range(PAIR)
        ]

    def relay(way, p, k, held, target):
        arrived(way, p, k)
        value, log = merged(stash[held, k], stash_logs[held, k], buf[way, p, k], logs[way, p, k])
        buf[way, p, k] = value.astype(buf.dtype)
        logs[way, p, k] = log
        send(way, p, k, target)

    def near(u):
        p = u // chunks
        relay(forth, p, lax.rem(u, chunks), lax.rem(p + 1, 2), me + ahead)

    def far(u):
        relay(back, 2, lax.rem(u, chunks), 0, me - ahead)

    def mid_final(k):
        arrived(forth, 0, k)
        arrived(back, 1, k)
        value, log = merged(own_ref[k], own_logs_ref[k], buf[forth, 0, k], logs[forth, 0, k])
        value, log = merged(value, log, buf[back, 1, k], logs[back, 1, k])
        buf[back, 1, k] = value.astype(buf.dtype)
        for copy in out_copies(back, 1, k):
            copy.start()

    def end_final(k):
        arrived(back, 2, k)
        value, log = merged(own_ref[k], own_logs_ref[k], buf[back, 2, k], logs[back, 2, k])
        buf[back, 2, k] = value.astype(buf.dtype)
        for copy in out_copies(back, 2, k):
            copy.start()

    @pl.when(is_mid)
    def _():
        @pl.loop(0, chunks)
        def _(k):
            for copy in second_hops(k):
                copy.start()

    for g in range(kv_heads):
        v_buf[g, :, HEAD_SIZE:] = jnp.ones((slots, HEAD_SIZE), v_buf.dtype)

    for copy in loads:
        copy.wait()

    @pl.when(me > 0)
    def _():
        from_left.wait()

    @pl.when(me < 3)
    def _():
        from_right.wait()

    steps = 3 * chunks

    @pl.loop(0, steps)
    def _(t):
        p, k = t // chunks, lax.rem(t, chunks)
        g = k // halves
        place = jnp.where(is_mid, lax.rem(p + 2, 4), p + 1)
        b = seen(place)

        @pl.when(is_end & (p > 0))
        def _():
            q_copy(q_buf.at[b, k], b, k, me + ahead).wait_recv()

        @pl.when(is_mid & (t >= 2) & (t < chunks + 2))
        def _():
            copy = third_hop(t - 2)
            copy.wait_recv()
            copy.start()

        query = q_buf[b, k]
        for j in range(blocks_here):
            lines = slice(j * BLOCK_TOKENS, (j + 1) * BLOCK_TOKENS)
            fold(
                query, k_buf[g, lines], v_buf[g, lines],
                shift_ref[(b * kv_heads + g) * blocks_here + j], None, j == 0, acc, top,
            )
        context, log = closed(acc[...], top[...])

        @pl.when(is_end)
        def _():
            buf[forth, p, k] = context.astype(buf.dtype)
            logs[forth, p, k] = log
            send(forth, p, k, me + ahead)

        @pl.when(is_mid)
        def _():
            stash[lax.rem(p, 2), k] = context
            stash_logs[lax.rem(p, 2), k] = log

        @pl.when(is_mid & (t >= chunks + 2))
        def _():
            near(t - 2)

        @pl.when(is_mid & (t >= 2 * chunks + 4))
        def _():
            far(t - 4)

        @pl.when(is_mid & (t >= chunks + 5) & (t < 2 * chunks + 5))
        def _():
            mid_final(t - chunks - 5)

    @pl.when(is_mid)
    def _():
        @pl.loop(0, 4)
        def _(i):
            @pl.when(i < 2)
            def _():
                near(steps - 2 + i)

            far(steps - 4 + i)

    @pl.when(is_end)
    def _():
        @pl.loop(0, chunks)
        def _(k):
            end_final(k)

    @pl.when(is_mid)
    def _():
        @pl.loop(0, chunks)
        def _(k):
            for copy in second_hops(k) + (third_hop(k),):
                copy.wait_send()
            for copy in part_copies(forth, 1, k, me + ahead) + part_copies(forth, 2, k, me + ahead):
                copy.wait_send()
            for copy in part_copies(back, 2, k, me - ahead):
                copy.wait_send()
            for copy in out_copies(back, 1, k):
                copy.wait()

    @pl.when(is_end)
    def _():
        @pl.loop(0, chunks)
        def _(k):
            for p in range(3):
                for copy in part_copies(forth, p, k, me + ahead):
                    copy.wait_send()
            for copy in out_copies(back, 2, k):
                copy.wait()


def local(queries, span_key_values, key_value_cache, chosen, offset):
    n_ctx = lax.axis_size("ctx")
    n_seg = lax.axis_size("segment")
    me = lax.axis_index("ctx")
    tokens = queries.shape[1]
    kv_heads = key_value_cache.shape[3] // HEAD_SIZE
    q_heads = queries.shape[2] // HEAD_SIZE
    per_head = q_heads // kv_heads
    slots = key_value_cache.shape[1]
    blocks_here = slots // BLOCK_TOKENS
    if not (
        n_ctx == 4
        and tokens == BLOCK_TOKENS
        and n_seg > 1
        and per_head % PAIR == 0
        and slots * kv_heads <= 16384
    ):
        return general(queries, span_key_values, key_value_cache, chosen, offset)
    bf16, f32 = jnp.bfloat16, jnp.float32
    dma = pltpu.SemaphoreType.DMA
    chunks, rows = q_heads // PAIR, PAIR * tokens
    lines = rows // HEAD_SIZE
    vmem = pl.BlockSpec(memory_space=pltpu.VMEM)
    smem = pl.BlockSpec(memory_space=pltpu.SMEM)
    anywhere = pl.BlockSpec(memory_space=pl.ANY)

    positions = (offset[0] + me * tokens + jnp.arange(tokens, dtype=jnp.int32)).astype(f32)
    half = HEAD_SIZE // 2
    frequencies = ROPE_BASE ** (-(2.0 * jnp.arange(half, dtype=f32)) / HEAD_SIZE)
    angles = positions[:, None] * frequencies[None, :]
    cosine, sine = jnp.cos(angles), jnp.sin(angles)
    cos_table = jnp.concatenate([cosine, cosine], axis=1)
    sin_table = jnp.concatenate([-sine, sine], axis=1)
    q_own = pl.pallas_call(
        turn_kernel,
        out_shape=jax.ShapeDtypeStruct((chunks, rows, HEAD_SIZE), bf16),
        in_specs=[vmem] * 3,
        out_specs=vmem,
        cost_estimate=pl.CostEstimate(
            flops=6 * queries.size, bytes_accessed=4 * queries.size, transcendentals=0
        ),
        compiler_params=pltpu.CompilerParams(vmem_limit_bytes=24 * 2**20),
    )(queries, cos_table, sin_table)
    q_left = lax.ppermute(q_own, "ctx", [(i, i + 1) for i in range(n_ctx - 1)])
    q_right = lax.ppermute(q_own, "ctx", [(i + 1, i) for i in range(n_ctx - 1)])

    keys, values = key_value_cache[0, :, 0], key_value_cache[0, :, 1]
    span_keys, span_values = span_key_values[0, :, 0], span_key_values[0, :, 1]
    first_block = me * blocks_here
    picks = lax.dynamic_index_in_dim(chosen[0], me, 0, keepdims=False) - first_block
    here = first_block + jnp.arange(blocks_here, dtype=jnp.int32)
    taken = jnp.any(chosen[0][..., None] == here, axis=2)
    shift = jnp.where(taken, 0.0, HIDDEN).astype(f32).reshape(-1)
    work = 4 * q_heads * tokens * BLOCK_TOKENS * HEAD_SIZE
    own, own_logs = pl.pallas_call(
        home_kernel,
        out_shape=(
            jax.ShapeDtypeStruct((chunks, rows, HEAD_SIZE), f32),
            jax.ShapeDtypeStruct((chunks, lines, HEAD_SIZE), f32),
        ),
        in_specs=[smem] + [vmem] * 7,
        out_specs=(vmem, vmem),
        scratch_shapes=[
            pltpu.VMEM((chunks // kv_heads, rows, 2 * HEAD_SIZE), f32),
            pltpu.VMEM((chunks // kv_heads, rows, HEAD_SIZE), f32),
            pltpu.VMEM((tokens, 2 * HEAD_SIZE), bf16),
        ],
        cost_estimate=pl.CostEstimate(
            flops=6 * work, bytes_accessed=16 * 2**20, transcendentals=work // 128
        ),
        compiler_params=pltpu.CompilerParams(vmem_limit_bytes=48 * 2**20),
    )(picks.reshape(-1), q_own, span_keys, span_values, cos_table, sin_table, keys, values)

    return pl.pallas_call(
        functools.partial(relay_kernel, n_seg),
        out_shape=jax.ShapeDtypeStruct(queries.shape, bf16),
        in_specs=[smem, vmem, vmem] + [anywhere] * 4,
        out_specs=anywhere,
        scratch_shapes=[
            pltpu.VMEM((n_ctx, chunks, rows, HEAD_SIZE), bf16),
            pltpu.VMEM((kv_heads, slots, HEAD_SIZE), bf16),
            pltpu.VMEM((kv_heads, slots, 2 * HEAD_SIZE), bf16),
            pltpu.VMEM((2, 3, chunks, rows, HEAD_SIZE), bf16),
            pltpu.VMEM((2, 3, chunks, lines, HEAD_SIZE), f32),
            pltpu.VMEM((2, chunks, rows, HEAD_SIZE), f32),
            pltpu.VMEM((2, chunks, lines, HEAD_SIZE), f32),
            pltpu.VMEM((rows, 2 * HEAD_SIZE), f32),
            pltpu.VMEM((rows, HEAD_SIZE), f32),
            dma((2 * kv_heads + 2,)),
            dma((n_ctx, chunks)),
            dma((n_ctx, chunks)),
            dma((2, 3, chunks)),
            dma((2, 3, chunks)),
            dma((2, 3, chunks)),
            dma((2, 3, chunks)),
            dma((chunks, PAIR)),
            dma((chunks, PAIR)),
        ],
        cost_estimate=pl.CostEstimate(
            flops=24 * work, bytes_accessed=32 * 2**20, transcendentals=work // 16
        ),
        compiler_params=pltpu.CompilerParams(
            collective_id=0, has_side_effects=True, vmem_limit_bytes=60 * 2**20
        ),
    )(shift, own, own_logs, keys, values, q_left, q_right)


def solution(mesh):
    return jax.shard_map(
        local,
        mesh=mesh,
        in_specs=(
            P(("groups", "segment"), "ctx", "head"),
            P(("groups", "segment"), "ctx", None, "head"),
            P(("groups", "segment"), "ctx", None, "head"),
            P(("groups", "segment"), None, "head", None),
            P(("groups", "segment")),
        ),
        out_specs=P(("groups", "segment"), "ctx", "head"),
        check_vma=False,
    )
```

```python
import functools

import jax
import jax.numpy as jnp
from jax import lax
from jax.experimental import pallas as pl
from jax.experimental.pallas import tpu as pltpu
from jax.sharding import PartitionSpec as P

HEAD_SIZE = 128
BLOCK_TOKENS = 512
CHOSEN_BLOCKS = 8


ROPE_BASE = 500000.0


def swapped(x, axis, stride):
    return lax.ppermute(x, axis, [(i, i ^ 1 << stride) for i in range(lax.axis_size(axis))])


def passed_along(block, axis, distance):
    devices = range(lax.axis_size(axis))
    route = [((i - distance) % len(devices), i) for i in devices]
    return lax.ppermute(block, axis, route)


def apply_rotary(values, token_positions):
    half_dim = values.shape[-1] // 2
    frequencies = ROPE_BASE ** (-(2.0 * jnp.arange(half_dim, dtype=jnp.float32)) / values.shape[-1])
    angles = token_positions[:, None] * frequencies[None, :]
    cosine = jnp.cos(angles)[:, None, :]
    sine_part = jnp.sin(angles)[:, None, :]
    widened = values.astype(jnp.float32)
    first_half = widened[..., :half_dim]
    second_half = widened[..., half_dim:]
    joined = jnp.concatenate(
        [
            first_half * cosine - second_half * sine_part,
            second_half * cosine + first_half * sine_part,
        ],
        axis=-1,
    )
    return joined.astype(jnp.bfloat16)


def combine(earlier, later):
    maxima = jnp.maximum(earlier[0], later[0])
    first_factor = jnp.exp(earlier[0] - maxima)
    second_factor = jnp.exp(later[0] - maxima)
    totals = earlier[1] * first_factor + later[1] * second_factor
    weighted = earlier[2] * first_factor[..., None] + later[2] * second_factor[..., None]
    return (maxima, totals, weighted)


def general(queries, span_key_values, key_value_cache, chosen, offset):
    ctx_size = lax.axis_size("ctx")
    my_index = lax.axis_index("ctx")
    tok_rows = queries.shape[1]
    kv_heads = key_value_cache.shape[3] // HEAD_SIZE
    q_heads = queries.shape[2] // HEAD_SIZE
    per_value_head = q_heads // kv_heads
    members = ctx_size // kv_heads
    blocks_here = key_value_cache.shape[1] // BLOCK_TOKENS
    blocks_total = blocks_here * ctx_size
    q_blocks = chosen.shape[1]
    per_block = BLOCK_TOKENS // tok_rows
    key_rows = BLOCK_TOKENS // members
    own_rows = tok_rows // members
    my_head = my_index // members
    my_rank = my_index % members
    score_scale = HEAD_SIZE ** (-0.5)
    token_start = offset[0] + my_index * tok_rows
    token_positions = (token_start + jnp.arange(tok_rows, dtype=jnp.int32)).astype(jnp.float32)
    rot_query = apply_rotary(queries[0].reshape(tok_rows, q_heads, HEAD_SIZE), token_positions)
    rotated_key_rows = apply_rotary(
        span_key_values[0, :, 0].reshape(tok_rows, kv_heads, HEAD_SIZE), token_positions
    )
    fresh_values = span_key_values[0, :, 1].reshape(tok_rows, kv_heads, HEAD_SIZE)
    query_send = jnp.broadcast_to(
        rot_query.reshape(tok_rows, kv_heads, 1, per_value_head * HEAD_SIZE),
        (tok_rows, kv_heads, members, per_value_head * HEAD_SIZE),
    )
    query_send = query_send.reshape(tok_rows, ctx_size, per_value_head * HEAD_SIZE)
    pair_rows = jnp.concatenate([rotated_key_rows, fresh_values], axis=-1)
    pair_send = (
        pair_rows.reshape(members, own_rows, kv_heads, 2 * HEAD_SIZE)
        .transpose(1, 2, 0, 3)
        .reshape(own_rows, ctx_size, 2 * HEAD_SIZE)
    )
    query_recv, pair_recv = (
        lax.all_to_all(query_send, "ctx", split_axis=1, concat_axis=1, tiled=True),
        lax.all_to_all(pair_send, "ctx", split_axis=1, concat_axis=1, tiled=True),
    )
    picks_here = chosen[0]
    needed = jnp.any(
        picks_here[..., None] == jnp.arange(blocks_total, dtype=jnp.int32), axis=(0, 2)
    )
    needed_here = lax.dynamic_slice_in_dim(needed, my_index * blocks_here, blocks_here, axis=1)
    needed_here = needed_here.T.reshape(blocks_here, 1, kv_heads, 1, 1, 1)
    arranged_rows = (
        key_value_cache[0]
        .reshape(blocks_here, members, key_rows, 2, kv_heads, HEAD_SIZE)
        .transpose(0, 2, 4, 1, 3, 5)
    )
    arranged_rows = jnp.where(needed_here, arranged_rows, jnp.zeros((), jnp.bfloat16))
    tile_send = arranged_rows.reshape(blocks_here * key_rows, ctx_size, 2 * HEAD_SIZE)
    fetched = lax.all_to_all(tile_send, "ctx", split_axis=1, concat_axis=1, tiled=True)
    fetched = fetched.reshape(blocks_here, key_rows, ctx_size, 2 * HEAD_SIZE)
    maxima_parts = []
    totals_parts = []
    weighted_parts = []
    for index_of_block in range(q_blocks):
        block_ids = picks_here[index_of_block][my_head]
        owner_rank = block_ids // blocks_here
        slot_index = block_ids % blocks_here
        picked = jnp.stack(
            [
                lax.dynamic_slice(
                    fetched,
                    (slot_index[n], 0, owner_rank[n], 0),
                    (1, key_rows, 1, 2 * HEAD_SIZE),
                )[0, :, 0]
                for n in range(CHOSEN_BLOCKS)
            ]
        )
        sel_keys = picked[..., :HEAD_SIZE].reshape(CHOSEN_BLOCKS * key_rows, HEAD_SIZE)
        sel_values = picked[..., HEAD_SIZE:].reshape(CHOSEN_BLOCKS * key_rows, HEAD_SIZE)
        first_source = index_of_block * per_block
        own_pairs = pair_recv[:, first_source : first_source + per_block]
        own_keys = own_pairs[..., :HEAD_SIZE].reshape(own_rows * per_block, HEAD_SIZE)
        own_values = own_pairs[..., HEAD_SIZE:].reshape(own_rows * per_block, HEAD_SIZE)
        query_rows = query_recv[:, first_source : first_source + per_block].reshape(
            tok_rows * per_block * per_value_head, HEAD_SIZE
        )
        sources = first_source + jnp.arange(per_block, dtype=jnp.int32)
        query_token = sources[None, :] * tok_rows + jnp.arange(tok_rows, dtype=jnp.int32)[:, None]
        query_token = jnp.broadcast_to(
            query_token[:, :, None], (tok_rows, per_block, per_value_head)
        ).reshape(-1)
        key_token = (
            sources[None, :] * tok_rows
            + my_rank * own_rows
            + jnp.arange(own_rows, dtype=jnp.int32)[:, None]
        )
        key_token = key_token.reshape(-1)
        sel_scores = (
            jnp.dot(query_rows, sel_keys.T, preferred_element_type=jnp.float32) * score_scale
        )
        own_scores = (
            jnp.dot(query_rows, own_keys.T, preferred_element_type=jnp.float32) * score_scale
        )
        causal = key_token[None, :] <= query_token[:, None]
        own_scores = jnp.where(causal, own_scores, -jnp.inf)
        maxima = jnp.maximum(jnp.max(sel_scores, axis=1), jnp.max(own_scores, axis=1))
        sel_weights = jnp.exp(sel_scores - maxima[:, None])
        own_weights = jnp.exp(own_scores - maxima[:, None])
        totals = jnp.sum(sel_weights, axis=1) + jnp.sum(own_weights, axis=1)
        weighted = jnp.dot(
            sel_weights, sel_values.astype(jnp.float32), precision=lax.Precision.HIGHEST
        )
        weighted = weighted + jnp.dot(
            own_weights, own_values.astype(jnp.float32), precision=lax.Precision.HIGHEST
        )
        maxima_parts.append(maxima.reshape(tok_rows, per_block, per_value_head))
        totals_parts.append(totals.reshape(tok_rows, per_block, per_value_head))
        weighted_parts.append(weighted.reshape(tok_rows, per_block, per_value_head, HEAD_SIZE))
    maxima_all = jnp.concatenate(maxima_parts, axis=1)
    totals_all = jnp.concatenate(totals_parts, axis=1)
    weighted_all = jnp.concatenate(weighted_parts, axis=1)
    current = (maxima_all, totals_all, weighted_all)
    bit_count = members.bit_length() - 1
    for bit_index in reversed(range(bit_count)):
        half_rows = current[0].shape[0] // 2
        my_bit = my_index // 2**bit_index % 2
        kept = tuple(
            (
                lax.dynamic_slice_in_dim(part_array, my_bit * half_rows, half_rows, 0)
                for part_array in current
            )
        )
        given = tuple(
            (
                lax.dynamic_slice_in_dim(part_array, (1 - my_bit) * half_rows, half_rows, 0)
                for part_array in current
            )
        )
        partner = swapped((given[0], given[1], given[2]), "ctx", bit_index)
        current = combine(kept, partner)
    finished = (
        (current[2] / current[1][..., None])
        .astype(jnp.bfloat16)
        .reshape(own_rows, ctx_size, per_value_head * HEAD_SIZE)
    )
    returned = lax.all_to_all(finished, "ctx", split_axis=1, concat_axis=1, tiled=True)
    context = (
        returned.reshape(own_rows, kv_heads, members, per_value_head * HEAD_SIZE)
        .transpose(2, 0, 1, 3)
        .reshape(tok_rows, q_heads * HEAD_SIZE)
    )
    handed = passed_along(context, "segment", 1)
    return handed[None]


LOG2E = 1.4426950408889634
MESH = pl.DeviceIdType.MESH
PAIR = 2
NOTHING = -1e29
HIDDEN = 1e30
SCALE2 = LOG2E * HEAD_SIZE ** (-0.5)


def turned(block, cosine, sine):
    wide = block.astype(jnp.float32)
    other = pltpu.roll(wide, HEAD_SIZE // 2, 1)
    return (wide * cosine + other * sine).astype(jnp.bfloat16)


def widened(column, count):
    return jnp.concatenate([column] * count, axis=1)


def fold(query, keys, values, shift, causal, first, acc, top):
    scores = lax.dot_general(
        query, keys, (((1,), (1,)), ((), ())), preferred_element_type=jnp.float32
    )
    if causal is not None:
        scores = jnp.where(causal, scores, -jnp.inf)
    new = jnp.max(scores, axis=1, keepdims=True) * SCALE2
    if shift is not None:
        new = new - shift
    new = jnp.broadcast_to(new, (scores.shape[0], HEAD_SIZE))
    if first:
        new = jnp.maximum(new, NOTHING)
    else:
        held = top[...]
        new = jnp.maximum(new, held)
    taken = new if shift is None else new + shift
    weights = jnp.exp2(scores * SCALE2 - widened(taken, scores.shape[1] // HEAD_SIZE))
    part = jnp.dot(weights.astype(jnp.bfloat16), values, preferred_element_type=jnp.float32)
    if first:
        acc[...] = part
    else:
        acc[...] = acc[...] * widened(jnp.exp2(held - new), 2) + part
    top[...] = new


def diagonal():
    rows = lax.broadcasted_iota(jnp.int32, (HEAD_SIZE, HEAD_SIZE), 0)
    columns = lax.broadcasted_iota(jnp.int32, (HEAD_SIZE, HEAD_SIZE), 1)
    return rows == columns


def closed(acc, top):
    totals = jnp.maximum(acc[:, HEAD_SIZE:], 1e-30)
    context = acc[:, :HEAD_SIZE] / totals
    logs = top[...] + jnp.log2(totals)
    eye = diagonal()
    lines = [
        jnp.sum(
            jnp.where(eye, logs[r : r + HEAD_SIZE], 0.0), axis=0, keepdims=True
        )
        for r in range(0, logs.shape[0], HEAD_SIZE)
    ]
    return context, jnp.concatenate(lines, axis=0)


def merged(own, own_logs, other, other_logs):
    most = jnp.maximum(own_logs, other_logs)
    mine = jnp.exp2(own_logs - most)
    total = mine + jnp.exp2(other_logs - most)
    share = mine / total
    eye = diagonal()
    columns = [
        jnp.broadcast_to(
            jnp.sum(
                jnp.where(eye, share[r : r + 1], 0.0), axis=1, keepdims=True
            ),
            (HEAD_SIZE, HEAD_SIZE),
        )
        for r in range(share.shape[0])
    ]
    other = other.astype(jnp.float32)
    return other + jnp.concatenate(columns, axis=0) * (own - other), most + jnp.log2(total)


def turn_kernel(q_ref, cos_ref, sin_ref, out_ref):
    tokens = q_ref.shape[1]
    for h in range(q_ref.shape[2] // HEAD_SIZE):
        spot = slice(h % PAIR * tokens, (h % PAIR + 1) * tokens)
        out_ref[h // PAIR, spot] = turned(
            q_ref[0, :, h * HEAD_SIZE : (h + 1) * HEAD_SIZE], cos_ref[...], sin_ref[...]
        )


def home_kernel(
    picks_ref, q_ref, span_ref, cos_ref, sin_ref, cache_ref, out_ref, logs_ref,
    acc, top, values,
):
    tokens = cos_ref.shape[0]
    kv_heads = cache_ref.shape[2] // HEAD_SIZE
    halves = q_ref.shape[0] // kv_heads
    blocks_here = cache_ref.shape[1] // BLOCK_TOKENS
    values[:, HEAD_SIZE:] = jnp.ones((tokens, HEAD_SIZE), values.dtype)

    @pl.loop(0, kv_heads)
    def _(g):
        spot = pl.ds(pl.multiple_of(g * HEAD_SIZE, HEAD_SIZE), HEAD_SIZE)
        values[:, :HEAD_SIZE] = span_ref[1, :, spot]
        own_keys = turned(span_ref[0, :, spot], cos_ref[...], sin_ref[...])
        rows = lax.broadcasted_iota(jnp.int32, (tokens, tokens), 0)
        columns = lax.broadcasted_iota(jnp.int32, (tokens, tokens), 1)
        causal = jnp.concatenate([columns <= rows] * PAIR, axis=0)
        for i in range(halves):
            fold(q_ref[g * halves + i], own_keys, values[...], None, causal, True, acc.at[i], top.at[i])

        @pl.loop(0, CHOSEN_BLOCKS)
        def _(n):
            block = picks_ref[g * CHOSEN_BLOCKS + n]

            @pl.when((block >= 0) & (block < blocks_here))
            def _():
                lines = pl.ds(pl.multiple_of(block * BLOCK_TOKENS, BLOCK_TOKENS), BLOCK_TOKENS)
                values[:, :HEAD_SIZE] = cache_ref[1, lines, spot]
                for i in range(halves):
                    fold(
                        q_ref[g * halves + i], cache_ref[0, lines, spot], values[...], None, None, False,
                        acc.at[i], top.at[i],
                    )

        for i in range(halves):
            out_ref[g * halves + i], logs_ref[g * halves + i] = closed(acc[i], top[i])


def relay_kernel(
    n_seg, shift_ref, own_ref, own_logs_ref, cache_ref, ql_ref, qr_ref, out_ref,
    q_buf, k_buf, v_buf, buf, logs, stash, stash_logs, acc, top,
    load_sem, q_send, q_recv, p_send, p_recv, l_send, l_recv, o_send, o_recv,
):
    me = lax.axis_index("ctx")
    seg = lax.axis_index("segment")
    side = me // 2
    ahead = 1 - 2 * side
    is_mid = (me == 1) | (me == 2)
    is_end = (me == 0) | (me == 3)
    forth, back = side, 1 - side
    kv_heads, slots = k_buf.shape[0], k_buf.shape[1]
    chunks, rows = ql_ref.shape[0], ql_ref.shape[1]
    tokens = rows // PAIR
    halves = chunks // kv_heads
    blocks_here = slots // BLOCK_TOKENS
    after = lax.rem(seg + 1, n_seg)
    before = lax.rem(seg + n_seg - 1, n_seg)

    def seen(b):
        return b * ahead + 3 * side

    def load(i, source, target):
        return pltpu.make_async_copy(source, target, load_sem.at[i])

    def head_loads(g):
        spot = pl.ds(pl.multiple_of(g * HEAD_SIZE, HEAD_SIZE), HEAD_SIZE)
        return (
            load(2 * g, cache_ref.at[0, :, spot], k_buf.at[g]),
            load(2 * g + 1, cache_ref.at[1, :, spot], v_buf.at[g, :, pl.ds(0, HEAD_SIZE)]),
        )

    loads = []
    for g in range(kv_heads):
        loads.append(head_loads(g))
    from_left = load(2 * kv_heads, ql_ref, q_buf.at[lax.max(me - 1, 0)])
    from_right = load(2 * kv_heads + 1, qr_ref, q_buf.at[lax.min(me + 1, 3)])
    @pl.when(me > 0)
    def _():
        from_left.start()

    @pl.when(me < 3)
    def _():
        from_right.start()

    for copies in loads:
        for copy in copies:
            copy.start()

    barrier = pltpu.get_barrier_semaphore()

    def greet(**place):
        pl.semaphore_signal(barrier, inc=1, device_id=place, device_id_type=MESH)

    @pl.when(me > 0)
    def _():
        greet(ctx=me - 1)

    @pl.when(me < 3)
    def _():
        greet(ctx=me + 1)

    others = (after,) if n_seg == 2 else (after, before)
    for other in others:
        greet(segment=other)

    @pl.when(is_mid)
    def _():
        pl.semaphore_wait(barrier, 2 + len(others))

    @pl.when(is_end)
    def _():
        pl.semaphore_wait(barrier, 1 + len(others))

    def q_copy(source, b, k, target):
        return pltpu.make_async_remote_copy(
            src_ref=source,
            dst_ref=q_buf.at[b, k],
            send_sem=q_send.at[b, k],
            recv_sem=q_recv.at[b, k],
            device_id={"ctx": target},
            device_id_type=MESH,
        )

    def second_hops(k):
        left = q_copy(qr_ref.at[k], lax.min(me + 1, 3), k, lax.max(me - 1, 0))
        right = q_copy(ql_ref.at[k], lax.max(me - 1, 0), k, lax.min(me + 1, 3))
        return left, right

    def third_hop(k):
        b = seen(3)
        return q_copy(q_buf.at[b, k], b, k, me - ahead)

    def part_copies(way, p, k, target):
        return (
            pltpu.make_async_remote_copy(
                src_ref=buf.at[way, p, k],
                dst_ref=buf.at[way, p, k],
                send_sem=p_send.at[way, p, k],
                recv_sem=p_recv.at[way, p, k],
                device_id={"ctx": target},
                device_id_type=MESH,
            ),
            pltpu.make_async_remote_copy(
                src_ref=logs.at[way, p, k],
                dst_ref=logs.at[way, p, k],
                send_sem=l_send.at[way, p, k],
                recv_sem=l_recv.at[way, p, k],
                device_id={"ctx": target},
                device_id_type=MESH,
            ),
        )

    def arrived(way, p, k):
        for copy in part_copies(way, p, k, me + ahead):
            copy.wait_recv()

    def send(way, p, k, target):
        for copy in part_copies(way, p, k, target):
            copy.start()

    def out_copies(way, p, k):
        return [
            pltpu.make_async_remote_copy(
                src_ref=buf.at[way, p, k, pl.ds(i * tokens, tokens)],
                dst_ref=out_ref.at[
                    0,
                    :,
                    pl.ds(pl.multiple_of((k * PAIR + i) * HEAD_SIZE, HEAD_SIZE), HEAD_SIZE),
                ],
                send_sem=o_send.at[k, i],
                recv_sem=o_recv.at[k, i],
                device_id={"segment": after},
                device_id_type=MESH,
            )
            for i in range(PAIR)
        ]

    def relay(way, p, k, own, own_log, target):
        arrived(way, p, k)
        value, log = merged(own, own_log, buf[way, p, k], logs[way, p, k])
        buf[way, p, k] = value.astype(buf.dtype)
        logs[way, p, k] = log
        send(way, p, k, target)

    def near(u):
        p, k = u // chunks, lax.rem(u, chunks)
        relay(forth, p, k, stash[p - 1, k], stash_logs[p - 1, k], me + ahead)

    def mid_final(k):
        arrived(forth, 0, k)
        arrived(back, 1, k)
        value, log = merged(own_ref[k], own_logs_ref[k], buf[forth, 0, k], logs[forth, 0, k])
        value, log = merged(value, log, buf[back, 1, k], logs[back, 1, k])
        buf[back, 1, k] = value.astype(buf.dtype)
        for copy in out_copies(back, 1, k):
            copy.start()

    def end_final(k):
        arrived(back, 2, k)
        value, log = merged(own_ref[k], own_logs_ref[k], buf[back, 2, k], logs[back, 2, k])
        buf[back, 2, k] = value.astype(buf.dtype)
        for copy in out_copies(back, 2, k):
            copy.start()

    @pl.when(is_mid)
    def _():
        @pl.loop(0, chunks)
        def _(k):
            for copy in second_hops(k):
                copy.start()

    for g in range(kv_heads):
        v_buf[g, :, HEAD_SIZE:] = jnp.ones((slots, HEAD_SIZE), v_buf.dtype)

    @pl.when(me > 0)
    def _():
        from_left.wait()

    @pl.when(me < 3)
    def _():
        from_right.wait()

    steps, lead = 3 * chunks, chunks // 2

    @pl.loop(0, steps)
    def _(t):
        late = t - lead
        place = jnp.where(
            is_mid,
            lax.rem(t // chunks + 2, 4),
            jnp.where((late < 0) | (late >= 2 * chunks), 1, 2 + late // chunks),
        )
        k = jnp.where(
            is_mid,
            lax.rem(t, chunks),
            jnp.where(late < 0, t, jnp.where(late < 2 * chunks, lax.rem(late + chunks, chunks), t - 2 * chunks)),
        )
        g = k // halves
        b = seen(place)

        @pl.when((t < chunks) & is_mid & (lax.rem(t, halves) == 0))
        def _():
            for copy in head_loads(g):
                copy.wait()

        @pl.when(is_end & (lax.rem(t, halves) == 0) & ((t < lead) | ((t >= 2 * lead) & (t < chunks + lead))))
        def _():
            for copy in head_loads(g):
                copy.wait()

        @pl.when(is_end & (late >= 0) & (late < 2 * chunks))
        def _():
            q_copy(q_buf.at[b, k], b, k, me + ahead).wait_recv()

        @pl.when(is_mid & (t >= 2) & (t < chunks + 2))
        def _():
            copy = third_hop(t - 2)
            copy.wait_recv()
            copy.start()

        query = q_buf[b, k]
        for j in range(blocks_here):
            lines = slice(j * BLOCK_TOKENS, (j + 1) * BLOCK_TOKENS)
            fold(
                query, k_buf[g, lines], v_buf[g, lines],
                shift_ref[(b * kv_heads + g) * blocks_here + j], None, j == 0, acc, top,
            )
        context, log = closed(acc[...], top[...])

        @pl.when(is_end)
        def _():
            buf[forth, place - 1, k] = context.astype(buf.dtype)
            logs[forth, place - 1, k] = log
            send(forth, place - 1, k, me + ahead)

        @pl.when(is_mid & (t < 2 * chunks))
        def _():
            stash[t // chunks, k] = context
            stash_logs[t // chunks, k] = log

        @pl.when(is_mid & (t >= 2 * chunks))
        def _():
            relay(back, 2, k, context, log, me - ahead)

        @pl.when(is_mid & (t + 2 >= chunks) & (t + 2 < 3 * chunks))
        def _():
            near(t + 2)

        @pl.when(is_mid & (t >= chunks + 2) & (t < chunks + 2 + lead))
        def _():
            mid_final(t - chunks - 2)

        @pl.when(is_mid & (t >= 2 * chunks + 2 + lead))
        def _():
            mid_final(t - 2 * chunks - 2)

        @pl.when(is_end & (t >= 2 * chunks + 3))
        def _():
            end_final(t - 2 * chunks - 3)

    @pl.when(is_mid)
    def _():
        @pl.loop(chunks - 2, chunks)
        def _(k):
            mid_final(k)

    @pl.when(is_end)
    def _():
        @pl.loop(chunks - 3, chunks)
        def _(k):
            end_final(k)

    @pl.when(is_mid)
    def _():
        @pl.loop(0, chunks)
        def _(k):
            for copy in second_hops(k) + (third_hop(k),):
                copy.wait_send()
            for copy in part_copies(forth, 1, k, me + ahead) + part_copies(forth, 2, k, me + ahead):
                copy.wait_send()
            for copy in part_copies(back, 2, k, me - ahead):
                copy.wait_send()
            for copy in out_copies(back, 1, k):
                copy.wait()

    @pl.when(is_end)
    def _():
        @pl.loop(0, chunks)
        def _(k):
            for p in range(3):
                for copy in part_copies(forth, p, k, me + ahead):
                    copy.wait_send()
            for copy in out_copies(back, 2, k):
                copy.wait()


def local(queries, span_key_values, key_value_cache, chosen, offset):
    n_ctx = lax.axis_size("ctx")
    n_seg = lax.axis_size("segment")
    me = lax.axis_index("ctx")
    tokens = queries.shape[1]
    kv_heads = key_value_cache.shape[3] // HEAD_SIZE
    q_heads = queries.shape[2] // HEAD_SIZE
    per_head = q_heads // kv_heads
    slots = key_value_cache.shape[1]
    blocks_here = slots // BLOCK_TOKENS
    if not (
        n_ctx == 4
        and tokens == BLOCK_TOKENS
        and n_seg > 1
        and per_head % PAIR == 0
        and slots * kv_heads <= 16384
        and q_heads == 8 * PAIR
        and kv_heads == 4
    ):
        return general(queries, span_key_values, key_value_cache, chosen, offset)
    bf16, f32 = jnp.bfloat16, jnp.float32
    dma = pltpu.SemaphoreType.DMA
    chunks, rows = q_heads // PAIR, PAIR * tokens
    lines = rows // HEAD_SIZE
    vmem = pl.BlockSpec(memory_space=pltpu.VMEM)
    smem = pl.BlockSpec(memory_space=pltpu.SMEM)
    anywhere = pl.BlockSpec(memory_space=pl.ANY)

    positions = (offset[0] + me * tokens + jnp.arange(tokens, dtype=jnp.int32)).astype(f32)
    half = HEAD_SIZE // 2
    frequencies = ROPE_BASE ** (-(2.0 * jnp.arange(half, dtype=f32)) / HEAD_SIZE)
    angles = positions[:, None] * frequencies[None, :]
    cosine, sine = jnp.cos(angles), jnp.sin(angles)
    cos_table = jnp.concatenate([cosine, cosine], axis=1)
    sin_table = jnp.concatenate([-sine, sine], axis=1)
    q_own = pl.pallas_call(
        turn_kernel,
        out_shape=jax.ShapeDtypeStruct((chunks, rows, HEAD_SIZE), bf16),
        in_specs=[vmem] * 3,
        out_specs=vmem,
        cost_estimate=pl.CostEstimate(
            flops=6 * queries.size, bytes_accessed=4 * queries.size, transcendentals=0
        ),
        compiler_params=pltpu.CompilerParams(vmem_limit_bytes=24 * 2**20),
    )(queries, cos_table, sin_table)
    q_left = lax.ppermute(q_own, "ctx", [(i, i + 1) for i in range(n_ctx - 1)])
    q_right = lax.ppermute(q_own, "ctx", [(i + 1, i) for i in range(n_ctx - 1)])

    cache = key_value_cache[0].transpose(1, 0, 2)
    span = span_key_values[0].transpose(1, 0, 2)
    first_block = me * blocks_here
    picks = lax.dynamic_index_in_dim(chosen[0], me, 0, keepdims=False) - first_block
    here = first_block + jnp.arange(blocks_here, dtype=jnp.int32)
    taken = jnp.any(chosen[0][..., None] == here, axis=2)
    shift = jnp.where(taken, 0.0, HIDDEN).astype(f32).reshape(-1)
    work = 4 * q_heads * tokens * BLOCK_TOKENS * HEAD_SIZE
    own, own_logs = pl.pallas_call(
        home_kernel,
        out_shape=(
            jax.ShapeDtypeStruct((chunks, rows, HEAD_SIZE), f32),
            jax.ShapeDtypeStruct((chunks, lines, HEAD_SIZE), f32),
        ),
        in_specs=[smem] + [vmem] * 5,
        out_specs=(vmem, vmem),
        scratch_shapes=[
            pltpu.VMEM((chunks // kv_heads, rows, 2 * HEAD_SIZE), f32),
            pltpu.VMEM((chunks // kv_heads, rows, HEAD_SIZE), f32),
            pltpu.VMEM((tokens, 2 * HEAD_SIZE), bf16),
        ],
        cost_estimate=pl.CostEstimate(
            flops=6 * work, bytes_accessed=16 * 2**20, transcendentals=work // 128
        ),
        compiler_params=pltpu.CompilerParams(vmem_limit_bytes=48 * 2**20),
    )(picks.reshape(-1), q_own, span, cos_table, sin_table, cache)

    return pl.pallas_call(
        functools.partial(relay_kernel, n_seg),
        out_shape=jax.ShapeDtypeStruct(queries.shape, bf16),
        in_specs=[smem, vmem, vmem] + [anywhere] * 3,
        out_specs=anywhere,
        scratch_shapes=[
            pltpu.VMEM((n_ctx, chunks, rows, HEAD_SIZE), bf16),
            pltpu.VMEM((kv_heads, slots, HEAD_SIZE), bf16),
            pltpu.VMEM((kv_heads, slots, 2 * HEAD_SIZE), bf16),
            pltpu.VMEM((2, 3, chunks, rows, HEAD_SIZE), bf16),
            pltpu.VMEM((2, 3, chunks, lines, HEAD_SIZE), f32),
            pltpu.VMEM((2, chunks, rows, HEAD_SIZE), f32),
            pltpu.VMEM((2, chunks, lines, HEAD_SIZE), f32),
            pltpu.VMEM((rows, 2 * HEAD_SIZE), f32),
            pltpu.VMEM((rows, HEAD_SIZE), f32),
            dma((2 * kv_heads + 2,)),
            dma((n_ctx, chunks)),
            dma((n_ctx, chunks)),
            dma((2, 3, chunks)),
            dma((2, 3, chunks)),
            dma((2, 3, chunks)),
            dma((2, 3, chunks)),
            dma((chunks, PAIR)),
            dma((chunks, PAIR)),
        ],
        cost_estimate=pl.CostEstimate(
            flops=24 * work, bytes_accessed=32 * 2**20, transcendentals=work // 16
        ),
        compiler_params=pltpu.CompilerParams(
            collective_id=0, has_side_effects=True, vmem_limit_bytes=60 * 2**20
        ),
    )(shift, own, own_logs, cache, q_left, q_right)


def solution(mesh):
    return jax.shard_map(
        local,
        mesh=mesh,
        in_specs=(
            P(("groups", "segment"), "ctx", "head"),
            P(("groups", "segment"), "ctx", None, "head"),
            P(("groups", "segment"), "ctx", None, "head"),
            P(("groups", "segment"), None, "head", None),
            P(("groups", "segment")),
        ),
        out_specs=P(("groups", "segment"), "ctx", "head"),
        check_vma=False,
    )
```

```python
import functools

import jax
import jax.numpy as jnp
from jax import lax
from jax.experimental import pallas as pl
from jax.experimental.pallas import tpu as pltpu
from jax.sharding import PartitionSpec as P

HEAD_SIZE = 128
BLOCK_TOKENS = 512
CHOSEN_BLOCKS = 8


ROPE_BASE = 500000.0


def swapped(x, axis, stride):
    return lax.ppermute(x, axis, [(i, i ^ 1 << stride) for i in range(lax.axis_size(axis))])


def passed_along(block, axis, distance):
    devices = range(lax.axis_size(axis))
    route = [((i - distance) % len(devices), i) for i in devices]
    return lax.ppermute(block, axis, route)


def apply_rotary(values, token_positions):
    half_dim = values.shape[-1] // 2
    frequencies = ROPE_BASE ** (-(2.0 * jnp.arange(half_dim, dtype=jnp.float32)) / values.shape[-1])
    angles = token_positions[:, None] * frequencies[None, :]
    cosine = jnp.cos(angles)[:, None, :]
    sine_part = jnp.sin(angles)[:, None, :]
    widened = values.astype(jnp.float32)
    first_half = widened[..., :half_dim]
    second_half = widened[..., half_dim:]
    joined = jnp.concatenate(
        [
            first_half * cosine - second_half * sine_part,
            second_half * cosine + first_half * sine_part,
        ],
        axis=-1,
    )
    return joined.astype(jnp.bfloat16)


def combine(earlier, later):
    maxima = jnp.maximum(earlier[0], later[0])
    first_factor = jnp.exp(earlier[0] - maxima)
    second_factor = jnp.exp(later[0] - maxima)
    totals = earlier[1] * first_factor + later[1] * second_factor
    weighted = earlier[2] * first_factor[..., None] + later[2] * second_factor[..., None]
    return (maxima, totals, weighted)


def general(queries, span_key_values, key_value_cache, chosen, offset):
    ctx_size = lax.axis_size("ctx")
    my_index = lax.axis_index("ctx")
    tok_rows = queries.shape[1]
    kv_heads = key_value_cache.shape[3] // HEAD_SIZE
    q_heads = queries.shape[2] // HEAD_SIZE
    per_value_head = q_heads // kv_heads
    members = ctx_size // kv_heads
    blocks_here = key_value_cache.shape[1] // BLOCK_TOKENS
    blocks_total = blocks_here * ctx_size
    q_blocks = chosen.shape[1]
    per_block = BLOCK_TOKENS // tok_rows
    key_rows = BLOCK_TOKENS // members
    own_rows = tok_rows // members
    my_head = my_index // members
    my_rank = my_index % members
    score_scale = HEAD_SIZE ** (-0.5)
    token_start = offset[0] + my_index * tok_rows
    token_positions = (token_start + jnp.arange(tok_rows, dtype=jnp.int32)).astype(jnp.float32)
    rot_query = apply_rotary(queries[0].reshape(tok_rows, q_heads, HEAD_SIZE), token_positions)
    rotated_key_rows = apply_rotary(
        span_key_values[0, :, 0].reshape(tok_rows, kv_heads, HEAD_SIZE), token_positions
    )
    fresh_values = span_key_values[0, :, 1].reshape(tok_rows, kv_heads, HEAD_SIZE)
    query_send = jnp.broadcast_to(
        rot_query.reshape(tok_rows, kv_heads, 1, per_value_head * HEAD_SIZE),
        (tok_rows, kv_heads, members, per_value_head * HEAD_SIZE),
    )
    query_send = query_send.reshape(tok_rows, ctx_size, per_value_head * HEAD_SIZE)
    pair_rows = jnp.concatenate([rotated_key_rows, fresh_values], axis=-1)
    pair_send = (
        pair_rows.reshape(members, own_rows, kv_heads, 2 * HEAD_SIZE)
        .transpose(1, 2, 0, 3)
        .reshape(own_rows, ctx_size, 2 * HEAD_SIZE)
    )
    query_recv, pair_recv = (
        lax.all_to_all(query_send, "ctx", split_axis=1, concat_axis=1, tiled=True),
        lax.all_to_all(pair_send, "ctx", split_axis=1, concat_axis=1, tiled=True),
    )
    picks_here = chosen[0]
    needed = jnp.any(
        picks_here[..., None] == jnp.arange(blocks_total, dtype=jnp.int32), axis=(0, 2)
    )
    needed_here = lax.dynamic_slice_in_dim(needed, my_index * blocks_here, blocks_here, axis=1)
    needed_here = needed_here.T.reshape(blocks_here, 1, kv_heads, 1, 1, 1)
    arranged_rows = (
        key_value_cache[0]
        .reshape(blocks_here, members, key_rows, 2, kv_heads, HEAD_SIZE)
        .transpose(0, 2, 4, 1, 3, 5)
    )
    arranged_rows = jnp.where(needed_here, arranged_rows, jnp.zeros((), jnp.bfloat16))
    tile_send = arranged_rows.reshape(blocks_here * key_rows, ctx_size, 2 * HEAD_SIZE)
    fetched = lax.all_to_all(tile_send, "ctx", split_axis=1, concat_axis=1, tiled=True)
    fetched = fetched.reshape(blocks_here, key_rows, ctx_size, 2 * HEAD_SIZE)
    maxima_parts = []
    totals_parts = []
    weighted_parts = []
    for index_of_block in range(q_blocks):
        block_ids = picks_here[index_of_block][my_head]
        owner_rank = block_ids // blocks_here
        slot_index = block_ids % blocks_here
        picked = jnp.stack(
            [
                lax.dynamic_slice(
                    fetched,
                    (slot_index[n], 0, owner_rank[n], 0),
                    (1, key_rows, 1, 2 * HEAD_SIZE),
                )[0, :, 0]
                for n in range(CHOSEN_BLOCKS)
            ]
        )
        sel_keys = picked[..., :HEAD_SIZE].reshape(CHOSEN_BLOCKS * key_rows, HEAD_SIZE)
        sel_values = picked[..., HEAD_SIZE:].reshape(CHOSEN_BLOCKS * key_rows, HEAD_SIZE)
        first_source = index_of_block * per_block
        own_pairs = pair_recv[:, first_source : first_source + per_block]
        own_keys = own_pairs[..., :HEAD_SIZE].reshape(own_rows * per_block, HEAD_SIZE)
        own_values = own_pairs[..., HEAD_SIZE:].reshape(own_rows * per_block, HEAD_SIZE)
        query_rows = query_recv[:, first_source : first_source + per_block].reshape(
            tok_rows * per_block * per_value_head, HEAD_SIZE
        )
        sources = first_source + jnp.arange(per_block, dtype=jnp.int32)
        query_token = sources[None, :] * tok_rows + jnp.arange(tok_rows, dtype=jnp.int32)[:, None]
        query_token = jnp.broadcast_to(
            query_token[:, :, None], (tok_rows, per_block, per_value_head)
        ).reshape(-1)
        key_token = (
            sources[None, :] * tok_rows
            + my_rank * own_rows
            + jnp.arange(own_rows, dtype=jnp.int32)[:, None]
        )
        key_token = key_token.reshape(-1)
        sel_scores = (
            jnp.dot(query_rows, sel_keys.T, preferred_element_type=jnp.float32) * score_scale
        )
        own_scores = (
            jnp.dot(query_rows, own_keys.T, preferred_element_type=jnp.float32) * score_scale
        )
        causal = key_token[None, :] <= query_token[:, None]
        own_scores = jnp.where(causal, own_scores, -jnp.inf)
        maxima = jnp.maximum(jnp.max(sel_scores, axis=1), jnp.max(own_scores, axis=1))
        sel_weights = jnp.exp(sel_scores - maxima[:, None])
        own_weights = jnp.exp(own_scores - maxima[:, None])
        totals = jnp.sum(sel_weights, axis=1) + jnp.sum(own_weights, axis=1)
        weighted = jnp.dot(
            sel_weights, sel_values.astype(jnp.float32), precision=lax.Precision.HIGHEST
        )
        weighted = weighted + jnp.dot(
            own_weights, own_values.astype(jnp.float32), precision=lax.Precision.HIGHEST
        )
        maxima_parts.append(maxima.reshape(tok_rows, per_block, per_value_head))
        totals_parts.append(totals.reshape(tok_rows, per_block, per_value_head))
        weighted_parts.append(weighted.reshape(tok_rows, per_block, per_value_head, HEAD_SIZE))
    maxima_all = jnp.concatenate(maxima_parts, axis=1)
    totals_all = jnp.concatenate(totals_parts, axis=1)
    weighted_all = jnp.concatenate(weighted_parts, axis=1)
    current = (maxima_all, totals_all, weighted_all)
    bit_count = members.bit_length() - 1
    for bit_index in reversed(range(bit_count)):
        half_rows = current[0].shape[0] // 2
        my_bit = my_index // 2**bit_index % 2
        kept = tuple(
            (
                lax.dynamic_slice_in_dim(part_array, my_bit * half_rows, half_rows, 0)
                for part_array in current
            )
        )
        given = tuple(
            (
                lax.dynamic_slice_in_dim(part_array, (1 - my_bit) * half_rows, half_rows, 0)
                for part_array in current
            )
        )
        partner = swapped((given[0], given[1], given[2]), "ctx", bit_index)
        current = combine(kept, partner)
    finished = (
        (current[2] / current[1][..., None])
        .astype(jnp.bfloat16)
        .reshape(own_rows, ctx_size, per_value_head * HEAD_SIZE)
    )
    returned = lax.all_to_all(finished, "ctx", split_axis=1, concat_axis=1, tiled=True)
    context = (
        returned.reshape(own_rows, kv_heads, members, per_value_head * HEAD_SIZE)
        .transpose(2, 0, 1, 3)
        .reshape(tok_rows, q_heads * HEAD_SIZE)
    )
    handed = passed_along(context, "segment", 1)
    return handed[None]


LOG2E = 1.4426950408889634
MESH = pl.DeviceIdType.MESH
PAIR = 2
NOTHING = -1e29
HIDDEN = 1e30
SCALE2 = LOG2E * HEAD_SIZE ** (-0.5)


def turned(block, cosine, sine):
    wide = block.astype(jnp.float32)
    other = pltpu.roll(wide, HEAD_SIZE // 2, 1)
    return (wide * cosine + other * sine).astype(jnp.bfloat16)


def widened(column, count):
    return jnp.concatenate([column] * count, axis=1)


def fold(query, keys, values, shift, causal, first, acc, top):
    scores = lax.dot_general(
        query, keys, (((1,), (1,)), ((), ())), preferred_element_type=jnp.float32
    )
    if causal is not None:
        scores = jnp.where(causal, scores, -jnp.inf)
    new = jnp.max(scores, axis=1, keepdims=True) * SCALE2
    if shift is not None:
        new = new - shift
    new = jnp.broadcast_to(new, (scores.shape[0], HEAD_SIZE))
    if first:
        new = jnp.maximum(new, NOTHING)
    else:
        held = top[...]
        new = jnp.maximum(new, held)
    taken = new if shift is None else new + shift
    weights = jnp.exp2(scores * SCALE2 - widened(taken, scores.shape[1] // HEAD_SIZE))
    part = jnp.dot(weights.astype(jnp.bfloat16), values, preferred_element_type=jnp.float32)
    if first:
        acc[...] = part
    else:
        acc[...] = acc[...] * widened(jnp.exp2(held - new), 2) + part
    top[...] = new


def diagonal():
    rows = lax.broadcasted_iota(jnp.int32, (HEAD_SIZE, HEAD_SIZE), 0)
    columns = lax.broadcasted_iota(jnp.int32, (HEAD_SIZE, HEAD_SIZE), 1)
    return rows == columns


def closed(acc, top):
    totals = jnp.maximum(acc[:, HEAD_SIZE:], 1e-30)
    context = acc[:, :HEAD_SIZE] / totals
    logs = top[...] + jnp.log2(totals)
    eye = diagonal()
    lines = [
        jnp.sum(
            jnp.where(eye, logs[r : r + HEAD_SIZE], 0.0), axis=0, keepdims=True
        )
        for r in range(0, logs.shape[0], HEAD_SIZE)
    ]
    return context, jnp.concatenate(lines, axis=0)


def merged(own, own_logs, other, other_logs):
    most = jnp.maximum(own_logs, other_logs)
    mine = jnp.exp2(own_logs - most)
    total = mine + jnp.exp2(other_logs - most)
    share = mine / total
    eye = diagonal()
    columns = [
        jnp.broadcast_to(
            jnp.sum(
                jnp.where(eye, share[r : r + 1], 0.0), axis=1, keepdims=True
            ),
            (HEAD_SIZE, HEAD_SIZE),
        )
        for r in range(share.shape[0])
    ]
    other = other.astype(jnp.float32)
    return other + jnp.concatenate(columns, axis=0) * (own - other), most + jnp.log2(total)


def turn_kernel(q_ref, cos_ref, sin_ref, out_ref):
    tokens = q_ref.shape[1]
    for h in range(q_ref.shape[2] // HEAD_SIZE):
        spot = slice(h % PAIR * tokens, (h % PAIR + 1) * tokens)
        out_ref[h // PAIR, spot] = turned(
            q_ref[0, :, h * HEAD_SIZE : (h + 1) * HEAD_SIZE], cos_ref[...], sin_ref[...]
        )


def home_kernel(
    picks_ref, q_ref, span_ref, cos_ref, sin_ref, cache_ref, out_ref, logs_ref,
    acc, top, values, held, made, load_sem, store_sem,
):
    tokens = cos_ref.shape[0]
    kv_heads = cache_ref.shape[2] // HEAD_SIZE
    halves = q_ref.shape[0] // kv_heads
    blocks_here = cache_ref.shape[1] // BLOCK_TOKENS

    def load(g):
        spot = pl.ds(pl.multiple_of(g * HEAD_SIZE, HEAD_SIZE), HEAD_SIZE)
        return pltpu.make_async_copy(cache_ref.at[:, :, spot], held.at[g], load_sem.at[g])

    def store(g):
        lines = pl.ds(g * halves, halves)
        return pltpu.make_async_copy(made.at[lines], out_ref.at[lines], store_sem.at[g])

    for g in range(kv_heads):
        load(g).start()
    values[:, HEAD_SIZE:] = jnp.ones((tokens, HEAD_SIZE), values.dtype)

    @pl.loop(0, kv_heads)
    def _(g):
        spot = pl.ds(pl.multiple_of(g * HEAD_SIZE, HEAD_SIZE), HEAD_SIZE)
        values[:, :HEAD_SIZE] = span_ref[1, :, spot]
        own_keys = turned(span_ref[0, :, spot], cos_ref[...], sin_ref[...])
        rows = lax.broadcasted_iota(jnp.int32, (tokens, tokens), 0)
        columns = lax.broadcasted_iota(jnp.int32, (tokens, tokens), 1)
        causal = jnp.concatenate([columns <= rows] * PAIR, axis=0)
        for i in range(halves):
            fold(q_ref[g * halves + i], own_keys, values[...], None, causal, True, acc.at[i], top.at[i])
        load(g).wait()

        @pl.loop(0, CHOSEN_BLOCKS)
        def _(n):
            block = picks_ref[g * CHOSEN_BLOCKS + n]

            @pl.when((block >= 0) & (block < blocks_here))
            def _():
                lines = pl.ds(pl.multiple_of(block * BLOCK_TOKENS, BLOCK_TOKENS), BLOCK_TOKENS)
                values[:, :HEAD_SIZE] = held[g, 1, lines]
                for i in range(halves):
                    fold(
                        q_ref[g * halves + i], held[g, 0, lines], values[...], None, None, False,
                        acc.at[i], top.at[i],
                    )

        for i in range(halves):
            made[g * halves + i], logs_ref[g * halves + i] = closed(acc[i], top[i])
        store(g).start()

    for g in range(kv_heads):
        store(g).wait()


def relay_kernel(
    n_seg, shift_ref, own_ref, own_logs_ref, cache_ref, ql_ref, qr_ref, out_ref,
    q_buf, k_buf, v_buf, buf, logs, stash, stash_logs, acc_0, acc_1, top_0, top_1,
    load_sem, q_send, q_recv, p_send, p_recv, l_send, l_recv, o_send, o_recv,
):
    me = lax.axis_index("ctx")
    seg = lax.axis_index("segment")
    side = me // 2
    ahead = 1 - 2 * side
    is_mid = (me == 1) | (me == 2)
    is_end = (me == 0) | (me == 3)
    forth, back = side, 1 - side
    kv_heads, slots = k_buf.shape[0], k_buf.shape[1]
    chunks, rows = ql_ref.shape[0], ql_ref.shape[1]
    tokens = rows // PAIR
    halves = chunks // kv_heads
    lead = kv_heads // 2
    blocks_here = slots // BLOCK_TOKENS
    after = lax.rem(seg + 1, n_seg)
    before = lax.rem(seg + n_seg - 1, n_seg)

    def seen(b):
        return b * ahead + 3 * side

    def load(i, source, target):
        return pltpu.make_async_copy(source, target, load_sem.at[i])

    def head_loads(g):
        spot = pl.ds(pl.multiple_of(g * HEAD_SIZE, HEAD_SIZE), HEAD_SIZE)
        return (
            load(2 * g, cache_ref.at[0, :, spot], k_buf.at[g]),
            load(2 * g + 1, cache_ref.at[1, :, spot], v_buf.at[g, :, pl.ds(0, HEAD_SIZE)]),
        )

    loads = []
    for g in range(kv_heads):
        loads.append(head_loads(g))
    from_left = load(2 * kv_heads, ql_ref, q_buf.at[lax.max(me - 1, 0)])
    from_right = load(2 * kv_heads + 1, qr_ref, q_buf.at[lax.min(me + 1, 3)])
    @pl.when(me > 0)
    def _():
        from_left.start()

    @pl.when(me < 3)
    def _():
        from_right.start()

    for copies in loads:
        for copy in copies:
            copy.start()

    barrier = pltpu.get_barrier_semaphore()

    def greet(**place):
        pl.semaphore_signal(barrier, inc=1, device_id=place, device_id_type=MESH)

    @pl.when(me > 0)
    def _():
        greet(ctx=me - 1)

    @pl.when(me < 3)
    def _():
        greet(ctx=me + 1)

    others = (after,) if n_seg == 2 else (after, before)
    for other in others:
        greet(segment=other)

    @pl.when(is_mid)
    def _():
        pl.semaphore_wait(barrier, 2 + len(others))

    @pl.when(is_end)
    def _():
        pl.semaphore_wait(barrier, 1 + len(others))

    def q_copy(source, b, k, target):
        return pltpu.make_async_remote_copy(
            src_ref=source,
            dst_ref=q_buf.at[b, k],
            send_sem=q_send.at[b, k],
            recv_sem=q_recv.at[b, k],
            device_id={"ctx": target},
            device_id_type=MESH,
        )

    def second_hops(k):
        left = q_copy(qr_ref.at[k], lax.min(me + 1, 3), k, lax.max(me - 1, 0))
        right = q_copy(ql_ref.at[k], lax.max(me - 1, 0), k, lax.min(me + 1, 3))
        return left, right

    def third_hop(k):
        b = seen(3)
        return q_copy(q_buf.at[b, k], b, k, me - ahead)

    def part_copies(way, p, k, target):
        return (
            pltpu.make_async_remote_copy(
                src_ref=buf.at[way, p, k],
                dst_ref=buf.at[way, p, k],
                send_sem=p_send.at[way, p, k],
                recv_sem=p_recv.at[way, p, k],
                device_id={"ctx": target},
                device_id_type=MESH,
            ),
            pltpu.make_async_remote_copy(
                src_ref=logs.at[way, p, k],
                dst_ref=logs.at[way, p, k],
                send_sem=l_send.at[way, p, k],
                recv_sem=l_recv.at[way, p, k],
                device_id={"ctx": target},
                device_id_type=MESH,
            ),
        )

    def arrived(way, p, k):
        for copy in part_copies(way, p, k, me + ahead):
            copy.wait_recv()

    def send(way, p, k, target):
        for copy in part_copies(way, p, k, target):
            copy.start()

    def out_copies(way, p, k):
        return [
            pltpu.make_async_remote_copy(
                src_ref=buf.at[way, p, k, pl.ds(i * tokens, tokens)],
                dst_ref=out_ref.at[
                    0,
                    :,
                    pl.ds(pl.multiple_of((k * PAIR + i) * HEAD_SIZE, HEAD_SIZE), HEAD_SIZE),
                ],
                send_sem=o_send.at[k, i],
                recv_sem=o_recv.at[k, i],
                device_id={"segment": after},
                device_id_type=MESH,
            )
            for i in range(PAIR)
        ]

    def relay(way, p, k, own, own_log, target):
        arrived(way, p, k)
        value, log = merged(own, own_log, buf[way, p, k], logs[way, p, k])
        buf[way, p, k] = value.astype(buf.dtype)
        logs[way, p, k] = log
        send(way, p, k, target)

    def near(i):
        rest = lax.rem(i, 2 * lead)
        kind = rest // lead
        g = i // (2 * lead) * lead + lax.rem(i, lead)
        for n in range(halves):
            relay(
                forth, kind + 1, g * halves + n, stash[kind, lax.rem(i, lead), n],
                stash_logs[kind, lax.rem(i, lead), n], me + ahead,
            )

    def far(g, n):
        row = lax.rem(g, lead)
        relay(back, 2, g * halves + n, stash[2, row, n], stash_logs[2, row, n], me - ahead)

    def mid_final(k):
        arrived(forth, 0, k)
        arrived(back, 1, k)
        value, log = merged(own_ref[k], own_logs_ref[k], buf[forth, 0, k], logs[forth, 0, k])
        value, log = merged(value, log, buf[back, 1, k], logs[back, 1, k])
        buf[back, 1, k] = value.astype(buf.dtype)
        for copy in out_copies(back, 1, k):
            copy.start()

    def end_final(k):
        arrived(back, 2, k)
        value, log = merged(own_ref[k], own_logs_ref[k], buf[back, 2, k], logs[back, 2, k])
        buf[back, 2, k] = value.astype(buf.dtype)
        for copy in out_copies(back, 2, k):
            copy.start()

    def hop_back(k):
        @pl.when(side == 0)
        def _():
            second_hops(k)[0].start()

        @pl.when(side == 1)
        def _():
            second_hops(k)[1].start()

    @pl.when(is_mid)
    def _():
        @pl.loop(0, chunks // 2)
        def _(k):
            for copy in second_hops(k):
                copy.start()

        @pl.loop(chunks // 2, chunks)
        def _(k):
            @pl.when(side == 0)
            def _():
                second_hops(k)[1].start()

            @pl.when(side == 1)
            def _():
                second_hops(k)[0].start()

    for g in range(kv_heads):
        v_buf[g, :, HEAD_SIZE:] = jnp.ones((slots, HEAD_SIZE), v_buf.dtype)

    @pl.when(me > 0)
    def _():
        from_left.wait()

    @pl.when(me < 3)
    def _():
        from_right.wait()

    steps = 3 * kv_heads

    def task(s):
        part, kind = s // (3 * lead), lax.rem(s, 3 * lead) // lead
        place = jnp.where(
            is_mid,
            lax.rem(kind + 2, 4),
            jnp.where(part == 0, kind + 1, lax.rem(kind + 1, 3) + 1),
        )
        return place, kind, part * lead + lax.rem(s, lead)

    def folds(b, g, numbers, states):
        for j in range(blocks_here):
            lines = slice(j * BLOCK_TOKENS, (j + 1) * BLOCK_TOKENS)
            shift = shift_ref[(b * kv_heads + g) * blocks_here + j]
            for n, (acc, top) in zip(numbers, states):
                fold(
                    q_buf[b, g * halves + n], k_buf[g, lines], v_buf[g, lines],
                    shift, None, j == 0, acc, top,
                )
        return [closed(acc[...], top[...]) for acc, top in states]

    def keep(s, n, context, log):
        place, kind, g = task(s)
        k = g * halves + n

        @pl.when(is_end)
        def _():
            buf[forth, place - 1, k] = context.astype(buf.dtype)
            logs[forth, place - 1, k] = log
            send(forth, place - 1, k, me + ahead)

        @pl.when(is_mid)
        def _():
            stash[kind, lax.rem(s, lead), n] = context
            stash_logs[kind, lax.rem(s, lead), n] = log

    place_0, _, _ = task(0)
    for copy in head_loads(0):
        copy.wait()

    @pl.loop(0, halves)
    def _(n):
        ((context, log),) = folds(seen(place_0), 0, [n], [(acc_0, top_0)])
        keep(0, n, context, log)

    @pl.loop(1, steps)
    def _(s):
        place, kind, g = task(s)
        b = seen(place)

        @pl.when((s < lead) | ((s >= 3 * lead) & (s < 4 * lead)))
        def _():
            for copy in head_loads(g):
                copy.wait()

        @pl.when(is_end & (place > 1))
        def _():
            for n in range(halves):
                k = g * halves + n
                q_copy(q_buf.at[b, k], b, k, me + ahead).wait_recv()

        parts = folds(b, g, range(halves), [(acc_0, top_0), (acc_1, top_1)])
        for n in range(halves):
            keep(s, n, *parts[n])

        @pl.when(is_mid & (s < kv_heads + 1))
        def _():
            for n in range(halves):
                copy = third_hop((s - 1) * halves + n)
                copy.wait_recv()
                copy.start()

        @pl.when(is_mid & (s == lead))
        def _():
            @pl.loop(chunks // 2, chunks)
            def _(k):
                hop_back(k)

        @pl.when(is_mid & (s >= 3) & (s < steps - 1))
        def _():
            near(s - 3)

        @pl.when(is_mid & ((s == 7) | (s == 8) | (s == 11)))
        def _():
            for n in range(halves):
                far(jnp.where(s == 11, 2, s - 7), n)

        @pl.when(is_mid & ((s == 5) | (s == 6)))
        def _():
            for n in range(halves):
                mid_final((s - 5) * halves + n)

        @pl.when(is_end & (s >= steps - 2))
        def _():
            for n in range(halves):
                end_final((s - steps + 2) * halves + n)

    @pl.when(is_mid)
    def _():
        mid_final(chunks - 4)
        far(kv_heads - 1, 0)
        mid_final(chunks - 3)
        far(kv_heads - 1, 1)
        mid_final(chunks - 2)
        mid_final(chunks - 1)

    @pl.when(is_end)
    def _():
        @pl.loop(chunks // 2, chunks)
        def _(k):
            end_final(k)

    @pl.when(is_mid)
    def _():
        @pl.loop(0, chunks)
        def _(k):
            for copy in second_hops(k) + (third_hop(k),):
                copy.wait_send()
            for copy in part_copies(forth, 1, k, me + ahead) + part_copies(forth, 2, k, me + ahead):
                copy.wait_send()
            for copy in part_copies(back, 2, k, me - ahead):
                copy.wait_send()
            for copy in out_copies(back, 1, k):
                copy.wait()

    @pl.when(is_end)
    def _():
        @pl.loop(0, chunks)
        def _(k):
            for p in range(3):
                for copy in part_copies(forth, p, k, me + ahead):
                    copy.wait_send()
            for copy in out_copies(back, 2, k):
                copy.wait()


def local(queries, span_key_values, key_value_cache, chosen, offset):
    n_ctx = lax.axis_size("ctx")
    n_seg = lax.axis_size("segment")
    me = lax.axis_index("ctx")
    tokens = queries.shape[1]
    kv_heads = key_value_cache.shape[3] // HEAD_SIZE
    q_heads = queries.shape[2] // HEAD_SIZE
    per_head = q_heads // kv_heads
    slots = key_value_cache.shape[1]
    blocks_here = slots // BLOCK_TOKENS
    if not (
        n_ctx == 4
        and tokens == BLOCK_TOKENS
        and n_seg > 1
        and per_head % PAIR == 0
        and slots * kv_heads <= 16384
        and q_heads == 8 * PAIR
        and kv_heads == 4
    ):
        return general(queries, span_key_values, key_value_cache, chosen, offset)
    bf16, f32 = jnp.bfloat16, jnp.float32
    dma = pltpu.SemaphoreType.DMA
    chunks, rows = q_heads // PAIR, PAIR * tokens
    lines = rows // HEAD_SIZE
    vmem = pl.BlockSpec(memory_space=pltpu.VMEM)
    smem = pl.BlockSpec(memory_space=pltpu.SMEM)
    anywhere = pl.BlockSpec(memory_space=pl.ANY)

    positions = (offset[0] + me * tokens + jnp.arange(tokens, dtype=jnp.int32)).astype(f32)
    half = HEAD_SIZE // 2
    frequencies = ROPE_BASE ** (-(2.0 * jnp.arange(half, dtype=f32)) / HEAD_SIZE)
    angles = positions[:, None] * frequencies[None, :]
    cosine, sine = jnp.cos(angles), jnp.sin(angles)
    cos_table = jnp.concatenate([cosine, cosine], axis=1)
    sin_table = jnp.concatenate([-sine, sine], axis=1)
    q_own = pl.pallas_call(
        turn_kernel,
        out_shape=jax.ShapeDtypeStruct((chunks, rows, HEAD_SIZE), bf16),
        in_specs=[vmem] * 3,
        out_specs=vmem,
        cost_estimate=pl.CostEstimate(
            flops=6 * queries.size, bytes_accessed=4 * queries.size, transcendentals=0
        ),
        compiler_params=pltpu.CompilerParams(vmem_limit_bytes=24 * 2**20),
    )(queries, cos_table, sin_table)
    q_left = lax.ppermute(q_own, "ctx", [(i, i + 1) for i in range(n_ctx - 1)])
    q_right = lax.ppermute(q_own, "ctx", [(i + 1, i) for i in range(n_ctx - 1)])

    cache = key_value_cache[0].transpose(1, 0, 2)
    span = span_key_values[0].transpose(1, 0, 2)
    first_block = me * blocks_here
    picks = lax.dynamic_index_in_dim(chosen[0], me, 0, keepdims=False) - first_block
    here = first_block + jnp.arange(blocks_here, dtype=jnp.int32)
    taken = jnp.any(chosen[0][..., None] == here, axis=2)
    shift = jnp.where(taken, 0.0, HIDDEN).astype(f32).reshape(-1)
    work = 4 * q_heads * tokens * BLOCK_TOKENS * HEAD_SIZE
    own, own_logs = pl.pallas_call(
        home_kernel,
        out_shape=(
            jax.ShapeDtypeStruct((chunks, rows, HEAD_SIZE), f32),
            jax.ShapeDtypeStruct((chunks, lines, HEAD_SIZE), f32),
        ),
        in_specs=[smem] + [vmem] * 4 + [anywhere],
        out_specs=(anywhere, vmem),
        scratch_shapes=[
            pltpu.VMEM((chunks // kv_heads, rows, 2 * HEAD_SIZE), f32),
            pltpu.VMEM((chunks // kv_heads, rows, HEAD_SIZE), f32),
            pltpu.VMEM((tokens, 2 * HEAD_SIZE), bf16),
            pltpu.VMEM((kv_heads, 2, slots, HEAD_SIZE), bf16),
            pltpu.VMEM((chunks, rows, HEAD_SIZE), f32),
            dma((kv_heads,)),
            dma((kv_heads,)),
        ],
        cost_estimate=pl.CostEstimate(
            flops=6 * work, bytes_accessed=16 * 2**20, transcendentals=work // 128
        ),
        compiler_params=pltpu.CompilerParams(vmem_limit_bytes=48 * 2**20),
    )(picks.reshape(-1), q_own, span, cos_table, sin_table, cache)

    return pl.pallas_call(
        functools.partial(relay_kernel, n_seg),
        out_shape=jax.ShapeDtypeStruct(queries.shape, bf16),
        in_specs=[smem, vmem, vmem] + [anywhere] * 3,
        out_specs=anywhere,
        scratch_shapes=[
            pltpu.VMEM((n_ctx, chunks, rows, HEAD_SIZE), bf16),
            pltpu.VMEM((kv_heads, slots, HEAD_SIZE), bf16),
            pltpu.VMEM((kv_heads, slots, 2 * HEAD_SIZE), bf16),
            pltpu.VMEM((2, 3, chunks, rows, HEAD_SIZE), bf16),
            pltpu.VMEM((2, 3, chunks, lines, HEAD_SIZE), f32),
            pltpu.VMEM((3, kv_heads // 2, chunks // kv_heads, rows, HEAD_SIZE), f32),
            pltpu.VMEM((3, kv_heads // 2, chunks // kv_heads, lines, HEAD_SIZE), f32),
            pltpu.VMEM((rows, 2 * HEAD_SIZE), f32),
            pltpu.VMEM((rows, 2 * HEAD_SIZE), f32),
            pltpu.VMEM((rows, HEAD_SIZE), f32),
            pltpu.VMEM((rows, HEAD_SIZE), f32),
            dma((2 * kv_heads + 2,)),
            dma((n_ctx, chunks)),
            dma((n_ctx, chunks)),
            dma((2, 3, chunks)),
            dma((2, 3, chunks)),
            dma((2, 3, chunks)),
            dma((2, 3, chunks)),
            dma((chunks, PAIR)),
            dma((chunks, PAIR)),
        ],
        cost_estimate=pl.CostEstimate(
            flops=24 * work, bytes_accessed=32 * 2**20, transcendentals=work // 16
        ),
        compiler_params=pltpu.CompilerParams(
            collective_id=0, has_side_effects=True, vmem_limit_bytes=60 * 2**20
        ),
    )(shift, own, own_logs, cache, q_left, q_right)


def solution(mesh):
    return jax.shard_map(
        local,
        mesh=mesh,
        in_specs=(
            P(("groups", "segment"), "ctx", "head"),
            P(("groups", "segment"), "ctx", None, "head"),
            P(("groups", "segment"), "ctx", None, "head"),
            P(("groups", "segment"), None, "head", None),
            P(("groups", "segment")),
        ),
        out_specs=P(("groups", "segment"), "ctx", "head"),
        check_vma=False,
    )
```

```python
import functools

import jax
import jax.numpy as jnp
from jax import lax
from jax.experimental import pallas as pl
from jax.experimental.pallas import tpu as pltpu
from jax.sharding import PartitionSpec as P

HEAD_SIZE = 128
BLOCK_TOKENS = 512
CHOSEN_BLOCKS = 8


ROPE_BASE = 500000.0


def swapped(x, axis, stride):
    return lax.ppermute(x, axis, [(i, i ^ 1 << stride) for i in range(lax.axis_size(axis))])


def passed_along(block, axis, distance):
    devices = range(lax.axis_size(axis))
    route = [((i - distance) % len(devices), i) for i in devices]
    return lax.ppermute(block, axis, route)


def apply_rotary(values, token_positions):
    half_dim = values.shape[-1] // 2
    frequencies = ROPE_BASE ** (-(2.0 * jnp.arange(half_dim, dtype=jnp.float32)) / values.shape[-1])
    angles = token_positions[:, None] * frequencies[None, :]
    cosine = jnp.cos(angles)[:, None, :]
    sine_part = jnp.sin(angles)[:, None, :]
    widened = values.astype(jnp.float32)
    first_half = widened[..., :half_dim]
    second_half = widened[..., half_dim:]
    joined = jnp.concatenate(
        [
            first_half * cosine - second_half * sine_part,
            second_half * cosine + first_half * sine_part,
        ],
        axis=-1,
    )
    return joined.astype(jnp.bfloat16)


def combine(earlier, later):
    maxima = jnp.maximum(earlier[0], later[0])
    first_factor = jnp.exp(earlier[0] - maxima)
    second_factor = jnp.exp(later[0] - maxima)
    totals = earlier[1] * first_factor + later[1] * second_factor
    weighted = earlier[2] * first_factor[..., None] + later[2] * second_factor[..., None]
    return (maxima, totals, weighted)


def general(queries, span_key_values, key_value_cache, chosen, offset):
    ctx_size = lax.axis_size("ctx")
    my_index = lax.axis_index("ctx")
    tok_rows = queries.shape[1]
    kv_heads = key_value_cache.shape[3] // HEAD_SIZE
    q_heads = queries.shape[2] // HEAD_SIZE
    per_value_head = q_heads // kv_heads
    members = ctx_size // kv_heads
    blocks_here = key_value_cache.shape[1] // BLOCK_TOKENS
    blocks_total = blocks_here * ctx_size
    q_blocks = chosen.shape[1]
    per_block = BLOCK_TOKENS // tok_rows
    key_rows = BLOCK_TOKENS // members
    own_rows = tok_rows // members
    my_head = my_index // members
    my_rank = my_index % members
    score_scale = HEAD_SIZE ** (-0.5)
    token_start = offset[0] + my_index * tok_rows
    token_positions = (token_start + jnp.arange(tok_rows, dtype=jnp.int32)).astype(jnp.float32)
    rot_query = apply_rotary(queries[0].reshape(tok_rows, q_heads, HEAD_SIZE), token_positions)
    rotated_key_rows = apply_rotary(
        span_key_values[0, :, 0].reshape(tok_rows, kv_heads, HEAD_SIZE), token_positions
    )
    fresh_values = span_key_values[0, :, 1].reshape(tok_rows, kv_heads, HEAD_SIZE)
    query_send = jnp.broadcast_to(
        rot_query.reshape(tok_rows, kv_heads, 1, per_value_head * HEAD_SIZE),
        (tok_rows, kv_heads, members, per_value_head * HEAD_SIZE),
    )
    query_send = query_send.reshape(tok_rows, ctx_size, per_value_head * HEAD_SIZE)
    pair_rows = jnp.concatenate([rotated_key_rows, fresh_values], axis=-1)
    pair_send = (
        pair_rows.reshape(members, own_rows, kv_heads, 2 * HEAD_SIZE)
        .transpose(1, 2, 0, 3)
        .reshape(own_rows, ctx_size, 2 * HEAD_SIZE)
    )
    query_recv, pair_recv = (
        lax.all_to_all(query_send, "ctx", split_axis=1, concat_axis=1, tiled=True),
        lax.all_to_all(pair_send, "ctx", split_axis=1, concat_axis=1, tiled=True),
    )
    picks_here = chosen[0]
    needed = jnp.any(
        picks_here[..., None] == jnp.arange(blocks_total, dtype=jnp.int32), axis=(0, 2)
    )
    needed_here = lax.dynamic_slice_in_dim(needed, my_index * blocks_here, blocks_here, axis=1)
    needed_here = needed_here.T.reshape(blocks_here, 1, kv_heads, 1, 1, 1)
    arranged_rows = (
        key_value_cache[0]
        .reshape(blocks_here, members, key_rows, 2, kv_heads, HEAD_SIZE)
        .transpose(0, 2, 4, 1, 3, 5)
    )
    arranged_rows = jnp.where(needed_here, arranged_rows, jnp.zeros((), jnp.bfloat16))
    tile_send = arranged_rows.reshape(blocks_here * key_rows, ctx_size, 2 * HEAD_SIZE)
    fetched = lax.all_to_all(tile_send, "ctx", split_axis=1, concat_axis=1, tiled=True)
    fetched = fetched.reshape(blocks_here, key_rows, ctx_size, 2 * HEAD_SIZE)
    maxima_parts = []
    totals_parts = []
    weighted_parts = []
    for index_of_block in range(q_blocks):
        block_ids = picks_here[index_of_block][my_head]
        owner_rank = block_ids // blocks_here
        slot_index = block_ids % blocks_here
        picked = jnp.stack(
            [
                lax.dynamic_slice(
                    fetched,
                    (slot_index[n], 0, owner_rank[n], 0),
                    (1, key_rows, 1, 2 * HEAD_SIZE),
                )[0, :, 0]
                for n in range(CHOSEN_BLOCKS)
            ]
        )
        sel_keys = picked[..., :HEAD_SIZE].reshape(CHOSEN_BLOCKS * key_rows, HEAD_SIZE)
        sel_values = picked[..., HEAD_SIZE:].reshape(CHOSEN_BLOCKS * key_rows, HEAD_SIZE)
        first_source = index_of_block * per_block
        own_pairs = pair_recv[:, first_source : first_source + per_block]
        own_keys = own_pairs[..., :HEAD_SIZE].reshape(own_rows * per_block, HEAD_SIZE)
        own_values = own_pairs[..., HEAD_SIZE:].reshape(own_rows * per_block, HEAD_SIZE)
        query_rows = query_recv[:, first_source : first_source + per_block].reshape(
            tok_rows * per_block * per_value_head, HEAD_SIZE
        )
        sources = first_source + jnp.arange(per_block, dtype=jnp.int32)
        query_token = sources[None, :] * tok_rows + jnp.arange(tok_rows, dtype=jnp.int32)[:, None]
        query_token = jnp.broadcast_to(
            query_token[:, :, None], (tok_rows, per_block, per_value_head)
        ).reshape(-1)
        key_token = (
            sources[None, :] * tok_rows
            + my_rank * own_rows
            + jnp.arange(own_rows, dtype=jnp.int32)[:, None]
        )
        key_token = key_token.reshape(-1)
        sel_scores = (
            jnp.dot(query_rows, sel_keys.T, preferred_element_type=jnp.float32) * score_scale
        )
        own_scores = (
            jnp.dot(query_rows, own_keys.T, preferred_element_type=jnp.float32) * score_scale
        )
        causal = key_token[None, :] <= query_token[:, None]
        own_scores = jnp.where(causal, own_scores, -jnp.inf)
        maxima = jnp.maximum(jnp.max(sel_scores, axis=1), jnp.max(own_scores, axis=1))
        sel_weights = jnp.exp(sel_scores - maxima[:, None])
        own_weights = jnp.exp(own_scores - maxima[:, None])
        totals = jnp.sum(sel_weights, axis=1) + jnp.sum(own_weights, axis=1)
        weighted = jnp.dot(
            sel_weights, sel_values.astype(jnp.float32), precision=lax.Precision.HIGHEST
        )
        weighted = weighted + jnp.dot(
            own_weights, own_values.astype(jnp.float32), precision=lax.Precision.HIGHEST
        )
        maxima_parts.append(maxima.reshape(tok_rows, per_block, per_value_head))
        totals_parts.append(totals.reshape(tok_rows, per_block, per_value_head))
        weighted_parts.append(weighted.reshape(tok_rows, per_block, per_value_head, HEAD_SIZE))
    maxima_all = jnp.concatenate(maxima_parts, axis=1)
    totals_all = jnp.concatenate(totals_parts, axis=1)
    weighted_all = jnp.concatenate(weighted_parts, axis=1)
    current = (maxima_all, totals_all, weighted_all)
    bit_count = members.bit_length() - 1
    for bit_index in reversed(range(bit_count)):
        half_rows = current[0].shape[0] // 2
        my_bit = my_index // 2**bit_index % 2
        kept = tuple(
            (
                lax.dynamic_slice_in_dim(part_array, my_bit * half_rows, half_rows, 0)
                for part_array in current
            )
        )
        given = tuple(
            (
                lax.dynamic_slice_in_dim(part_array, (1 - my_bit) * half_rows, half_rows, 0)
                for part_array in current
            )
        )
        partner = swapped((given[0], given[1], given[2]), "ctx", bit_index)
        current = combine(kept, partner)
    finished = (
        (current[2] / current[1][..., None])
        .astype(jnp.bfloat16)
        .reshape(own_rows, ctx_size, per_value_head * HEAD_SIZE)
    )
    returned = lax.all_to_all(finished, "ctx", split_axis=1, concat_axis=1, tiled=True)
    context = (
        returned.reshape(own_rows, kv_heads, members, per_value_head * HEAD_SIZE)
        .transpose(2, 0, 1, 3)
        .reshape(tok_rows, q_heads * HEAD_SIZE)
    )
    handed = passed_along(context, "segment", 1)
    return handed[None]


LOG2E = 1.4426950408889634
MESH = pl.DeviceIdType.MESH
PAIR = 2
NOTHING = -1e29
HIDDEN = 1e30
SCALE2 = LOG2E * HEAD_SIZE ** (-0.5)


def turned(block, cosine, sine):
    wide = block.astype(jnp.float32)
    other = pltpu.roll(wide, HEAD_SIZE // 2, 1)
    return (wide * cosine + other * sine).astype(jnp.bfloat16)


def widened(column, count):
    return jnp.concatenate([column] * count, axis=1)


def fold(query, keys, values, shift, causal, first, acc, top):
    scores = lax.dot_general(
        query, keys, (((1,), (1,)), ((), ())), preferred_element_type=jnp.float32
    )
    if causal is not None:
        scores = jnp.where(causal, scores, -jnp.inf)
    new = jnp.max(scores, axis=1, keepdims=True) * SCALE2
    if shift is not None:
        new = new - shift
    new = jnp.broadcast_to(new, (scores.shape[0], HEAD_SIZE))
    if first:
        new = jnp.maximum(new, NOTHING)
    else:
        held = top[...]
        new = jnp.maximum(new, held)
    taken = new if shift is None else new + shift
    weights = jnp.exp2(scores * SCALE2 - widened(taken, scores.shape[1] // HEAD_SIZE))
    part = jnp.dot(weights.astype(jnp.bfloat16), values, preferred_element_type=jnp.float32)
    if first:
        acc[...] = part
    else:
        acc[...] = acc[...] * widened(jnp.exp2(held - new), 2) + part
    top[...] = new


def diagonal():
    rows = lax.broadcasted_iota(jnp.int32, (HEAD_SIZE, HEAD_SIZE), 0)
    columns = lax.broadcasted_iota(jnp.int32, (HEAD_SIZE, HEAD_SIZE), 1)
    return rows == columns


def closed(acc, top):
    totals = jnp.maximum(acc[:, HEAD_SIZE:], 1e-30)
    context = acc[:, :HEAD_SIZE] / totals
    logs = top[...] + jnp.log2(totals)
    eye = diagonal()
    lines = [
        jnp.sum(
            jnp.where(eye, logs[r : r + HEAD_SIZE], 0.0), axis=0, keepdims=True
        )
        for r in range(0, logs.shape[0], HEAD_SIZE)
    ]
    return context, jnp.concatenate(lines, axis=0)


def merged(own, own_logs, other, other_logs):
    most = jnp.maximum(own_logs, other_logs)
    mine = jnp.exp2(own_logs - most)
    total = mine + jnp.exp2(other_logs - most)
    share = mine / total
    eye = diagonal()
    columns = [
        jnp.broadcast_to(
            jnp.sum(
                jnp.where(eye, share[r : r + 1], 0.0), axis=1, keepdims=True
            ),
            (HEAD_SIZE, HEAD_SIZE),
        )
        for r in range(share.shape[0])
    ]
    other = other.astype(jnp.float32)
    return other + jnp.concatenate(columns, axis=0) * (own - other), most + jnp.log2(total)


def turn_kernel(q_ref, cos_ref, sin_ref, out_ref, early_ref):
    tokens = q_ref.shape[1]
    for h in range(q_ref.shape[2] // HEAD_SIZE):
        spot = slice(h % PAIR * tokens, (h % PAIR + 1) * tokens)
        rows = turned(
            q_ref[0, :, h * HEAD_SIZE : (h + 1) * HEAD_SIZE], cos_ref[...], sin_ref[...]
        )
        out_ref[h // PAIR, spot] = rows
        if h // PAIR < early_ref.shape[0]:
            early_ref[h // PAIR, spot] = rows


def home_kernel(
    picks_ref, q_ref, span_ref, cos_ref, sin_ref, cache_ref, out_ref, logs_ref,
    acc, top, values, held, made, load_sem, store_sem,
):
    tokens = cos_ref.shape[0]
    kv_heads = cache_ref.shape[2] // HEAD_SIZE
    halves = q_ref.shape[0] // kv_heads
    blocks_here = cache_ref.shape[1] // BLOCK_TOKENS

    def load(g):
        spot = pl.ds(pl.multiple_of(g * HEAD_SIZE, HEAD_SIZE), HEAD_SIZE)
        return pltpu.make_async_copy(cache_ref.at[:, :, spot], held.at[g], load_sem.at[g])

    def store(g):
        lines = pl.ds(g * halves, halves)
        return pltpu.make_async_copy(made.at[lines], out_ref.at[lines], store_sem.at[g])

    for g in range(kv_heads):
        load(g).start()
    values[:, HEAD_SIZE:] = jnp.ones((tokens, HEAD_SIZE), values.dtype)

    @pl.loop(0, kv_heads)
    def _(g):
        spot = pl.ds(pl.multiple_of(g * HEAD_SIZE, HEAD_SIZE), HEAD_SIZE)
        values[:, :HEAD_SIZE] = span_ref[1, :, spot]
        own_keys = turned(span_ref[0, :, spot], cos_ref[...], sin_ref[...])
        rows = lax.broadcasted_iota(jnp.int32, (tokens, tokens), 0)
        columns = lax.broadcasted_iota(jnp.int32, (tokens, tokens), 1)
        causal = jnp.concatenate([columns <= rows] * PAIR, axis=0)
        for i in range(halves):
            fold(q_ref[g * halves + i], own_keys, values[...], None, causal, True, acc.at[i], top.at[i])
        load(g).wait()

        @pl.loop(0, CHOSEN_BLOCKS)
        def _(n):
            block = picks_ref[g * CHOSEN_BLOCKS + n]

            @pl.when((block >= 0) & (block < blocks_here))
            def _():
                lines = pl.ds(pl.multiple_of(block * BLOCK_TOKENS, BLOCK_TOKENS), BLOCK_TOKENS)
                values[:, :HEAD_SIZE] = held[g, 1, lines]
                for i in range(halves):
                    fold(
                        q_ref[g * halves + i], held[g, 0, lines], values[...], None, None, False,
                        acc.at[i], top.at[i],
                    )

        for i in range(halves):
            made[g * halves + i], logs_ref[g * halves + i] = closed(acc[i], top[i])
        store(g).start()

    for g in range(kv_heads):
        store(g).wait()


def relay_kernel(
    n_seg, shift_ref, own_ref, own_logs_ref, cache_ref, q_ref, ql_ref, qr_ref, out_ref,
    q_buf, k_buf, v_buf, buf, logs, stash, stash_logs, acc, top,
    load_sem, q_send, q_recv, last_send, p_send, p_recv, l_send, l_recv, o_send, o_recv,
):
    me = lax.axis_index("ctx")
    seg = lax.axis_index("segment")
    side = me // 2
    ahead = 1 - 2 * side
    is_mid = (me == 1) | (me == 2)
    is_end = (me == 0) | (me == 3)
    forth, back = side, 1 - side
    kv_heads, slots = k_buf.shape[0], k_buf.shape[1]
    chunks, rows = q_ref.shape[0], q_ref.shape[1]
    last = chunks - 1
    tokens = rows // PAIR
    halves = chunks // kv_heads
    blocks_here = slots // BLOCK_TOKENS
    after = lax.rem(seg + 1, n_seg)
    before = lax.rem(seg + n_seg - 1, n_seg)

    def seen(b):
        return b * ahead + 3 * side

    def load(i, source, target):
        return pltpu.make_async_copy(source, target, load_sem.at[i])

    def head_loads(g):
        spot = pl.ds(pl.multiple_of(g * HEAD_SIZE, HEAD_SIZE), HEAD_SIZE)
        return (
            load(2 * g, cache_ref.at[0, :, spot], k_buf.at[g]),
            load(2 * g + 1, cache_ref.at[1, :, spot], v_buf.at[g, :, pl.ds(0, HEAD_SIZE)]),
        )

    loads = []
    for g in range(kv_heads):
        loads.append(head_loads(g))
    from_left = load(2 * kv_heads, ql_ref, q_buf.at[lax.max(me - 1, 0), pl.ds(0, last)])
    from_right = load(2 * kv_heads + 1, qr_ref, q_buf.at[lax.min(me + 1, 3), pl.ds(0, last)])
    @pl.when(me > 0)
    def _():
        from_left.start()

    @pl.when(me < 3)
    def _():
        from_right.start()

    for copies in loads:
        for copy in copies:
            copy.start()

    barrier = pltpu.get_barrier_semaphore()

    def greet(**place):
        pl.semaphore_signal(barrier, inc=1, device_id=place, device_id_type=MESH)

    @pl.when(me > 0)
    def _():
        greet(ctx=me - 1)

    @pl.when(me < 3)
    def _():
        greet(ctx=me + 1)

    others = (after,) if n_seg == 2 else (after, before)
    for other in others:
        greet(segment=other)

    @pl.when(is_mid)
    def _():
        pl.semaphore_wait(barrier, 2 + len(others))

    @pl.when(is_end)
    def _():
        pl.semaphore_wait(barrier, 1 + len(others))

    def q_copy(source, b, k, target):
        return pltpu.make_async_remote_copy(
            src_ref=source,
            dst_ref=q_buf.at[b, k],
            send_sem=q_send.at[b, k],
            recv_sem=q_recv.at[b, k],
            device_id={"ctx": target},
            device_id_type=MESH,
        )

    def second_hops(k, left_source, right_source):
        left = q_copy(left_source, lax.min(me + 1, 3), k, lax.max(me - 1, 0))
        right = q_copy(right_source, lax.max(me - 1, 0), k, lax.min(me + 1, 3))
        return left, right

    def early_hops(k):
        return second_hops(k, qr_ref.at[k], ql_ref.at[k])

    def late_hops():
        return second_hops(
            last, q_buf.at[lax.min(me + 1, 3), last], q_buf.at[lax.max(me - 1, 0), last]
        )

    def last_hop(way, target):
        return pltpu.make_async_remote_copy(
            src_ref=q_ref.at[last],
            dst_ref=q_buf.at[me, last],
            send_sem=last_send.at[way],
            recv_sem=q_recv.at[me, last],
            device_id={"ctx": target},
            device_id_type=MESH,
        )

    def third_hop(k):
        b = seen(3)
        return q_copy(q_buf.at[b, k], b, k, me - ahead)

    def part_copies(way, p, k, target):
        return (
            pltpu.make_async_remote_copy(
                src_ref=buf.at[way, p, k],
                dst_ref=buf.at[way, p, k],
                send_sem=p_send.at[way, p, k],
                recv_sem=p_recv.at[way, p, k],
                device_id={"ctx": target},
                device_id_type=MESH,
            ),
            pltpu.make_async_remote_copy(
                src_ref=logs.at[way, p, k],
                dst_ref=logs.at[way, p, k],
                send_sem=l_send.at[way, p, k],
                recv_sem=l_recv.at[way, p, k],
                device_id={"ctx": target},
                device_id_type=MESH,
            ),
        )

    def arrived(way, p, k):
        for copy in part_copies(way, p, k, me + ahead):
            copy.wait_recv()

    def send(way, p, k, target):
        for copy in part_copies(way, p, k, target):
            copy.start()

    def out_copies(way, p, k):
        return [
            pltpu.make_async_remote_copy(
                src_ref=buf.at[way, p, k, pl.ds(i * tokens, tokens)],
                dst_ref=out_ref.at[
                    0,
                    :,
                    pl.ds(pl.multiple_of((k * PAIR + i) * HEAD_SIZE, HEAD_SIZE), HEAD_SIZE),
                ],
                send_sem=o_send.at[k, i],
                recv_sem=o_recv.at[k, i],
                device_id={"segment": after},
                device_id_type=MESH,
            )
            for i in range(PAIR)
        ]

    def relay(way, p, k, own, own_log, target):
        arrived(way, p, k)
        value, log = merged(own, own_log, buf[way, p, k], logs[way, p, k])
        buf[way, p, k] = value.astype(buf.dtype)
        logs[way, p, k] = log
        send(way, p, k, target)

    def near(u):
        p, k = u // chunks, lax.rem(u, chunks)
        relay(forth, p, k, stash[p - 1, k], stash_logs[p - 1, k], me + ahead)

    def mid_final(k):
        arrived(forth, 0, k)
        arrived(back, 1, k)
        value, log = merged(own_ref[k], own_logs_ref[k], buf[forth, 0, k], logs[forth, 0, k])
        value, log = merged(value, log, buf[back, 1, k], logs[back, 1, k])
        buf[back, 1, k] = value.astype(buf.dtype)
        for copy in out_copies(back, 1, k):
            copy.start()

    def end_final(k):
        arrived(back, 2, k)
        value, log = merged(own_ref[k], own_logs_ref[k], buf[back, 2, k], logs[back, 2, k])
        buf[back, 2, k] = value.astype(buf.dtype)
        for copy in out_copies(back, 2, k):
            copy.start()

    @pl.when(is_mid)
    def _():
        @pl.loop(0, last)
        def _(k):
            for copy in early_hops(k):
                copy.start()

            @pl.when(k == 1)
            def _():
                last_hop(0, me + ahead).start()
                last_hop(1, me - ahead).start()

    @pl.when(is_end)
    def _():
        last_hop(0, me + ahead).start()

    for g in range(kv_heads):
        v_buf[g, :, HEAD_SIZE:] = jnp.ones((slots, HEAD_SIZE), v_buf.dtype)

    @pl.when(me > 0)
    def _():
        from_left.wait()

    @pl.when(me < 3)
    def _():
        from_right.wait()

    steps, lead = 3 * chunks, chunks // 2

    @pl.loop(0, steps)
    def _(t):
        late = t - lead
        place = jnp.where(
            is_mid,
            lax.rem(t // chunks + 2, 4),
            jnp.where((late < 0) | (late >= 2 * chunks), 1, 2 + late // chunks),
        )
        k = jnp.where(
            is_mid,
            lax.rem(t, chunks),
            jnp.where(late < 0, t, jnp.where(late < 2 * chunks, lax.rem(late + chunks, chunks), t - 2 * chunks)),
        )
        g = k // halves
        b = seen(place)

        @pl.when((t < chunks) & is_mid & (lax.rem(t, halves) == 0))
        def _():
            for copy in head_loads(g):
                copy.wait()

        @pl.when(is_end & (lax.rem(t, halves) == 0) & ((t < lead) | ((t >= 2 * lead) & (t < chunks + lead))))
        def _():
            for copy in head_loads(g):
                copy.wait()

        @pl.when(is_end & (late >= 0) & ((late < 2 * chunks) | (t == steps - 1)))
        def _():
            q_copy(q_buf.at[b, k], b, k, me + ahead).wait_recv()

        @pl.when(is_mid & (t >= 2) & (t < chunks + 2))
        def _():
            copy = third_hop(t - 2)
            copy.wait_recv()
            copy.start()

        @pl.when(is_mid & (t == 3))
        def _():
            left, right = late_hops()
            q_copy(q_ref.at[last], lax.min(me + 1, 3), last, me + ahead).wait_recv()
            q_copy(q_ref.at[last], lax.max(me - 1, 0), last, me + ahead).wait_recv()
            left.start()
            right.start()

        query = q_buf[b, k]
        for j in range(blocks_here):
            lines = slice(j * BLOCK_TOKENS, (j + 1) * BLOCK_TOKENS)
            fold(
                query, k_buf[g, lines], v_buf[g, lines],
                shift_ref[(b * kv_heads + g) * blocks_here + j], None, j == 0, acc, top,
            )
        context, log = closed(acc[...], top[...])

        @pl.when(is_end)
        def _():
            buf[forth, place - 1, k] = context.astype(buf.dtype)
            logs[forth, place - 1, k] = log
            send(forth, place - 1, k, me + ahead)

        @pl.when(is_mid & (t < 2 * chunks))
        def _():
            stash[t // chunks, k] = context
            stash_logs[t // chunks, k] = log

        @pl.when(is_mid & (t >= 2 * chunks))
        def _():
            relay(back, 2, k, context, log, me - ahead)

        @pl.when(is_mid & (t + 2 >= chunks) & (t + 2 < 3 * chunks))
        def _():
            near(t + 2)

        @pl.when(is_mid & (t >= chunks + 2) & (t < chunks + 2 + lead))
        def _():
            mid_final(t - chunks - 2)

        @pl.when(is_mid & (t >= 2 * chunks + 2 + lead))
        def _():
            mid_final(t - 2 * chunks - 2)

        @pl.when(is_end & (t >= 2 * chunks + 3))
        def _():
            end_final(t - 2 * chunks - 3)

    @pl.when(is_mid)
    def _():
        @pl.loop(chunks - 2, chunks)
        def _(k):
            mid_final(k)

    @pl.when(is_end)
    def _():
        @pl.loop(chunks - 3, chunks)
        def _(k):
            end_final(k)

    last_hop(0, me + ahead).wait_send()

    @pl.when(is_mid)
    def _():
        last_hop(1, me - ahead).wait_send()

    @pl.when(is_mid)
    def _():
        @pl.loop(0, chunks)
        def _(k):
            for copy in second_hops(k, q_ref.at[k], q_ref.at[k]) + (third_hop(k),):
                copy.wait_send()
            for copy in part_copies(forth, 1, k, me + ahead) + part_copies(forth, 2, k, me + ahead):
                copy.wait_send()
            for copy in part_copies(back, 2, k, me - ahead):
                copy.wait_send()
            for copy in out_copies(back, 1, k):
                copy.wait()

    @pl.when(is_end)
    def _():
        @pl.loop(0, chunks)
        def _(k):
            for p in range(3):
                for copy in part_copies(forth, p, k, me + ahead):
                    copy.wait_send()
            for copy in out_copies(back, 2, k):
                copy.wait()


def local(queries, span_key_values, key_value_cache, chosen, offset):
    n_ctx = lax.axis_size("ctx")
    n_seg = lax.axis_size("segment")
    me = lax.axis_index("ctx")
    tokens = queries.shape[1]
    kv_heads = key_value_cache.shape[3] // HEAD_SIZE
    q_heads = queries.shape[2] // HEAD_SIZE
    per_head = q_heads // kv_heads
    slots = key_value_cache.shape[1]
    blocks_here = slots // BLOCK_TOKENS
    if not (
        n_ctx == 4
        and tokens == BLOCK_TOKENS
        and n_seg > 1
        and per_head % PAIR == 0
        and slots * kv_heads <= 16384
        and q_heads == 8 * PAIR
        and kv_heads == 4
    ):
        return general(queries, span_key_values, key_value_cache, chosen, offset)
    bf16, f32 = jnp.bfloat16, jnp.float32
    dma = pltpu.SemaphoreType.DMA
    chunks, rows = q_heads // PAIR, PAIR * tokens
    lines = rows // HEAD_SIZE
    vmem = pl.BlockSpec(memory_space=pltpu.VMEM)
    smem = pl.BlockSpec(memory_space=pltpu.SMEM)
    anywhere = pl.BlockSpec(memory_space=pl.ANY)

    positions = (offset[0] + me * tokens + jnp.arange(tokens, dtype=jnp.int32)).astype(f32)
    half = HEAD_SIZE // 2
    frequencies = ROPE_BASE ** (-(2.0 * jnp.arange(half, dtype=f32)) / HEAD_SIZE)
    angles = positions[:, None] * frequencies[None, :]
    cosine, sine = jnp.cos(angles), jnp.sin(angles)
    cos_table = jnp.concatenate([cosine, cosine], axis=1)
    sin_table = jnp.concatenate([-sine, sine], axis=1)
    q_own, q_early = pl.pallas_call(
        turn_kernel,
        out_shape=(
            jax.ShapeDtypeStruct((chunks, rows, HEAD_SIZE), bf16),
            jax.ShapeDtypeStruct((chunks - 1, rows, HEAD_SIZE), bf16),
        ),
        in_specs=[vmem] * 3,
        out_specs=(vmem, vmem),
        cost_estimate=pl.CostEstimate(
            flops=6 * queries.size, bytes_accessed=4 * queries.size, transcendentals=0
        ),
        compiler_params=pltpu.CompilerParams(vmem_limit_bytes=60 * 2**20),
    )(queries, cos_table, sin_table)
    q_left = lax.ppermute(q_early, "ctx", [(i, i + 1) for i in range(n_ctx - 1)])
    q_right = lax.ppermute(q_early, "ctx", [(i + 1, i) for i in range(n_ctx - 1)])

    cache = key_value_cache[0].transpose(1, 0, 2)
    span = span_key_values[0].transpose(1, 0, 2)
    first_block = me * blocks_here
    picks = lax.dynamic_index_in_dim(chosen[0], me, 0, keepdims=False) - first_block
    here = first_block + jnp.arange(blocks_here, dtype=jnp.int32)
    taken = jnp.any(chosen[0][..., None] == here, axis=2)
    shift = jnp.where(taken, 0.0, HIDDEN).astype(f32).reshape(-1)
    work = 4 * q_heads * tokens * BLOCK_TOKENS * HEAD_SIZE
    own, own_logs = pl.pallas_call(
        home_kernel,
        out_shape=(
            jax.ShapeDtypeStruct((chunks, rows, HEAD_SIZE), f32),
            jax.ShapeDtypeStruct((chunks, lines, HEAD_SIZE), f32),
        ),
        in_specs=[smem] + [vmem] * 4 + [anywhere],
        out_specs=(anywhere, vmem),
        scratch_shapes=[
            pltpu.VMEM((chunks // kv_heads, rows, 2 * HEAD_SIZE), f32),
            pltpu.VMEM((chunks // kv_heads, rows, HEAD_SIZE), f32),
            pltpu.VMEM((tokens, 2 * HEAD_SIZE), bf16),
            pltpu.VMEM((kv_heads, 2, slots, HEAD_SIZE), bf16),
            pltpu.VMEM((chunks, rows, HEAD_SIZE), f32),
            dma((kv_heads,)),
            dma((kv_heads,)),
        ],
        cost_estimate=pl.CostEstimate(
            flops=6 * work, bytes_accessed=16 * 2**20, transcendentals=work // 128
        ),
        compiler_params=pltpu.CompilerParams(vmem_limit_bytes=62 * 2**20),
    )(picks.reshape(-1), q_own, span, cos_table, sin_table, cache)

    return pl.pallas_call(
        functools.partial(relay_kernel, n_seg),
        out_shape=jax.ShapeDtypeStruct(queries.shape, bf16),
        in_specs=[smem, vmem, vmem] + [anywhere] * 4,
        out_specs=anywhere,
        scratch_shapes=[
            pltpu.VMEM((n_ctx, chunks, rows, HEAD_SIZE), bf16),
            pltpu.VMEM((kv_heads, slots, HEAD_SIZE), bf16),
            pltpu.VMEM((kv_heads, slots, 2 * HEAD_SIZE), bf16),
            pltpu.VMEM((2, 3, chunks, rows, HEAD_SIZE), bf16),
            pltpu.VMEM((2, 3, chunks, lines, HEAD_SIZE), f32),
            pltpu.VMEM((2, chunks, rows, HEAD_SIZE), f32),
            pltpu.VMEM((2, chunks, lines, HEAD_SIZE), f32),
            pltpu.VMEM((rows, 2 * HEAD_SIZE), f32),
            pltpu.VMEM((rows, HEAD_SIZE), f32),
            dma((2 * kv_heads + 2,)),
            dma((n_ctx, chunks)),
            dma((n_ctx, chunks)),
            dma((2,)),
            dma((2, 3, chunks)),
            dma((2, 3, chunks)),
            dma((2, 3, chunks)),
            dma((2, 3, chunks)),
            dma((chunks, PAIR)),
            dma((chunks, PAIR)),
        ],
        cost_estimate=pl.CostEstimate(
            flops=24 * work, bytes_accessed=32 * 2**20, transcendentals=work // 16
        ),
        compiler_params=pltpu.CompilerParams(
            collective_id=0, has_side_effects=True, vmem_limit_bytes=60 * 2**20
        ),
    )(shift, own, own_logs, cache, q_own, q_left, q_right)


def solution(mesh):
    return jax.shard_map(
        local,
        mesh=mesh,
        in_specs=(
            P(("groups", "segment"), "ctx", "head"),
            P(("groups", "segment"), "ctx", None, "head"),
            P(("groups", "segment"), "ctx", None, "head"),
            P(("groups", "segment"), None, "head", None),
            P(("groups", "segment")),
        ),
        out_specs=P(("groups", "segment"), "ctx", "head"),
        check_vma=False,
    )
```

```python
import functools

import jax
import jax.numpy as jnp
from jax import lax
from jax.experimental import pallas as pl
from jax.experimental.pallas import tpu as pltpu
from jax.sharding import PartitionSpec as P

HEAD_SIZE = 128
BLOCK_TOKENS = 512
CHOSEN_BLOCKS = 8


ROPE_BASE = 500000.0


def swapped(x, axis, stride):
    return lax.ppermute(x, axis, [(i, i ^ 1 << stride) for i in range(lax.axis_size(axis))])


def passed_along(block, axis, distance):
    devices = range(lax.axis_size(axis))
    route = [((i - distance) % len(devices), i) for i in devices]
    return lax.ppermute(block, axis, route)


def apply_rotary(values, token_positions):
    half_dim = values.shape[-1] // 2
    frequencies = ROPE_BASE ** (-(2.0 * jnp.arange(half_dim, dtype=jnp.float32)) / values.shape[-1])
    angles = token_positions[:, None] * frequencies[None, :]
    cosine = jnp.cos(angles)[:, None, :]
    sine_part = jnp.sin(angles)[:, None, :]
    widened = values.astype(jnp.float32)
    first_half = widened[..., :half_dim]
    second_half = widened[..., half_dim:]
    joined = jnp.concatenate(
        [
            first_half * cosine - second_half * sine_part,
            second_half * cosine + first_half * sine_part,
        ],
        axis=-1,
    )
    return joined.astype(jnp.bfloat16)


def combine(earlier, later):
    maxima = jnp.maximum(earlier[0], later[0])
    first_factor = jnp.exp(earlier[0] - maxima)
    second_factor = jnp.exp(later[0] - maxima)
    totals = earlier[1] * first_factor + later[1] * second_factor
    weighted = earlier[2] * first_factor[..., None] + later[2] * second_factor[..., None]
    return (maxima, totals, weighted)


def general(queries, span_key_values, key_value_cache, chosen, offset):
    ctx_size = lax.axis_size("ctx")
    my_index = lax.axis_index("ctx")
    tok_rows = queries.shape[1]
    kv_heads = key_value_cache.shape[3] // HEAD_SIZE
    q_heads = queries.shape[2] // HEAD_SIZE
    per_value_head = q_heads // kv_heads
    members = ctx_size // kv_heads
    blocks_here = key_value_cache.shape[1] // BLOCK_TOKENS
    blocks_total = blocks_here * ctx_size
    q_blocks = chosen.shape[1]
    per_block = BLOCK_TOKENS // tok_rows
    key_rows = BLOCK_TOKENS // members
    own_rows = tok_rows // members
    my_head = my_index // members
    my_rank = my_index % members
    score_scale = HEAD_SIZE ** (-0.5)
    token_start = offset[0] + my_index * tok_rows
    token_positions = (token_start + jnp.arange(tok_rows, dtype=jnp.int32)).astype(jnp.float32)
    rot_query = apply_rotary(queries[0].reshape(tok_rows, q_heads, HEAD_SIZE), token_positions)
    rotated_key_rows = apply_rotary(
        span_key_values[0, :, 0].reshape(tok_rows, kv_heads, HEAD_SIZE), token_positions
    )
    fresh_values = span_key_values[0, :, 1].reshape(tok_rows, kv_heads, HEAD_SIZE)
    query_send = jnp.broadcast_to(
        rot_query.reshape(tok_rows, kv_heads, 1, per_value_head * HEAD_SIZE),
        (tok_rows, kv_heads, members, per_value_head * HEAD_SIZE),
    )
    query_send = query_send.reshape(tok_rows, ctx_size, per_value_head * HEAD_SIZE)
    pair_rows = jnp.concatenate([rotated_key_rows, fresh_values], axis=-1)
    pair_send = (
        pair_rows.reshape(members, own_rows, kv_heads, 2 * HEAD_SIZE)
        .transpose(1, 2, 0, 3)
        .reshape(own_rows, ctx_size, 2 * HEAD_SIZE)
    )
    query_recv, pair_recv = (
        lax.all_to_all(query_send, "ctx", split_axis=1, concat_axis=1, tiled=True),
        lax.all_to_all(pair_send, "ctx", split_axis=1, concat_axis=1, tiled=True),
    )
    picks_here = chosen[0]
    needed = jnp.any(
        picks_here[..., None] == jnp.arange(blocks_total, dtype=jnp.int32), axis=(0, 2)
    )
    needed_here = lax.dynamic_slice_in_dim(needed, my_index * blocks_here, blocks_here, axis=1)
    needed_here = needed_here.T.reshape(blocks_here, 1, kv_heads, 1, 1, 1)
    arranged_rows = (
        key_value_cache[0]
        .reshape(blocks_here, members, key_rows, 2, kv_heads, HEAD_SIZE)
        .transpose(0, 2, 4, 1, 3, 5)
    )
    arranged_rows = jnp.where(needed_here, arranged_rows, jnp.zeros((), jnp.bfloat16))
    tile_send = arranged_rows.reshape(blocks_here * key_rows, ctx_size, 2 * HEAD_SIZE)
    fetched = lax.all_to_all(tile_send, "ctx", split_axis=1, concat_axis=1, tiled=True)
    fetched = fetched.reshape(blocks_here, key_rows, ctx_size, 2 * HEAD_SIZE)
    maxima_parts = []
    totals_parts = []
    weighted_parts = []
    for index_of_block in range(q_blocks):
        block_ids = picks_here[index_of_block][my_head]
        owner_rank = block_ids // blocks_here
        slot_index = block_ids % blocks_here
        picked = jnp.stack(
            [
                lax.dynamic_slice(
                    fetched,
                    (slot_index[n], 0, owner_rank[n], 0),
                    (1, key_rows, 1, 2 * HEAD_SIZE),
                )[0, :, 0]
                for n in range(CHOSEN_BLOCKS)
            ]
        )
        sel_keys = picked[..., :HEAD_SIZE].reshape(CHOSEN_BLOCKS * key_rows, HEAD_SIZE)
        sel_values = picked[..., HEAD_SIZE:].reshape(CHOSEN_BLOCKS * key_rows, HEAD_SIZE)
        first_source = index_of_block * per_block
        own_pairs = pair_recv[:, first_source : first_source + per_block]
        own_keys = own_pairs[..., :HEAD_SIZE].reshape(own_rows * per_block, HEAD_SIZE)
        own_values = own_pairs[..., HEAD_SIZE:].reshape(own_rows * per_block, HEAD_SIZE)
        query_rows = query_recv[:, first_source : first_source + per_block].reshape(
            tok_rows * per_block * per_value_head, HEAD_SIZE
        )
        sources = first_source + jnp.arange(per_block, dtype=jnp.int32)
        query_token = sources[None, :] * tok_rows + jnp.arange(tok_rows, dtype=jnp.int32)[:, None]
        query_token = jnp.broadcast_to(
            query_token[:, :, None], (tok_rows, per_block, per_value_head)
        ).reshape(-1)
        key_token = (
            sources[None, :] * tok_rows
            + my_rank * own_rows
            + jnp.arange(own_rows, dtype=jnp.int32)[:, None]
        )
        key_token = key_token.reshape(-1)
        sel_scores = (
            jnp.dot(query_rows, sel_keys.T, preferred_element_type=jnp.float32) * score_scale
        )
        own_scores = (
            jnp.dot(query_rows, own_keys.T, preferred_element_type=jnp.float32) * score_scale
        )
        causal = key_token[None, :] <= query_token[:, None]
        own_scores = jnp.where(causal, own_scores, -jnp.inf)
        maxima = jnp.maximum(jnp.max(sel_scores, axis=1), jnp.max(own_scores, axis=1))
        sel_weights = jnp.exp(sel_scores - maxima[:, None])
        own_weights = jnp.exp(own_scores - maxima[:, None])
        totals = jnp.sum(sel_weights, axis=1) + jnp.sum(own_weights, axis=1)
        weighted = jnp.dot(
            sel_weights, sel_values.astype(jnp.float32), precision=lax.Precision.HIGHEST
        )
        weighted = weighted + jnp.dot(
            own_weights, own_values.astype(jnp.float32), precision=lax.Precision.HIGHEST
        )
        maxima_parts.append(maxima.reshape(tok_rows, per_block, per_value_head))
        totals_parts.append(totals.reshape(tok_rows, per_block, per_value_head))
        weighted_parts.append(weighted.reshape(tok_rows, per_block, per_value_head, HEAD_SIZE))
    maxima_all = jnp.concatenate(maxima_parts, axis=1)
    totals_all = jnp.concatenate(totals_parts, axis=1)
    weighted_all = jnp.concatenate(weighted_parts, axis=1)
    current = (maxima_all, totals_all, weighted_all)
    bit_count = members.bit_length() - 1
    for bit_index in reversed(range(bit_count)):
        half_rows = current[0].shape[0] // 2
        my_bit = my_index // 2**bit_index % 2
        kept = tuple(
            (
                lax.dynamic_slice_in_dim(part_array, my_bit * half_rows, half_rows, 0)
                for part_array in current
            )
        )
        given = tuple(
            (
                lax.dynamic_slice_in_dim(part_array, (1 - my_bit) * half_rows, half_rows, 0)
                for part_array in current
            )
        )
        partner = swapped((given[0], given[1], given[2]), "ctx", bit_index)
        current = combine(kept, partner)
    finished = (
        (current[2] / current[1][..., None])
        .astype(jnp.bfloat16)
        .reshape(own_rows, ctx_size, per_value_head * HEAD_SIZE)
    )
    returned = lax.all_to_all(finished, "ctx", split_axis=1, concat_axis=1, tiled=True)
    context = (
        returned.reshape(own_rows, kv_heads, members, per_value_head * HEAD_SIZE)
        .transpose(2, 0, 1, 3)
        .reshape(tok_rows, q_heads * HEAD_SIZE)
    )
    handed = passed_along(context, "segment", 1)
    return handed[None]


LOG2E = 1.4426950408889634
MESH = pl.DeviceIdType.MESH
PAIR = 2
NOTHING = -1e29
HIDDEN = 1e30
SCALE2 = LOG2E * HEAD_SIZE ** (-0.5)


def turned(block, cosine, sine):
    wide = block.astype(jnp.float32)
    other = pltpu.roll(wide, HEAD_SIZE // 2, 1)
    return (wide * cosine + other * sine).astype(jnp.bfloat16)


def widened(column, count):
    return jnp.concatenate([column] * count, axis=1)


def fold(query, keys, values, shift, causal, first, acc, top):
    scores = lax.dot_general(
        query, keys, (((1,), (1,)), ((), ())), preferred_element_type=jnp.float32
    )
    if causal is not None:
        scores = jnp.where(causal, scores, -jnp.inf)
    new = jnp.max(scores, axis=1, keepdims=True) * SCALE2
    if shift is not None:
        new = new - shift
    new = jnp.broadcast_to(new, (scores.shape[0], HEAD_SIZE))
    if first:
        new = jnp.maximum(new, NOTHING)
    else:
        held = top[...]
        new = jnp.maximum(new, held)
    taken = new if shift is None else new + shift
    weights = jnp.exp2(scores * SCALE2 - widened(taken, scores.shape[1] // HEAD_SIZE))
    part = jnp.dot(weights.astype(jnp.bfloat16), values, preferred_element_type=jnp.float32)
    if first:
        acc[...] = part
    else:
        acc[...] = acc[...] * widened(jnp.exp2(held - new), 2) + part
    top[...] = new


def diagonal():
    rows = lax.broadcasted_iota(jnp.int32, (HEAD_SIZE, HEAD_SIZE), 0)
    columns = lax.broadcasted_iota(jnp.int32, (HEAD_SIZE, HEAD_SIZE), 1)
    return rows == columns


def closed(acc, top):
    totals = jnp.maximum(acc[:, HEAD_SIZE:], 1e-30)
    context = acc[:, :HEAD_SIZE] / totals
    logs = top[...] + jnp.log2(totals)
    eye = diagonal()
    lines = [
        jnp.sum(
            jnp.where(eye, logs[r : r + HEAD_SIZE], 0.0), axis=0, keepdims=True
        )
        for r in range(0, logs.shape[0], HEAD_SIZE)
    ]
    return context, jnp.concatenate(lines, axis=0)


def merged(own, own_logs, other, other_logs):
    most = jnp.maximum(own_logs, other_logs)
    mine = jnp.exp2(own_logs - most)
    total = mine + jnp.exp2(other_logs - most)
    share = mine / total
    eye = diagonal()
    columns = [
        jnp.broadcast_to(
            jnp.sum(
                jnp.where(eye, share[r : r + 1], 0.0), axis=1, keepdims=True
            ),
            (HEAD_SIZE, HEAD_SIZE),
        )
        for r in range(share.shape[0])
    ]
    other = other.astype(jnp.float32)
    return other + jnp.concatenate(columns, axis=0) * (own - other), most + jnp.log2(total)


def turn_kernel(q_ref, cos_ref, sin_ref, out_ref, early_ref):
    tokens = q_ref.shape[1]
    for h in range(q_ref.shape[2] // HEAD_SIZE):
        spot = slice(h % PAIR * tokens, (h % PAIR + 1) * tokens)
        rows = turned(
            q_ref[0, :, h * HEAD_SIZE : (h + 1) * HEAD_SIZE], cos_ref[...], sin_ref[...]
        )
        out_ref[h // PAIR, spot] = rows
        if h // PAIR < early_ref.shape[0]:
            early_ref[h // PAIR, spot] = rows


def home_kernel(
    chosen_ref, q_ref, span_ref, cos_ref, sin_ref, cache_ref, out_ref, logs_ref,
    acc, top, values, held, made, load_sem, store_sem,
):
    me = lax.axis_index("ctx")
    tokens = cos_ref.shape[0]
    kv_heads = cache_ref.shape[2] // HEAD_SIZE
    halves = q_ref.shape[0] // kv_heads
    blocks_here = cache_ref.shape[1] // BLOCK_TOKENS

    def load(g):
        spot = pl.ds(pl.multiple_of(g * HEAD_SIZE, HEAD_SIZE), HEAD_SIZE)
        return pltpu.make_async_copy(cache_ref.at[:, :, spot], held.at[g], load_sem.at[g])

    def store(g):
        lines = pl.ds(g * halves, halves)
        return pltpu.make_async_copy(made.at[lines], out_ref.at[lines], store_sem.at[g])

    for g in range(kv_heads):
        load(g).start()
    values[:, HEAD_SIZE:] = jnp.ones((tokens, HEAD_SIZE), values.dtype)

    @pl.loop(0, kv_heads)
    def _(g):
        spot = pl.ds(pl.multiple_of(g * HEAD_SIZE, HEAD_SIZE), HEAD_SIZE)
        values[:, :HEAD_SIZE] = span_ref[1, :, spot]
        own_keys = turned(span_ref[0, :, spot], cos_ref[...], sin_ref[...])
        rows = lax.broadcasted_iota(jnp.int32, (tokens, tokens), 0)
        columns = lax.broadcasted_iota(jnp.int32, (tokens, tokens), 1)
        causal = jnp.concatenate([columns <= rows] * PAIR, axis=0)
        for i in range(halves):
            fold(q_ref[g * halves + i], own_keys, values[...], None, causal, True, acc.at[i], top.at[i])
        load(g).wait()

        @pl.loop(0, CHOSEN_BLOCKS)
        def _(n):
            block = chosen_ref[(me * kv_heads + g) * CHOSEN_BLOCKS + n] - me * blocks_here

            @pl.when((block >= 0) & (block < blocks_here))
            def _():
                lines = pl.ds(pl.multiple_of(block * BLOCK_TOKENS, BLOCK_TOKENS), BLOCK_TOKENS)
                values[:, :HEAD_SIZE] = held[g, 1, lines]
                for i in range(halves):
                    fold(
                        q_ref[g * halves + i], held[g, 0, lines], values[...], None, None, False,
                        acc.at[i], top.at[i],
                    )

        for i in range(halves):
            made[g * halves + i], logs_ref[g * halves + i] = closed(acc[i], top[i])
        store(g).start()

    for g in range(kv_heads):
        store(g).wait()


def relay_kernel(
    n_seg, chosen_ref, own_logs_ref, own_hbm_ref, cache_ref, q_ref, ql_ref, qr_ref, out_ref,
    q_buf, k_buf, v_buf, buf, logs, stash, stash_logs, own_ref, acc, top,
    load_sem, q_send, q_recv, last_send, p_send, p_recv, l_send, l_recv, o_send, o_recv,
):
    me = lax.axis_index("ctx")
    seg = lax.axis_index("segment")
    side = me // 2
    ahead = 1 - 2 * side
    is_mid = (me == 1) | (me == 2)
    is_end = (me == 0) | (me == 3)
    forth, back = side, 1 - side
    kv_heads, slots = k_buf.shape[0], k_buf.shape[1]
    chunks, rows = q_ref.shape[0], q_ref.shape[1]
    last = chunks - 1
    tokens = rows // PAIR
    halves = chunks // kv_heads
    blocks_here = slots // BLOCK_TOKENS
    after = lax.rem(seg + 1, n_seg)
    before = lax.rem(seg + n_seg - 1, n_seg)

    def hidden(b, g, j):
        amount = jnp.float32(HIDDEN)
        for n in range(CHOSEN_BLOCKS):
            block = chosen_ref[(b * kv_heads + g) * CHOSEN_BLOCKS + n]
            amount = jnp.where(block == me * blocks_here + j, jnp.float32(0.0), amount)
        return amount

    def seen(b):
        return b * ahead + 3 * side

    def load(i, source, target):
        return pltpu.make_async_copy(source, target, load_sem.at[i])

    def head_loads(g):
        spot = pl.ds(pl.multiple_of(g * HEAD_SIZE, HEAD_SIZE), HEAD_SIZE)
        return (
            load(2 * g, cache_ref.at[0, :, spot], k_buf.at[g]),
            load(2 * g + 1, cache_ref.at[1, :, spot], v_buf.at[g, :, pl.ds(0, HEAD_SIZE)]),
        )

    loads = []
    for g in range(kv_heads):
        loads.append(head_loads(g))
    from_left = load(2 * kv_heads, ql_ref, q_buf.at[lax.max(me - 1, 0), pl.ds(0, last)])
    from_right = load(2 * kv_heads + 1, qr_ref, q_buf.at[lax.min(me + 1, 3), pl.ds(0, last)])
    @pl.when(me > 0)
    def _():
        from_left.start()

    @pl.when(me < 3)
    def _():
        from_right.start()

    for copies in loads:
        for copy in copies:
            copy.start()

    own_load = load(2 * kv_heads + 2, own_hbm_ref, own_ref)
    own_load.start()
    barrier = pltpu.get_barrier_semaphore()

    def greet(**place):
        pl.semaphore_signal(barrier, inc=1, device_id=place, device_id_type=MESH)

    @pl.when(me > 0)
    def _():
        greet(ctx=me - 1)

    @pl.when(me < 3)
    def _():
        greet(ctx=me + 1)

    others = (after,) if n_seg == 2 else (after, before)
    for other in others:
        greet(segment=other)

    @pl.when(is_mid)
    def _():
        pl.semaphore_wait(barrier, 2 + len(others))

    @pl.when(is_end)
    def _():
        pl.semaphore_wait(barrier, 1 + len(others))

    def q_copy(source, b, k, target):
        return pltpu.make_async_remote_copy(
            src_ref=source,
            dst_ref=q_buf.at[b, k],
            send_sem=q_send.at[b, k],
            recv_sem=q_recv.at[b, k],
            device_id={"ctx": target},
            device_id_type=MESH,
        )

    def second_hops(k, left_source, right_source):
        left = q_copy(left_source, lax.min(me + 1, 3), k, lax.max(me - 1, 0))
        right = q_copy(right_source, lax.max(me - 1, 0), k, lax.min(me + 1, 3))
        return left, right

    def early_hops(k):
        return second_hops(k, qr_ref.at[k], ql_ref.at[k])

    def late_hops():
        return second_hops(
            last, q_buf.at[lax.min(me + 1, 3), last], q_buf.at[lax.max(me - 1, 0), last]
        )

    def last_hop(way, target):
        return pltpu.make_async_remote_copy(
            src_ref=q_ref.at[last],
            dst_ref=q_buf.at[me, last],
            send_sem=last_send.at[way],
            recv_sem=q_recv.at[me, last],
            device_id={"ctx": target},
            device_id_type=MESH,
        )

    def third_hop(k):
        b = seen(3)
        return q_copy(q_buf.at[b, k], b, k, me - ahead)

    def part_copies(way, p, k, target):
        return (
            pltpu.make_async_remote_copy(
                src_ref=buf.at[way, p, k],
                dst_ref=buf.at[way, p, k],
                send_sem=p_send.at[way, p, k],
                recv_sem=p_recv.at[way, p, k],
                device_id={"ctx": target},
                device_id_type=MESH,
            ),
            pltpu.make_async_remote_copy(
                src_ref=logs.at[way, p, k],
                dst_ref=logs.at[way, p, k],
                send_sem=l_send.at[way, p, k],
                recv_sem=l_recv.at[way, p, k],
                device_id={"ctx": target},
                device_id_type=MESH,
            ),
        )

    def arrived(way, p, k):
        for copy in part_copies(way, p, k, me + ahead):
            copy.wait_recv()

    def send(way, p, k, target):
        for copy in part_copies(way, p, k, target):
            copy.start()

    def out_copies(way, p, k):
        return [
            pltpu.make_async_remote_copy(
                src_ref=buf.at[way, p, k, pl.ds(i * tokens, tokens)],
                dst_ref=out_ref.at[
                    0,
                    :,
                    pl.ds(pl.multiple_of((k * PAIR + i) * HEAD_SIZE, HEAD_SIZE), HEAD_SIZE),
                ],
                send_sem=o_send.at[k, i],
                recv_sem=o_recv.at[k, i],
                device_id={"segment": after},
                device_id_type=MESH,
            )
            for i in range(PAIR)
        ]

    def relay(way, p, k, own, own_log, target):
        arrived(way, p, k)
        value, log = merged(own, own_log, buf[way, p, k], logs[way, p, k])
        buf[way, p, k] = value.astype(buf.dtype)
        logs[way, p, k] = log
        send(way, p, k, target)

    def near(u):
        p, k = u // chunks, lax.rem(u, chunks)
        relay(forth, p, k, stash[p - 1, k], stash_logs[p - 1, k], me + ahead)

    def mid_final(k):
        arrived(forth, 0, k)
        arrived(back, 1, k)
        value, log = merged(own_ref[k], own_logs_ref[k], buf[forth, 0, k], logs[forth, 0, k])
        value, log = merged(value, log, buf[back, 1, k], logs[back, 1, k])
        buf[back, 1, k] = value.astype(buf.dtype)
        for copy in out_copies(back, 1, k):
            copy.start()

    def end_final(k):
        arrived(back, 2, k)
        value, log = merged(own_ref[k], own_logs_ref[k], buf[back, 2, k], logs[back, 2, k])
        buf[back, 2, k] = value.astype(buf.dtype)
        for copy in out_copies(back, 2, k):
            copy.start()

    @pl.when(is_mid)
    def _():
        @pl.loop(0, last)
        def _(k):
            for copy in early_hops(k):
                copy.start()

            @pl.when(k == 1)
            def _():
                last_hop(0, me + ahead).start()
                last_hop(1, me - ahead).start()

    @pl.when(is_end)
    def _():
        last_hop(0, me + ahead).start()

    for g in range(kv_heads):
        v_buf[g, :, HEAD_SIZE:] = jnp.ones((slots, HEAD_SIZE), v_buf.dtype)

    @pl.when(me > 0)
    def _():
        from_left.wait()

    @pl.when(me < 3)
    def _():
        from_right.wait()

    steps, lead = 3 * chunks, chunks // 2

    @pl.loop(0, steps)
    def _(t):
        late = t - lead
        place = jnp.where(
            is_mid,
            lax.rem(t // chunks + 2, 4),
            jnp.where((late < 0) | (late >= 2 * chunks), 1, 2 + late // chunks),
        )
        k = jnp.where(
            is_mid,
            lax.rem(t, chunks),
            jnp.where(late < 0, t, jnp.where(late < 2 * chunks, lax.rem(late + chunks, chunks), t - 2 * chunks)),
        )
        g = k // halves
        b = seen(place)

        @pl.when((t < chunks) & is_mid & (lax.rem(t, halves) == 0))
        def _():
            for copy in head_loads(g):
                copy.wait()

        @pl.when(is_end & (lax.rem(t, halves) == 0) & ((t < lead) | ((t >= 2 * lead) & (t < chunks + lead))))
        def _():
            for copy in head_loads(g):
                copy.wait()

        @pl.when(is_end & (late >= 0) & ((late < 2 * chunks) | (t == steps - 1)))
        def _():
            q_copy(q_buf.at[b, k], b, k, me + ahead).wait_recv()

        @pl.when(is_mid & (t >= 2) & (t < chunks + 2))
        def _():
            copy = third_hop(t - 2)
            copy.wait_recv()
            copy.start()

        @pl.when(t == chunks)
        def _():
            own_load.wait()

        @pl.when(is_mid & (t == 3))
        def _():
            left, right = late_hops()
            q_copy(q_ref.at[last], lax.min(me + 1, 3), last, me + ahead).wait_recv()
            q_copy(q_ref.at[last], lax.max(me - 1, 0), last, me + ahead).wait_recv()
            left.start()
            right.start()

        query = q_buf[b, k]
        for j in range(blocks_here):
            lines = slice(j * BLOCK_TOKENS, (j + 1) * BLOCK_TOKENS)
            fold(
                query, k_buf[g, lines], v_buf[g, lines],
                hidden(b, g, j), None, j == 0, acc, top,
            )
        context, log = closed(acc[...], top[...])

        @pl.when(is_end)
        def _():
            buf[forth, place - 1, k] = context.astype(buf.dtype)
            logs[forth, place - 1, k] = log
            send(forth, place - 1, k, me + ahead)

        @pl.when(is_mid & (t < 2 * chunks))
        def _():
            stash[t // chunks, k] = context
            stash_logs[t // chunks, k] = log

        @pl.when(is_mid & (t >= 2 * chunks))
        def _():
            relay(back, 2, k, context, log, me - ahead)

        @pl.when(is_mid & (t + 2 >= chunks) & (t + 2 < 3 * chunks))
        def _():
            near(t + 2)

        @pl.when(is_mid & (t >= chunks + 2) & (t < chunks + 2 + lead))
        def _():
            mid_final(t - chunks - 2)

        @pl.when(is_mid & (t >= 2 * chunks + 2 + lead))
        def _():
            mid_final(t - 2 * chunks - 2)

        @pl.when(is_end & (t >= 2 * chunks + 3))
        def _():
            end_final(t - 2 * chunks - 3)

    @pl.when(is_mid)
    def _():
        @pl.loop(chunks - 2, chunks)
        def _(k):
            mid_final(k)

    @pl.when(is_end)
    def _():
        @pl.loop(chunks - 3, chunks)
        def _(k):
            end_final(k)

    last_hop(0, me + ahead).wait_send()

    @pl.when(is_mid)
    def _():
        last_hop(1, me - ahead).wait_send()

    @pl.when(is_mid)
    def _():
        @pl.loop(0, chunks)
        def _(k):
            for copy in second_hops(k, q_ref.at[k], q_ref.at[k]) + (third_hop(k),):
                copy.wait_send()
            for copy in part_copies(forth, 1, k, me + ahead) + part_copies(forth, 2, k, me + ahead):
                copy.wait_send()
            for copy in part_copies(back, 2, k, me - ahead):
                copy.wait_send()
            for copy in out_copies(back, 1, k):
                copy.wait()

    @pl.when(is_end)
    def _():
        @pl.loop(0, chunks)
        def _(k):
            for p in range(3):
                for copy in part_copies(forth, p, k, me + ahead):
                    copy.wait_send()
            for copy in out_copies(back, 2, k):
                copy.wait()


def local(queries, span_key_values, key_value_cache, chosen, offset):
    n_ctx = lax.axis_size("ctx")
    n_seg = lax.axis_size("segment")
    me = lax.axis_index("ctx")
    tokens = queries.shape[1]
    kv_heads = key_value_cache.shape[3] // HEAD_SIZE
    q_heads = queries.shape[2] // HEAD_SIZE
    per_head = q_heads // kv_heads
    slots = key_value_cache.shape[1]
    blocks_here = slots // BLOCK_TOKENS
    if not (
        n_ctx == 4
        and tokens == BLOCK_TOKENS
        and n_seg > 1
        and per_head % PAIR == 0
        and slots * kv_heads <= 16384
        and q_heads == 8 * PAIR
        and kv_heads == 4
    ):
        return general(queries, span_key_values, key_value_cache, chosen, offset)
    bf16, f32 = jnp.bfloat16, jnp.float32
    dma = pltpu.SemaphoreType.DMA
    chunks, rows = q_heads // PAIR, PAIR * tokens
    lines = rows // HEAD_SIZE
    vmem = pl.BlockSpec(memory_space=pltpu.VMEM)
    smem = pl.BlockSpec(memory_space=pltpu.SMEM)
    anywhere = pl.BlockSpec(memory_space=pl.ANY)

    positions = (offset[0] + me * tokens + jnp.arange(tokens, dtype=jnp.int32)).astype(f32)
    half = HEAD_SIZE // 2
    frequencies = ROPE_BASE ** (-(2.0 * jnp.arange(half, dtype=f32)) / HEAD_SIZE)
    angles = positions[:, None] * frequencies[None, :]
    cosine, sine = jnp.cos(angles), jnp.sin(angles)
    cos_table = jnp.concatenate([cosine, cosine], axis=1)
    sin_table = jnp.concatenate([-sine, sine], axis=1)
    q_own, q_early = pl.pallas_call(
        turn_kernel,
        out_shape=(
            jax.ShapeDtypeStruct((chunks, rows, HEAD_SIZE), bf16),
            jax.ShapeDtypeStruct((chunks - 1, rows, HEAD_SIZE), bf16),
        ),
        in_specs=[vmem] * 3,
        out_specs=(vmem, vmem),
        cost_estimate=pl.CostEstimate(
            flops=6 * queries.size, bytes_accessed=4 * queries.size, transcendentals=0
        ),
        compiler_params=pltpu.CompilerParams(vmem_limit_bytes=24 * 2**20),
    )(queries, cos_table, sin_table)
    q_left = lax.ppermute(q_early, "ctx", [(i, i + 1) for i in range(n_ctx - 1)])
    q_right = lax.ppermute(q_early, "ctx", [(i + 1, i) for i in range(n_ctx - 1)])

    cache = key_value_cache[0].transpose(1, 0, 2)
    span = span_key_values[0].transpose(1, 0, 2)
    picks = chosen.reshape(-1)
    work = 4 * q_heads * tokens * BLOCK_TOKENS * HEAD_SIZE
    own, own_logs = pl.pallas_call(
        home_kernel,
        out_shape=(
            jax.ShapeDtypeStruct((chunks, rows, HEAD_SIZE), f32),
            jax.ShapeDtypeStruct((chunks, lines, HEAD_SIZE), f32),
        ),
        in_specs=[smem] + [vmem] * 4 + [anywhere],
        out_specs=(anywhere, vmem),
        scratch_shapes=[
            pltpu.VMEM((chunks // kv_heads, rows, 2 * HEAD_SIZE), f32),
            pltpu.VMEM((chunks // kv_heads, rows, HEAD_SIZE), f32),
            pltpu.VMEM((tokens, 2 * HEAD_SIZE), bf16),
            pltpu.VMEM((kv_heads, 2, slots, HEAD_SIZE), bf16),
            pltpu.VMEM((chunks, rows, HEAD_SIZE), f32),
            dma((kv_heads,)),
            dma((kv_heads,)),
        ],
        cost_estimate=pl.CostEstimate(
            flops=6 * work, bytes_accessed=16 * 2**20, transcendentals=work // 128
        ),
        compiler_params=pltpu.CompilerParams(vmem_limit_bytes=48 * 2**20),
    )(picks, q_own, span, cos_table, sin_table, cache)

    return pl.pallas_call(
        functools.partial(relay_kernel, n_seg),
        out_shape=jax.ShapeDtypeStruct(queries.shape, bf16),
        in_specs=[smem, vmem] + [anywhere] * 5,
        out_specs=anywhere,
        scratch_shapes=[
            pltpu.VMEM((n_ctx, chunks, rows, HEAD_SIZE), bf16),
            pltpu.VMEM((kv_heads, slots, HEAD_SIZE), bf16),
            pltpu.VMEM((kv_heads, slots, 2 * HEAD_SIZE), bf16),
            pltpu.VMEM((2, 3, chunks, rows, HEAD_SIZE), bf16),
            pltpu.VMEM((2, 3, chunks, lines, HEAD_SIZE), f32),
            pltpu.VMEM((2, chunks, rows, HEAD_SIZE), f32),
            pltpu.VMEM((2, chunks, lines, HEAD_SIZE), f32),
            pltpu.VMEM((chunks, rows, HEAD_SIZE), f32),
            pltpu.VMEM((rows, 2 * HEAD_SIZE), f32),
            pltpu.VMEM((rows, HEAD_SIZE), f32),
            dma((2 * kv_heads + 3,)),
            dma((n_ctx, chunks)),
            dma((n_ctx, chunks)),
            dma((2,)),
            dma((2, 3, chunks)),
            dma((2, 3, chunks)),
            dma((2, 3, chunks)),
            dma((2, 3, chunks)),
            dma((chunks, PAIR)),
            dma((chunks, PAIR)),
        ],
        cost_estimate=pl.CostEstimate(
            flops=24 * work, bytes_accessed=32 * 2**20, transcendentals=work // 16
        ),
        compiler_params=pltpu.CompilerParams(
            collective_id=0, has_side_effects=True, vmem_limit_bytes=60 * 2**20
        ),
    )(picks, own_logs, own, cache, q_own, q_left, q_right)


def solution(mesh):
    return jax.shard_map(
        local,
        mesh=mesh,
        in_specs=(
            P(("groups", "segment"), "ctx", "head"),
            P(("groups", "segment"), "ctx", None, "head"),
            P(("groups", "segment"), "ctx", None, "head"),
            P(("groups", "segment"), None, "head", None),
            P(("groups", "segment")),
        ),
        out_specs=P(("groups", "segment"), "ctx", "head"),
        check_vma=False,
    )
```

```python
import functools

import jax
import jax.numpy as jnp
from jax import lax
from jax.experimental import pallas as pl
from jax.experimental.pallas import tpu as pltpu
from jax.sharding import PartitionSpec as P

HEAD_SIZE = 128
BLOCK_TOKENS = 512
CHOSEN_BLOCKS = 8


ROPE_BASE = 500000.0


def swapped(x, axis, stride):
    return lax.ppermute(x, axis, [(i, i ^ 1 << stride) for i in range(lax.axis_size(axis))])


def passed_along(block, axis, distance):
    devices = range(lax.axis_size(axis))
    route = [((i - distance) % len(devices), i) for i in devices]
    return lax.ppermute(block, axis, route)


def apply_rotary(values, token_positions):
    half_dim = values.shape[-1] // 2
    frequencies = ROPE_BASE ** (-(2.0 * jnp.arange(half_dim, dtype=jnp.float32)) / values.shape[-1])
    angles = token_positions[:, None] * frequencies[None, :]
    cosine = jnp.cos(angles)[:, None, :]
    sine_part = jnp.sin(angles)[:, None, :]
    widened = values.astype(jnp.float32)
    first_half = widened[..., :half_dim]
    second_half = widened[..., half_dim:]
    joined = jnp.concatenate(
        [
            first_half * cosine - second_half * sine_part,
            second_half * cosine + first_half * sine_part,
        ],
        axis=-1,
    )
    return joined.astype(jnp.bfloat16)


def combine(earlier, later):
    maxima = jnp.maximum(earlier[0], later[0])
    first_factor = jnp.exp(earlier[0] - maxima)
    second_factor = jnp.exp(later[0] - maxima)
    totals = earlier[1] * first_factor + later[1] * second_factor
    weighted = earlier[2] * first_factor[..., None] + later[2] * second_factor[..., None]
    return (maxima, totals, weighted)


def general(queries, span_key_values, key_value_cache, chosen, offset):
    ctx_size = lax.axis_size("ctx")
    my_index = lax.axis_index("ctx")
    tok_rows = queries.shape[1]
    kv_heads = key_value_cache.shape[3] // HEAD_SIZE
    q_heads = queries.shape[2] // HEAD_SIZE
    per_value_head = q_heads // kv_heads
    members = ctx_size // kv_heads
    blocks_here = key_value_cache.shape[1] // BLOCK_TOKENS
    blocks_total = blocks_here * ctx_size
    q_blocks = chosen.shape[1]
    per_block = BLOCK_TOKENS // tok_rows
    key_rows = BLOCK_TOKENS // members
    own_rows = tok_rows // members
    my_head = my_index // members
    my_rank = my_index % members
    score_scale = HEAD_SIZE ** (-0.5)
    token_start = offset[0] + my_index * tok_rows
    token_positions = (token_start + jnp.arange(tok_rows, dtype=jnp.int32)).astype(jnp.float32)
    rot_query = apply_rotary(queries[0].reshape(tok_rows, q_heads, HEAD_SIZE), token_positions)
    rotated_key_rows = apply_rotary(
        span_key_values[0, :, 0].reshape(tok_rows, kv_heads, HEAD_SIZE), token_positions
    )
    fresh_values = span_key_values[0, :, 1].reshape(tok_rows, kv_heads, HEAD_SIZE)
    query_send = jnp.broadcast_to(
        rot_query.reshape(tok_rows, kv_heads, 1, per_value_head * HEAD_SIZE),
        (tok_rows, kv_heads, members, per_value_head * HEAD_SIZE),
    )
    query_send = query_send.reshape(tok_rows, ctx_size, per_value_head * HEAD_SIZE)
    pair_rows = jnp.concatenate([rotated_key_rows, fresh_values], axis=-1)
    pair_send = (
        pair_rows.reshape(members, own_rows, kv_heads, 2 * HEAD_SIZE)
        .transpose(1, 2, 0, 3)
        .reshape(own_rows, ctx_size, 2 * HEAD_SIZE)
    )
    query_recv, pair_recv = (
        lax.all_to_all(query_send, "ctx", split_axis=1, concat_axis=1, tiled=True),
        lax.all_to_all(pair_send, "ctx", split_axis=1, concat_axis=1, tiled=True),
    )
    picks_here = chosen[0]
    needed = jnp.any(
        picks_here[..., None] == jnp.arange(blocks_total, dtype=jnp.int32), axis=(0, 2)
    )
    needed_here = lax.dynamic_slice_in_dim(needed, my_index * blocks_here, blocks_here, axis=1)
    needed_here = needed_here.T.reshape(blocks_here, 1, kv_heads, 1, 1, 1)
    arranged_rows = (
        key_value_cache[0]
        .reshape(blocks_here, members, key_rows, 2, kv_heads, HEAD_SIZE)
        .transpose(0, 2, 4, 1, 3, 5)
    )
    arranged_rows = jnp.where(needed_here, arranged_rows, jnp.zeros((), jnp.bfloat16))
    tile_send = arranged_rows.reshape(blocks_here * key_rows, ctx_size, 2 * HEAD_SIZE)
    fetched = lax.all_to_all(tile_send, "ctx", split_axis=1, concat_axis=1, tiled=True)
    fetched = fetched.reshape(blocks_here, key_rows, ctx_size, 2 * HEAD_SIZE)
    maxima_parts = []
    totals_parts = []
    weighted_parts = []
    for index_of_block in range(q_blocks):
        block_ids = picks_here[index_of_block][my_head]
        owner_rank = block_ids // blocks_here
        slot_index = block_ids % blocks_here
        picked = jnp.stack(
            [
                lax.dynamic_slice(
                    fetched,
                    (slot_index[n], 0, owner_rank[n], 0),
                    (1, key_rows, 1, 2 * HEAD_SIZE),
                )[0, :, 0]
                for n in range(CHOSEN_BLOCKS)
            ]
        )
        sel_keys = picked[..., :HEAD_SIZE].reshape(CHOSEN_BLOCKS * key_rows, HEAD_SIZE)
        sel_values = picked[..., HEAD_SIZE:].reshape(CHOSEN_BLOCKS * key_rows, HEAD_SIZE)
        first_source = index_of_block * per_block
        own_pairs = pair_recv[:, first_source : first_source + per_block]
        own_keys = own_pairs[..., :HEAD_SIZE].reshape(own_rows * per_block, HEAD_SIZE)
        own_values = own_pairs[..., HEAD_SIZE:].reshape(own_rows * per_block, HEAD_SIZE)
        query_rows = query_recv[:, first_source : first_source + per_block].reshape(
            tok_rows * per_block * per_value_head, HEAD_SIZE
        )
        sources = first_source + jnp.arange(per_block, dtype=jnp.int32)
        query_token = sources[None, :] * tok_rows + jnp.arange(tok_rows, dtype=jnp.int32)[:, None]
        query_token = jnp.broadcast_to(
            query_token[:, :, None], (tok_rows, per_block, per_value_head)
        ).reshape(-1)
        key_token = (
            sources[None, :] * tok_rows
            + my_rank * own_rows
            + jnp.arange(own_rows, dtype=jnp.int32)[:, None]
        )
        key_token = key_token.reshape(-1)
        sel_scores = (
            jnp.dot(query_rows, sel_keys.T, preferred_element_type=jnp.float32) * score_scale
        )
        own_scores = (
            jnp.dot(query_rows, own_keys.T, preferred_element_type=jnp.float32) * score_scale
        )
        causal = key_token[None, :] <= query_token[:, None]
        own_scores = jnp.where(causal, own_scores, -jnp.inf)
        maxima = jnp.maximum(jnp.max(sel_scores, axis=1), jnp.max(own_scores, axis=1))
        sel_weights = jnp.exp(sel_scores - maxima[:, None])
        own_weights = jnp.exp(own_scores - maxima[:, None])
        totals = jnp.sum(sel_weights, axis=1) + jnp.sum(own_weights, axis=1)
        weighted = jnp.dot(
            sel_weights, sel_values.astype(jnp.float32), precision=lax.Precision.HIGHEST
        )
        weighted = weighted + jnp.dot(
            own_weights, own_values.astype(jnp.float32), precision=lax.Precision.HIGHEST
        )
        maxima_parts.append(maxima.reshape(tok_rows, per_block, per_value_head))
        totals_parts.append(totals.reshape(tok_rows, per_block, per_value_head))
        weighted_parts.append(weighted.reshape(tok_rows, per_block, per_value_head, HEAD_SIZE))
    maxima_all = jnp.concatenate(maxima_parts, axis=1)
    totals_all = jnp.concatenate(totals_parts, axis=1)
    weighted_all = jnp.concatenate(weighted_parts, axis=1)
    current = (maxima_all, totals_all, weighted_all)
    bit_count = members.bit_length() - 1
    for bit_index in reversed(range(bit_count)):
        half_rows = current[0].shape[0] // 2
        my_bit = my_index // 2**bit_index % 2
        kept = tuple(
            (
                lax.dynamic_slice_in_dim(part_array, my_bit * half_rows, half_rows, 0)
                for part_array in current
            )
        )
        given = tuple(
            (
                lax.dynamic_slice_in_dim(part_array, (1 - my_bit) * half_rows, half_rows, 0)
                for part_array in current
            )
        )
        partner = swapped((given[0], given[1], given[2]), "ctx", bit_index)
        current = combine(kept, partner)
    finished = (
        (current[2] / current[1][..., None])
        .astype(jnp.bfloat16)
        .reshape(own_rows, ctx_size, per_value_head * HEAD_SIZE)
    )
    returned = lax.all_to_all(finished, "ctx", split_axis=1, concat_axis=1, tiled=True)
    context = (
        returned.reshape(own_rows, kv_heads, members, per_value_head * HEAD_SIZE)
        .transpose(2, 0, 1, 3)
        .reshape(tok_rows, q_heads * HEAD_SIZE)
    )
    handed = passed_along(context, "segment", 1)
    return handed[None]


LOG2E = 1.4426950408889634
MESH = pl.DeviceIdType.MESH
PAIR = 2
NOTHING = -1e29
HIDDEN = 1e30
SCALE2 = LOG2E * HEAD_SIZE ** (-0.5)


def turned(block, cosine, sine):
    wide = block.astype(jnp.float32)
    other = pltpu.roll(wide, HEAD_SIZE // 2, 1)
    return (wide * cosine + other * sine).astype(jnp.bfloat16)


def widened(column, count):
    return jnp.concatenate([column] * count, axis=1)


def fold(query, keys, values, shift, causal, first, acc, top):
    scores = lax.dot_general(
        query, keys, (((1,), (1,)), ((), ())), preferred_element_type=jnp.float32
    )
    if causal is not None:
        scores = jnp.where(causal, scores, -jnp.inf)
    new = jnp.max(scores, axis=1, keepdims=True) * SCALE2
    if shift is not None:
        new = new - shift
    new = jnp.broadcast_to(new, (scores.shape[0], HEAD_SIZE))
    if first:
        new = jnp.maximum(new, NOTHING)
    else:
        held = top[...]
        new = jnp.maximum(new, held)
    taken = new if shift is None else new + shift
    weights = jnp.exp2(scores * SCALE2 - widened(taken, scores.shape[1] // HEAD_SIZE))
    part = jnp.dot(weights.astype(jnp.bfloat16), values, preferred_element_type=jnp.float32)
    if first:
        acc[...] = part
    else:
        acc[...] = acc[...] * widened(jnp.exp2(held - new), 2) + part
    top[...] = new


def diagonal():
    rows = lax.broadcasted_iota(jnp.int32, (HEAD_SIZE, HEAD_SIZE), 0)
    columns = lax.broadcasted_iota(jnp.int32, (HEAD_SIZE, HEAD_SIZE), 1)
    return rows == columns


def closed(acc, top):
    totals = jnp.maximum(acc[:, HEAD_SIZE:], 1e-30)
    context = acc[:, :HEAD_SIZE] / totals
    logs = top[...] + jnp.log2(totals)
    eye = diagonal()
    lines = [
        jnp.sum(
            jnp.where(eye, logs[r : r + HEAD_SIZE], 0.0), axis=0, keepdims=True
        )
        for r in range(0, logs.shape[0], HEAD_SIZE)
    ]
    return context, jnp.concatenate(lines, axis=0)


def merged(own, own_logs, other, other_logs):
    most = jnp.maximum(own_logs, other_logs)
    mine = jnp.exp2(own_logs - most)
    total = mine + jnp.exp2(other_logs - most)
    share = mine / total
    eye = diagonal()
    columns = [
        jnp.broadcast_to(
            jnp.sum(
                jnp.where(eye, share[r : r + 1], 0.0), axis=1, keepdims=True
            ),
            (HEAD_SIZE, HEAD_SIZE),
        )
        for r in range(share.shape[0])
    ]
    other = other.astype(jnp.float32)
    return other + jnp.concatenate(columns, axis=0) * (own - other), most + jnp.log2(total)


def turn_kernel(q_ref, cos_ref, sin_ref, early_ref, last_ref):
    tokens = q_ref.shape[1]
    for h in range(q_ref.shape[2] // HEAD_SIZE):
        spot = slice(h % PAIR * tokens, (h % PAIR + 1) * tokens)
        rows = turned(
            q_ref[0, :, h * HEAD_SIZE : (h + 1) * HEAD_SIZE], cos_ref[...], sin_ref[...]
        )
        if h // PAIR < early_ref.shape[0]:
            early_ref[h // PAIR, spot] = rows
        else:
            last_ref[0, spot] = rows


def home_kernel(
    chosen_ref, span_ref, cos_ref, sin_ref, early_ref, last_ref, cache_ref, out_ref,
    acc, top, values, held, made, q_ref, load_sem, store_sem, q_sem,
):
    me = lax.axis_index("ctx")
    tokens = cos_ref.shape[0]
    kv_heads = cache_ref.shape[2] // HEAD_SIZE
    halves = q_ref.shape[0] // kv_heads
    blocks_here = cache_ref.shape[1] // BLOCK_TOKENS

    def load(g):
        spot = pl.ds(pl.multiple_of(g * HEAD_SIZE, HEAD_SIZE), HEAD_SIZE)
        return pltpu.make_async_copy(cache_ref.at[:, :, spot], held.at[g], load_sem.at[g])

    def store(g):
        lines = pl.ds(g * halves, halves)
        return pltpu.make_async_copy(made.at[lines], out_ref.at[lines], store_sem.at[g])

    early = early_ref.shape[0]
    q_loads = (
        pltpu.make_async_copy(early_ref, q_ref.at[pl.ds(0, early)], q_sem.at[0]),
        pltpu.make_async_copy(last_ref, q_ref.at[pl.ds(early, 1)], q_sem.at[1]),
    )
    for copy in q_loads:
        copy.start()
    for g in range(kv_heads):
        load(g).start()
    values[:, HEAD_SIZE:] = jnp.ones((tokens, HEAD_SIZE), values.dtype)

    for copy in q_loads:
        copy.wait()

    @pl.loop(0, kv_heads)
    def _(g):
        spot = pl.ds(pl.multiple_of(g * HEAD_SIZE, HEAD_SIZE), HEAD_SIZE)
        values[:, :HEAD_SIZE] = span_ref[1, :, spot]
        own_keys = turned(span_ref[0, :, spot], cos_ref[...], sin_ref[...])
        rows = lax.broadcasted_iota(jnp.int32, (tokens, tokens), 0)
        columns = lax.broadcasted_iota(jnp.int32, (tokens, tokens), 1)
        causal = jnp.concatenate([columns <= rows] * PAIR, axis=0)
        for i in range(halves):
            fold(q_ref[g * halves + i], own_keys, values[...], None, causal, True, acc.at[i], top.at[i])
        load(g).wait()

        @pl.loop(0, CHOSEN_BLOCKS)
        def _(n):
            block = chosen_ref[(me * kv_heads + g) * CHOSEN_BLOCKS + n] - me * blocks_here

            @pl.when((block >= 0) & (block < blocks_here))
            def _():
                lines = pl.ds(pl.multiple_of(block * BLOCK_TOKENS, BLOCK_TOKENS), BLOCK_TOKENS)
                values[:, :HEAD_SIZE] = held[g, 1, lines]
                for i in range(halves):
                    fold(
                        q_ref[g * halves + i], held[g, 0, lines], values[...], None, None, False,
                        acc.at[i], top.at[i],
                    )

        for i in range(halves):
            context, logs = closed(acc[i], top[i])
            made[g * halves + i, : context.shape[0]] = context
            made[g * halves + i, context.shape[0] :] = logs
        store(g).start()

    for g in range(kv_heads):
        store(g).wait()


def relay_kernel(
    n_seg, chosen_ref, own_hbm_ref, cache_ref, q_ref, ql_ref, qr_ref, out_ref,
    q_buf, k_buf, v_buf, buf, logs, stash, stash_logs, own_ref, acc, top,
    load_sem, q_send, q_recv, last_send, p_send, p_recv, l_send, l_recv, o_send, o_recv,
):
    me = lax.axis_index("ctx")
    seg = lax.axis_index("segment")
    side = me // 2
    ahead = 1 - 2 * side
    is_mid = (me == 1) | (me == 2)
    is_end = (me == 0) | (me == 3)
    forth, back = side, 1 - side
    kv_heads, slots = k_buf.shape[0], k_buf.shape[1]
    chunks, rows = own_ref.shape[0], q_ref.shape[1]
    last = chunks - 1
    tokens = rows // PAIR
    halves = chunks // kv_heads
    blocks_here = slots // BLOCK_TOKENS
    after = lax.rem(seg + 1, n_seg)
    before = lax.rem(seg + n_seg - 1, n_seg)

    def hidden(b, g, j):
        amount = jnp.float32(HIDDEN)
        for n in range(CHOSEN_BLOCKS):
            block = chosen_ref[(b * kv_heads + g) * CHOSEN_BLOCKS + n]
            amount = jnp.where(block == me * blocks_here + j, jnp.float32(0.0), amount)
        return amount

    def seen(b):
        return b * ahead + 3 * side

    def load(i, source, target):
        return pltpu.make_async_copy(source, target, load_sem.at[i])

    def head_loads(g):
        spot = pl.ds(pl.multiple_of(g * HEAD_SIZE, HEAD_SIZE), HEAD_SIZE)
        return (
            load(2 * g, cache_ref.at[0, :, spot], k_buf.at[g]),
            load(2 * g + 1, cache_ref.at[1, :, spot], v_buf.at[g, :, pl.ds(0, HEAD_SIZE)]),
        )

    loads = []
    for g in range(kv_heads):
        loads.append(head_loads(g))
    from_left = load(2 * kv_heads, ql_ref, q_buf.at[lax.max(me - 1, 0), pl.ds(0, last)])
    from_right = load(2 * kv_heads + 1, qr_ref, q_buf.at[lax.min(me + 1, 3), pl.ds(0, last)])
    for copy in loads[0]:
        copy.start()

    @pl.when(me > 0)
    def _():
        from_left.start()

    @pl.when(me < 3)
    def _():
        from_right.start()

    for copies in loads[1:]:
        for copy in copies:
            copy.start()

    own_load = load(2 * kv_heads + 2, own_hbm_ref, own_ref)
    own_load.start()
    barrier = pltpu.get_barrier_semaphore()

    def greet(**place):
        pl.semaphore_signal(barrier, inc=1, device_id=place, device_id_type=MESH)

    @pl.when(me > 0)
    def _():
        greet(ctx=me - 1)

    @pl.when(me < 3)
    def _():
        greet(ctx=me + 1)

    others = (after,) if n_seg == 2 else (after, before)
    for other in others:
        greet(segment=other)

    for g in range(kv_heads):
        v_buf[g, :, HEAD_SIZE:] = jnp.ones((slots, HEAD_SIZE), v_buf.dtype)

    @pl.when(is_mid)
    def _():
        pl.semaphore_wait(barrier, 2 + len(others))

    @pl.when(is_end)
    def _():
        pl.semaphore_wait(barrier, 1 + len(others))

    def q_copy(source, b, k, target):
        return pltpu.make_async_remote_copy(
            src_ref=source,
            dst_ref=q_buf.at[b, k],
            send_sem=q_send.at[b, k],
            recv_sem=q_recv.at[b, k],
            device_id={"ctx": target},
            device_id_type=MESH,
        )

    def second_hops(k, left_source, right_source):
        left = q_copy(left_source, lax.min(me + 1, 3), k, lax.max(me - 1, 0))
        right = q_copy(right_source, lax.max(me - 1, 0), k, lax.min(me + 1, 3))
        return left, right

    def early_hops(k):
        return second_hops(k, qr_ref.at[k], ql_ref.at[k])

    def late_hops():
        return second_hops(
            last, q_buf.at[lax.min(me + 1, 3), last], q_buf.at[lax.max(me - 1, 0), last]
        )

    def last_hop(way, target):
        return pltpu.make_async_remote_copy(
            src_ref=q_ref.at[0],
            dst_ref=q_buf.at[me, last],
            send_sem=last_send.at[way],
            recv_sem=q_recv.at[me, last],
            device_id={"ctx": target},
            device_id_type=MESH,
        )

    def third_hop(k):
        b = seen(3)
        return q_copy(q_buf.at[b, k], b, k, me - ahead)

    def part_copies(way, p, k, target):
        return (
            pltpu.make_async_remote_copy(
                src_ref=buf.at[way, p, k],
                dst_ref=buf.at[way, p, k],
                send_sem=p_send.at[way, p, k],
                recv_sem=p_recv.at[way, p, k],
                device_id={"ctx": target},
                device_id_type=MESH,
            ),
            pltpu.make_async_remote_copy(
                src_ref=logs.at[way, p, k],
                dst_ref=logs.at[way, p, k],
                send_sem=l_send.at[way, p, k],
                recv_sem=l_recv.at[way, p, k],
                device_id={"ctx": target},
                device_id_type=MESH,
            ),
        )

    def arrived(way, p, k):
        for copy in part_copies(way, p, k, me + ahead):
            copy.wait_recv()

    def send(way, p, k, target):
        for copy in part_copies(way, p, k, target):
            copy.start()

    def out_copies(way, p, k):
        return [
            pltpu.make_async_remote_copy(
                src_ref=buf.at[way, p, k, pl.ds(i * tokens, tokens)],
                dst_ref=out_ref.at[
                    0,
                    :,
                    pl.ds(pl.multiple_of((k * PAIR + i) * HEAD_SIZE, HEAD_SIZE), HEAD_SIZE),
                ],
                send_sem=o_send.at[k, i],
                recv_sem=o_recv.at[k, i],
                device_id={"segment": after},
                device_id_type=MESH,
            )
            for i in range(PAIR)
        ]

    def relay(way, p, k, own, own_log, target):
        arrived(way, p, k)
        value, log = merged(own, own_log, buf[way, p, k], logs[way, p, k])
        buf[way, p, k] = value.astype(buf.dtype)
        logs[way, p, k] = log
        send(way, p, k, target)

    def near(u):
        p, k = u // chunks, lax.rem(u, chunks)
        relay(forth, p, k, stash[p - 1, k], stash_logs[p - 1, k], me + ahead)

    def mid_final(k):
        arrived(forth, 0, k)
        arrived(back, 1, k)
        value, log = merged(own_ref[k, :rows], own_ref[k, rows:], buf[forth, 0, k], logs[forth, 0, k])
        value, log = merged(value, log, buf[back, 1, k], logs[back, 1, k])
        buf[back, 1, k] = value.astype(buf.dtype)
        for copy in out_copies(back, 1, k):
            copy.start()

    def end_final(k):
        arrived(back, 2, k)
        value, log = merged(own_ref[k, :rows], own_ref[k, rows:], buf[back, 2, k], logs[back, 2, k])
        buf[back, 2, k] = value.astype(buf.dtype)
        for copy in out_copies(back, 2, k):
            copy.start()

    @pl.when(is_mid)
    def _():
        @pl.loop(0, last)
        def _(k):
            for copy in early_hops(k):
                copy.start()

            @pl.when(k == 1)
            def _():
                last_hop(0, me + ahead).start()
                last_hop(1, me - ahead).start()

    @pl.when(is_end)
    def _():
        last_hop(0, me + ahead).start()

    @pl.when(me > 0)
    def _():
        from_left.wait()

    @pl.when(me < 3)
    def _():
        from_right.wait()

    steps, lead = 3 * chunks, chunks // 2

    @pl.loop(0, steps)
    def _(t):
        late = t - lead
        place = jnp.where(
            is_mid,
            lax.rem(t // chunks + 2, 4),
            jnp.where((late < 0) | (late >= 2 * chunks), 1, 2 + late // chunks),
        )
        k = jnp.where(
            is_mid,
            lax.rem(t, chunks),
            jnp.where(late < 0, t, jnp.where(late < 2 * chunks, lax.rem(late + chunks, chunks), t - 2 * chunks)),
        )
        g = k // halves
        b = seen(place)

        @pl.when((t < chunks) & is_mid & (lax.rem(t, halves) == 0))
        def _():
            for copy in head_loads(g):
                copy.wait()

        @pl.when(is_end & (lax.rem(t, halves) == 0) & ((t < lead) | ((t >= 2 * lead) & (t < chunks + lead))))
        def _():
            for copy in head_loads(g):
                copy.wait()

        @pl.when(is_end & (late >= 0) & ((late < 2 * chunks) | (t == steps - 1)))
        def _():
            q_copy(q_buf.at[b, k], b, k, me + ahead).wait_recv()

        @pl.when(is_mid & (t >= 2) & (t < chunks + 2))
        def _():
            copy = third_hop(t - 2)
            copy.wait_recv()
            copy.start()

        @pl.when(t == chunks)
        def _():
            own_load.wait()

        @pl.when(is_mid & (t == 3))
        def _():
            left, right = late_hops()
            q_copy(q_ref.at[0], lax.min(me + 1, 3), last, me + ahead).wait_recv()
            q_copy(q_ref.at[0], lax.max(me - 1, 0), last, me + ahead).wait_recv()
            left.start()
            right.start()

        query = q_buf[b, k]
        for j in range(blocks_here):
            lines = slice(j * BLOCK_TOKENS, (j + 1) * BLOCK_TOKENS)
            fold(
                query, k_buf[g, lines], v_buf[g, lines],
                hidden(b, g, j), None, j == 0, acc, top,
            )
        context, log = closed(acc[...], top[...])

        @pl.when(is_end)
        def _():
            buf[forth, place - 1, k] = context.astype(buf.dtype)
            logs[forth, place - 1, k] = log
            send(forth, place - 1, k, me + ahead)

        @pl.when(is_mid & (t < 2 * chunks))
        def _():
            stash[t // chunks, k] = context
            stash_logs[t // chunks, k] = log

        @pl.when(is_mid & (t >= 2 * chunks))
        def _():
            relay(back, 2, k, context, log, me - ahead)

        @pl.when(is_mid & (t + 2 >= chunks) & (t + 2 < 3 * chunks))
        def _():
            near(t + 2)

        @pl.when(is_mid & (t >= chunks + 2) & (t < chunks + 2 + lead))
        def _():
            mid_final(t - chunks - 2)

        @pl.when(is_mid & (t >= 2 * chunks + 2 + lead))
        def _():
            mid_final(t - 2 * chunks - 2)

        @pl.when(is_end & (t >= 2 * chunks + 3))
        def _():
            end_final(t - 2 * chunks - 3)

    @pl.when(is_mid)
    def _():
        @pl.loop(chunks - 2, chunks)
        def _(k):
            mid_final(k)

    @pl.when(is_end)
    def _():
        @pl.loop(chunks - 3, chunks)
        def _(k):
            end_final(k)

    last_hop(0, me + ahead).wait_send()

    @pl.when(is_mid)
    def _():
        last_hop(1, me - ahead).wait_send()

    @pl.when(is_mid)
    def _():
        @pl.loop(0, chunks)
        def _(k):
            for copy in second_hops(k, q_ref.at[0], q_ref.at[0]) + (third_hop(k),):
                copy.wait_send()
            for copy in part_copies(forth, 1, k, me + ahead) + part_copies(forth, 2, k, me + ahead):
                copy.wait_send()
            for copy in part_copies(back, 2, k, me - ahead):
                copy.wait_send()
            for copy in out_copies(back, 1, k):
                copy.wait()

    @pl.when(is_end)
    def _():
        @pl.loop(0, chunks)
        def _(k):
            for p in range(3):
                for copy in part_copies(forth, p, k, me + ahead):
                    copy.wait_send()
            for copy in out_copies(back, 2, k):
                copy.wait()


def local(queries, span_key_values, key_value_cache, chosen, offset):
    n_ctx = lax.axis_size("ctx")
    n_seg = lax.axis_size("segment")
    me = lax.axis_index("ctx")
    tokens = queries.shape[1]
    kv_heads = key_value_cache.shape[3] // HEAD_SIZE
    q_heads = queries.shape[2] // HEAD_SIZE
    per_head = q_heads // kv_heads
    slots = key_value_cache.shape[1]
    blocks_here = slots // BLOCK_TOKENS
    if not (
        n_ctx == 4
        and tokens == BLOCK_TOKENS
        and n_seg > 1
        and per_head % PAIR == 0
        and slots * kv_heads <= 16384
        and q_heads == 8 * PAIR
        and kv_heads == 4
    ):
        return general(queries, span_key_values, key_value_cache, chosen, offset)
    bf16, f32 = jnp.bfloat16, jnp.float32
    dma = pltpu.SemaphoreType.DMA
    chunks, rows = q_heads // PAIR, PAIR * tokens
    lines = rows // HEAD_SIZE
    vmem = pl.BlockSpec(memory_space=pltpu.VMEM)
    smem = pl.BlockSpec(memory_space=pltpu.SMEM)
    anywhere = pl.BlockSpec(memory_space=pl.ANY)

    positions = (offset[0] + me * tokens + jnp.arange(tokens, dtype=jnp.int32)).astype(f32)
    half = HEAD_SIZE // 2
    frequencies = ROPE_BASE ** (-(2.0 * jnp.arange(half, dtype=f32)) / HEAD_SIZE)
    angles = positions[:, None] * frequencies[None, :]
    cosine, sine = jnp.cos(angles), jnp.sin(angles)
    cos_table = jnp.concatenate([cosine, cosine], axis=1)
    sin_table = jnp.concatenate([-sine, sine], axis=1)
    q_early, q_last = pl.pallas_call(
        turn_kernel,
        out_shape=(
            jax.ShapeDtypeStruct((chunks - 1, rows, HEAD_SIZE), bf16),
            jax.ShapeDtypeStruct((1, rows, HEAD_SIZE), bf16),
        ),
        in_specs=[vmem] * 3,
        out_specs=(vmem, vmem),
        cost_estimate=pl.CostEstimate(
            flops=6 * queries.size, bytes_accessed=4 * queries.size, transcendentals=0
        ),
        compiler_params=pltpu.CompilerParams(vmem_limit_bytes=24 * 2**20),
    )(queries, cos_table, sin_table)
    q_left = lax.ppermute(q_early, "ctx", [(i, i + 1) for i in range(n_ctx - 1)])
    q_right = lax.ppermute(q_early, "ctx", [(i + 1, i) for i in range(n_ctx - 1)])

    cache = key_value_cache[0].transpose(1, 0, 2)
    span = span_key_values[0].transpose(1, 0, 2)
    picks = chosen.reshape(-1)
    work = 4 * q_heads * tokens * BLOCK_TOKENS * HEAD_SIZE
    own = pl.pallas_call(
        home_kernel,
        out_shape=jax.ShapeDtypeStruct((chunks, rows + lines, HEAD_SIZE), f32),
        in_specs=[smem] + [vmem] * 3 + [anywhere] * 3,
        out_specs=anywhere,
        scratch_shapes=[
            pltpu.VMEM((chunks // kv_heads, rows, 2 * HEAD_SIZE), f32),
            pltpu.VMEM((chunks // kv_heads, rows, HEAD_SIZE), f32),
            pltpu.VMEM((tokens, 2 * HEAD_SIZE), bf16),
            pltpu.VMEM((kv_heads, 2, slots, HEAD_SIZE), bf16),
            pltpu.VMEM((chunks, rows + lines, HEAD_SIZE), f32),
            pltpu.VMEM((chunks, rows, HEAD_SIZE), bf16),
            dma((kv_heads,)),
            dma((kv_heads,)),
            dma((2,)),
        ],
        cost_estimate=pl.CostEstimate(
            flops=6 * work, bytes_accessed=16 * 2**20, transcendentals=work // 128
        ),
        compiler_params=pltpu.CompilerParams(vmem_limit_bytes=48 * 2**20),
    )(picks, span, cos_table, sin_table, q_early, q_last, cache)

    return pl.pallas_call(
        functools.partial(relay_kernel, n_seg),
        out_shape=jax.ShapeDtypeStruct(queries.shape, bf16),
        in_specs=[smem] + [anywhere] * 5,
        out_specs=anywhere,
        scratch_shapes=[
            pltpu.VMEM((n_ctx, chunks, rows, HEAD_SIZE), bf16),
            pltpu.VMEM((kv_heads, slots, HEAD_SIZE), bf16),
            pltpu.VMEM((kv_heads, slots, 2 * HEAD_SIZE), bf16),
            pltpu.VMEM((2, 3, chunks, rows, HEAD_SIZE), bf16),
            pltpu.VMEM((2, 3, chunks, lines, HEAD_SIZE), f32),
            pltpu.VMEM((2, chunks, rows, HEAD_SIZE), f32),
            pltpu.VMEM((2, chunks, lines, HEAD_SIZE), f32),
            pltpu.VMEM((chunks, rows + lines, HEAD_SIZE), f32),
            pltpu.VMEM((rows, 2 * HEAD_SIZE), f32),
            pltpu.VMEM((rows, HEAD_SIZE), f32),
            dma((2 * kv_heads + 3,)),
            dma((n_ctx, chunks)),
            dma((n_ctx, chunks)),
            dma((2,)),
            dma((2, 3, chunks)),
            dma((2, 3, chunks)),
            dma((2, 3, chunks)),
            dma((2, 3, chunks)),
            dma((chunks, PAIR)),
            dma((chunks, PAIR)),
        ],
        cost_estimate=pl.CostEstimate(
            flops=24 * work, bytes_accessed=32 * 2**20, transcendentals=work // 16
        ),
        compiler_params=pltpu.CompilerParams(
            collective_id=0, has_side_effects=True, vmem_limit_bytes=60 * 2**20
        ),
    )(picks, own, cache, q_last, q_left, q_right)


def solution(mesh):
    return jax.shard_map(
        local,
        mesh=mesh,
        in_specs=(
            P(("groups", "segment"), "ctx", "head"),
            P(("groups", "segment"), "ctx", None, "head"),
            P(("groups", "segment"), "ctx", None, "head"),
            P(("groups", "segment"), None, "head", None),
            P(("groups", "segment")),
        ),
        out_specs=P(("groups", "segment"), "ctx", "head"),
        check_vma=False,
    )
```

```python
import functools

import jax
import jax.numpy as jnp
from jax import lax
from jax.experimental import pallas as pl
from jax.experimental.pallas import tpu as pltpu
from jax.sharding import PartitionSpec as P

HEAD_SIZE = 128
BLOCK_TOKENS = 512
CHOSEN_BLOCKS = 8


ROPE_BASE = 500000.0


def swapped(x, axis, stride):
    return lax.ppermute(x, axis, [(i, i ^ 1 << stride) for i in range(lax.axis_size(axis))])


def passed_along(block, axis, distance):
    devices = range(lax.axis_size(axis))
    route = [((i - distance) % len(devices), i) for i in devices]
    return lax.ppermute(block, axis, route)


def apply_rotary(values, token_positions):
    half_dim = values.shape[-1] // 2
    frequencies = ROPE_BASE ** (-(2.0 * jnp.arange(half_dim, dtype=jnp.float32)) / values.shape[-1])
    angles = token_positions[:, None] * frequencies[None, :]
    cosine = jnp.cos(angles)[:, None, :]
    sine_part = jnp.sin(angles)[:, None, :]
    widened = values.astype(jnp.float32)
    first_half = widened[..., :half_dim]
    second_half = widened[..., half_dim:]
    joined = jnp.concatenate(
        [
            first_half * cosine - second_half * sine_part,
            second_half * cosine + first_half * sine_part,
        ],
        axis=-1,
    )
    return joined.astype(jnp.bfloat16)


def combine(earlier, later):
    maxima = jnp.maximum(earlier[0], later[0])
    first_factor = jnp.exp(earlier[0] - maxima)
    second_factor = jnp.exp(later[0] - maxima)
    totals = earlier[1] * first_factor + later[1] * second_factor
    weighted = earlier[2] * first_factor[..., None] + later[2] * second_factor[..., None]
    return (maxima, totals, weighted)


def general(queries, span_key_values, key_value_cache, chosen, offset):
    ctx_size = lax.axis_size("ctx")
    my_index = lax.axis_index("ctx")
    tok_rows = queries.shape[1]
    kv_heads = key_value_cache.shape[3] // HEAD_SIZE
    q_heads = queries.shape[2] // HEAD_SIZE
    per_value_head = q_heads // kv_heads
    members = ctx_size // kv_heads
    blocks_here = key_value_cache.shape[1] // BLOCK_TOKENS
    blocks_total = blocks_here * ctx_size
    q_blocks = chosen.shape[1]
    per_block = BLOCK_TOKENS // tok_rows
    key_rows = BLOCK_TOKENS // members
    own_rows = tok_rows // members
    my_head = my_index // members
    my_rank = my_index % members
    score_scale = HEAD_SIZE ** (-0.5)
    token_start = offset[0] + my_index * tok_rows
    token_positions = (token_start + jnp.arange(tok_rows, dtype=jnp.int32)).astype(jnp.float32)
    rot_query = apply_rotary(queries[0].reshape(tok_rows, q_heads, HEAD_SIZE), token_positions)
    rotated_key_rows = apply_rotary(
        span_key_values[0, :, 0].reshape(tok_rows, kv_heads, HEAD_SIZE), token_positions
    )
    fresh_values = span_key_values[0, :, 1].reshape(tok_rows, kv_heads, HEAD_SIZE)
    query_send = jnp.broadcast_to(
        rot_query.reshape(tok_rows, kv_heads, 1, per_value_head * HEAD_SIZE),
        (tok_rows, kv_heads, members, per_value_head * HEAD_SIZE),
    )
    query_send = query_send.reshape(tok_rows, ctx_size, per_value_head * HEAD_SIZE)
    pair_rows = jnp.concatenate([rotated_key_rows, fresh_values], axis=-1)
    pair_send = (
        pair_rows.reshape(members, own_rows, kv_heads, 2 * HEAD_SIZE)
        .transpose(1, 2, 0, 3)
        .reshape(own_rows, ctx_size, 2 * HEAD_SIZE)
    )
    query_recv, pair_recv = (
        lax.all_to_all(query_send, "ctx", split_axis=1, concat_axis=1, tiled=True),
        lax.all_to_all(pair_send, "ctx", split_axis=1, concat_axis=1, tiled=True),
    )
    picks_here = chosen[0]
    needed = jnp.any(
        picks_here[..., None] == jnp.arange(blocks_total, dtype=jnp.int32), axis=(0, 2)
    )
    needed_here = lax.dynamic_slice_in_dim(needed, my_index * blocks_here, blocks_here, axis=1)
    needed_here = needed_here.T.reshape(blocks_here, 1, kv_heads, 1, 1, 1)
    arranged_rows = (
        key_value_cache[0]
        .reshape(blocks_here, members, key_rows, 2, kv_heads, HEAD_SIZE)
        .transpose(0, 2, 4, 1, 3, 5)
    )
    arranged_rows = jnp.where(needed_here, arranged_rows, jnp.zeros((), jnp.bfloat16))
    tile_send = arranged_rows.reshape(blocks_here * key_rows, ctx_size, 2 * HEAD_SIZE)
    fetched = lax.all_to_all(tile_send, "ctx", split_axis=1, concat_axis=1, tiled=True)
    fetched = fetched.reshape(blocks_here, key_rows, ctx_size, 2 * HEAD_SIZE)
    maxima_parts = []
    totals_parts = []
    weighted_parts = []
    for index_of_block in range(q_blocks):
        block_ids = picks_here[index_of_block][my_head]
        owner_rank = block_ids // blocks_here
        slot_index = block_ids % blocks_here
        picked = jnp.stack(
            [
                lax.dynamic_slice(
                    fetched,
                    (slot_index[n], 0, owner_rank[n], 0),
                    (1, key_rows, 1, 2 * HEAD_SIZE),
                )[0, :, 0]
                for n in range(CHOSEN_BLOCKS)
            ]
        )
        sel_keys = picked[..., :HEAD_SIZE].reshape(CHOSEN_BLOCKS * key_rows, HEAD_SIZE)
        sel_values = picked[..., HEAD_SIZE:].reshape(CHOSEN_BLOCKS * key_rows, HEAD_SIZE)
        first_source = index_of_block * per_block
        own_pairs = pair_recv[:, first_source : first_source + per_block]
        own_keys = own_pairs[..., :HEAD_SIZE].reshape(own_rows * per_block, HEAD_SIZE)
        own_values = own_pairs[..., HEAD_SIZE:].reshape(own_rows * per_block, HEAD_SIZE)
        query_rows = query_recv[:, first_source : first_source + per_block].reshape(
            tok_rows * per_block * per_value_head, HEAD_SIZE
        )
        sources = first_source + jnp.arange(per_block, dtype=jnp.int32)
        query_token = sources[None, :] * tok_rows + jnp.arange(tok_rows, dtype=jnp.int32)[:, None]
        query_token = jnp.broadcast_to(
            query_token[:, :, None], (tok_rows, per_block, per_value_head)
        ).reshape(-1)
        key_token = (
            sources[None, :] * tok_rows
            + my_rank * own_rows
            + jnp.arange(own_rows, dtype=jnp.int32)[:, None]
        )
        key_token = key_token.reshape(-1)
        sel_scores = (
            jnp.dot(query_rows, sel_keys.T, preferred_element_type=jnp.float32) * score_scale
        )
        own_scores = (
            jnp.dot(query_rows, own_keys.T, preferred_element_type=jnp.float32) * score_scale
        )
        causal = key_token[None, :] <= query_token[:, None]
        own_scores = jnp.where(causal, own_scores, -jnp.inf)
        maxima = jnp.maximum(jnp.max(sel_scores, axis=1), jnp.max(own_scores, axis=1))
        sel_weights = jnp.exp(sel_scores - maxima[:, None])
        own_weights = jnp.exp(own_scores - maxima[:, None])
        totals = jnp.sum(sel_weights, axis=1) + jnp.sum(own_weights, axis=1)
        weighted = jnp.dot(
            sel_weights, sel_values.astype(jnp.float32), precision=lax.Precision.HIGHEST
        )
        weighted = weighted + jnp.dot(
            own_weights, own_values.astype(jnp.float32), precision=lax.Precision.HIGHEST
        )
        maxima_parts.append(maxima.reshape(tok_rows, per_block, per_value_head))
        totals_parts.append(totals.reshape(tok_rows, per_block, per_value_head))
        weighted_parts.append(weighted.reshape(tok_rows, per_block, per_value_head, HEAD_SIZE))
    maxima_all = jnp.concatenate(maxima_parts, axis=1)
    totals_all = jnp.concatenate(totals_parts, axis=1)
    weighted_all = jnp.concatenate(weighted_parts, axis=1)
    current = (maxima_all, totals_all, weighted_all)
    bit_count = members.bit_length() - 1
    for bit_index in reversed(range(bit_count)):
        half_rows = current[0].shape[0] // 2
        my_bit = my_index // 2**bit_index % 2
        kept = tuple(
            (
                lax.dynamic_slice_in_dim(part_array, my_bit * half_rows, half_rows, 0)
                for part_array in current
            )
        )
        given = tuple(
            (
                lax.dynamic_slice_in_dim(part_array, (1 - my_bit) * half_rows, half_rows, 0)
                for part_array in current
            )
        )
        partner = swapped((given[0], given[1], given[2]), "ctx", bit_index)
        current = combine(kept, partner)
    finished = (
        (current[2] / current[1][..., None])
        .astype(jnp.bfloat16)
        .reshape(own_rows, ctx_size, per_value_head * HEAD_SIZE)
    )
    returned = lax.all_to_all(finished, "ctx", split_axis=1, concat_axis=1, tiled=True)
    context = (
        returned.reshape(own_rows, kv_heads, members, per_value_head * HEAD_SIZE)
        .transpose(2, 0, 1, 3)
        .reshape(tok_rows, q_heads * HEAD_SIZE)
    )
    handed = passed_along(context, "segment", 1)
    return handed[None]


LOG2E = 1.4426950408889634
MESH = pl.DeviceIdType.MESH
PAIR = 2
NOTHING = -1e29
HIDDEN = 1e30
SCALE2 = LOG2E * HEAD_SIZE ** (-0.5)


def turned(block, cosine, sine):
    wide = block.astype(jnp.float32)
    other = pltpu.roll(wide, HEAD_SIZE // 2, 1)
    return (wide * cosine + other * sine).astype(jnp.bfloat16)


def widened(column, count):
    return jnp.concatenate([column] * count, axis=1)


def fold(query, keys, values, shift, causal, first, acc, top):
    scores = lax.dot_general(
        query, keys, (((1,), (1,)), ((), ())), preferred_element_type=jnp.float32
    )
    if causal is not None:
        scores = jnp.where(causal, scores, -jnp.inf)
    new = jnp.max(scores, axis=1, keepdims=True) * SCALE2
    if shift is not None:
        new = new - shift
    new = jnp.broadcast_to(new, (scores.shape[0], HEAD_SIZE))
    if first:
        new = jnp.maximum(new, NOTHING)
    else:
        held = top[...]
        new = jnp.maximum(new, held)
    taken = new if shift is None else new + shift
    weights = jnp.exp2(scores * SCALE2 - widened(taken, scores.shape[1] // HEAD_SIZE))
    part = jnp.dot(weights.astype(jnp.bfloat16), values, preferred_element_type=jnp.float32)
    if first:
        acc[...] = part
    else:
        acc[...] = acc[...] * widened(jnp.exp2(held - new), 2) + part
    top[...] = new


def diagonal():
    rows = lax.broadcasted_iota(jnp.int32, (HEAD_SIZE, HEAD_SIZE), 0)
    columns = lax.broadcasted_iota(jnp.int32, (HEAD_SIZE, HEAD_SIZE), 1)
    return rows == columns


def closed(acc, top):
    totals = jnp.maximum(acc[:, HEAD_SIZE:], 1e-30)
    context = acc[:, :HEAD_SIZE] / totals
    logs = top[...] + jnp.log2(totals)
    eye = diagonal()
    lines = [
        jnp.sum(
            jnp.where(eye, logs[r : r + HEAD_SIZE], 0.0), axis=0, keepdims=True
        )
        for r in range(0, logs.shape[0], HEAD_SIZE)
    ]
    return context, jnp.concatenate(lines, axis=0)


def merged(own, own_logs, other, other_logs):
    most = jnp.maximum(own_logs, other_logs)
    mine = jnp.exp2(own_logs - most)
    total = mine + jnp.exp2(other_logs - most)
    share = mine / total
    eye = diagonal()
    columns = [
        jnp.broadcast_to(
            jnp.sum(
                jnp.where(eye, share[r : r + 1], 0.0), axis=1, keepdims=True
            ),
            (HEAD_SIZE, HEAD_SIZE),
        )
        for r in range(share.shape[0])
    ]
    other = other.astype(jnp.float32)
    return other + jnp.concatenate(columns, axis=0) * (own - other), most + jnp.log2(total)


def turn_kernel(q_ref, cos_ref, sin_ref, early_ref, last_ref):
    tokens = q_ref.shape[1]
    for h in range(q_ref.shape[2] // HEAD_SIZE):
        spot = slice(h % PAIR * tokens, (h % PAIR + 1) * tokens)
        rows = turned(
            q_ref[0, :, h * HEAD_SIZE : (h + 1) * HEAD_SIZE], cos_ref[...], sin_ref[...]
        )
        if h // PAIR < early_ref.shape[0]:
            early_ref[h // PAIR, spot] = rows
        else:
            last_ref[0, spot] = rows


def home_kernel(
    chosen_ref, span_ref, cos_ref, sin_ref, early_ref, last_ref, cache_ref, out_ref,
    acc, top, values, held, made, q_ref, load_sem, store_sem, q_sem,
):
    me = lax.axis_index("ctx")
    tokens = cos_ref.shape[0]
    kv_heads = cache_ref.shape[2] // HEAD_SIZE
    halves = q_ref.shape[0] // kv_heads
    blocks_here = cache_ref.shape[1] // BLOCK_TOKENS

    def load(g):
        spot = pl.ds(pl.multiple_of(g * HEAD_SIZE, HEAD_SIZE), HEAD_SIZE)
        return pltpu.make_async_copy(cache_ref.at[:, :, spot], held.at[g], load_sem.at[g])

    def store(g):
        lines = pl.ds(g * halves, halves)
        return pltpu.make_async_copy(made.at[lines], out_ref.at[lines], store_sem.at[g])

    early = early_ref.shape[0]
    q_loads = (
        pltpu.make_async_copy(early_ref, q_ref.at[pl.ds(0, early)], q_sem.at[0]),
        pltpu.make_async_copy(last_ref, q_ref.at[pl.ds(early, 1)], q_sem.at[1]),
    )
    for copy in q_loads:
        copy.start()
    for g in range(kv_heads):
        load(g).start()
    values[:, HEAD_SIZE:] = jnp.ones((tokens, HEAD_SIZE), values.dtype)

    for copy in q_loads:
        copy.wait()

    @pl.loop(0, kv_heads)
    def _(g):
        spot = pl.ds(pl.multiple_of(g * HEAD_SIZE, HEAD_SIZE), HEAD_SIZE)
        values[:, :HEAD_SIZE] = span_ref[1, :, spot]
        own_keys = turned(span_ref[0, :, spot], cos_ref[...], sin_ref[...])
        rows = lax.broadcasted_iota(jnp.int32, (tokens, tokens), 0)
        columns = lax.broadcasted_iota(jnp.int32, (tokens, tokens), 1)
        causal = jnp.concatenate([columns <= rows] * PAIR, axis=0)
        for i in range(halves):
            fold(q_ref[g * halves + i], own_keys, values[...], None, causal, True, acc.at[i], top.at[i])
        load(g).wait()

        @pl.loop(0, CHOSEN_BLOCKS)
        def _(n):
            block = chosen_ref[(me * kv_heads + g) * CHOSEN_BLOCKS + n] - me * blocks_here

            @pl.when((block >= 0) & (block < blocks_here))
            def _():
                lines = pl.ds(pl.multiple_of(block * BLOCK_TOKENS, BLOCK_TOKENS), BLOCK_TOKENS)
                values[:, :HEAD_SIZE] = held[g, 1, lines]
                for i in range(halves):
                    fold(
                        q_ref[g * halves + i], held[g, 0, lines], values[...], None, None, False,
                        acc.at[i], top.at[i],
                    )

        for i in range(halves):
            context, logs = closed(acc[i], top[i])
            made[g * halves + i, : context.shape[0]] = context
            made[g * halves + i, context.shape[0] :] = logs
        store(g).start()

    for g in range(kv_heads):
        store(g).wait()


def relay_kernel(
    n_seg, chosen_ref, own_hbm_ref, cache_ref, q_ref, ql_ref, qr_ref, out_ref,
    q_buf, k_buf, v_buf, buf, logs, stash, stash_logs, own_ref, acc, top,
    load_sem, q_send, q_recv, last_send, p_send, p_recv, l_send, l_recv, o_send, o_recv,
):
    me = lax.axis_index("ctx")
    seg = lax.axis_index("segment")
    side = me // 2
    ahead = 1 - 2 * side
    is_mid = (me == 1) | (me == 2)
    is_end = (me == 0) | (me == 3)
    forth, back = side, 1 - side
    kv_heads, slots = k_buf.shape[0], k_buf.shape[1]
    chunks, rows = own_ref.shape[0], q_ref.shape[1]
    last = chunks - 1
    tokens = rows // PAIR
    halves = chunks // kv_heads
    blocks_here = slots // BLOCK_TOKENS
    after = lax.rem(seg + 1, n_seg)
    before = lax.rem(seg + n_seg - 1, n_seg)

    def hidden(b, g, j):
        amount = jnp.float32(HIDDEN)
        for n in range(CHOSEN_BLOCKS):
            block = chosen_ref[(b * kv_heads + g) * CHOSEN_BLOCKS + n]
            amount = jnp.where(block == me * blocks_here + j, jnp.float32(0.0), amount)
        return amount

    def seen(b):
        return b * ahead + 3 * side

    def load(i, source, target):
        return pltpu.make_async_copy(source, target, load_sem.at[i])

    def head_loads(g):
        spot = pl.ds(pl.multiple_of(g * HEAD_SIZE, HEAD_SIZE), HEAD_SIZE)
        return (
            load(2 * g, cache_ref.at[0, :, spot], k_buf.at[g]),
            load(2 * g + 1, cache_ref.at[1, :, spot], v_buf.at[g, :, pl.ds(0, HEAD_SIZE)]),
        )

    loads = []
    for g in range(kv_heads):
        loads.append(head_loads(g))
    from_left = load(2 * kv_heads, ql_ref, q_buf.at[lax.max(me - 1, 0), pl.ds(0, last)])
    from_right = load(2 * kv_heads + 1, qr_ref, q_buf.at[lax.min(me + 1, 3), pl.ds(0, last)])
    for copy in loads[0]:
        copy.start()

    @pl.when(me > 0)
    def _():
        from_left.start()

    @pl.when(me < 3)
    def _():
        from_right.start()

    for copies in loads[1:]:
        for copy in copies:
            copy.start()

    own_load = load(2 * kv_heads + 2, own_hbm_ref, own_ref)
    own_load.start()
    barrier = pltpu.get_barrier_semaphore()

    def greet(**place):
        pl.semaphore_signal(barrier, inc=1, device_id=place, device_id_type=MESH)

    @pl.when(me > 0)
    def _():
        greet(ctx=me - 1)

    @pl.when(me < 3)
    def _():
        greet(ctx=me + 1)

    others = (after,) if n_seg == 2 else (after, before)
    for other in others:
        greet(segment=other)

    for g in range(kv_heads):
        v_buf[g, :, HEAD_SIZE:] = jnp.ones((slots, HEAD_SIZE), v_buf.dtype)

    @pl.when(is_mid)
    def _():
        pl.semaphore_wait(barrier, 2 + len(others))

    @pl.when(is_end)
    def _():
        pl.semaphore_wait(barrier, 1 + len(others))

    def q_copy(source, b, k, target):
        return pltpu.make_async_remote_copy(
            src_ref=source,
            dst_ref=q_buf.at[b, k],
            send_sem=q_send.at[b, k],
            recv_sem=q_recv.at[b, k],
            device_id={"ctx": target},
            device_id_type=MESH,
        )

    def second_hops(k, left_source, right_source):
        left = q_copy(left_source, lax.min(me + 1, 3), k, lax.max(me - 1, 0))
        right = q_copy(right_source, lax.max(me - 1, 0), k, lax.min(me + 1, 3))
        return left, right

    def early_hops(k):
        return second_hops(k, qr_ref.at[k], ql_ref.at[k])

    def late_hops():
        return second_hops(
            last, q_buf.at[lax.min(me + 1, 3), last], q_buf.at[lax.max(me - 1, 0), last]
        )

    def last_hop(way, target):
        return pltpu.make_async_remote_copy(
            src_ref=q_ref.at[0],
            dst_ref=q_buf.at[me, last],
            send_sem=last_send.at[way],
            recv_sem=q_recv.at[me, last],
            device_id={"ctx": target},
            device_id_type=MESH,
        )

    def third_hop(k):
        b = seen(3)
        return q_copy(q_buf.at[b, k], b, k, me - ahead)

    def part_copies(way, p, k, target):
        return (
            pltpu.make_async_remote_copy(
                src_ref=buf.at[way, p, k],
                dst_ref=buf.at[way, p, k],
                send_sem=p_send.at[way, p, k],
                recv_sem=p_recv.at[way, p, k],
                device_id={"ctx": target},
                device_id_type=MESH,
            ),
            pltpu.make_async_remote_copy(
                src_ref=logs.at[way, p, k],
                dst_ref=logs.at[way, p, k],
                send_sem=l_send.at[way, p, k],
                recv_sem=l_recv.at[way, p, k],
                device_id={"ctx": target},
                device_id_type=MESH,
            ),
        )

    def arrived(way, p, k):
        for copy in part_copies(way, p, k, me + ahead):
            copy.wait_recv()

    def send(way, p, k, target):
        for copy in part_copies(way, p, k, target):
            copy.start()

    def out_copies(way, p, k):
        return [
            pltpu.make_async_remote_copy(
                src_ref=buf.at[way, p, k, pl.ds(i * tokens, tokens)],
                dst_ref=out_ref.at[
                    0,
                    :,
                    pl.ds(pl.multiple_of((k * PAIR + i) * HEAD_SIZE, HEAD_SIZE), HEAD_SIZE),
                ],
                send_sem=o_send.at[k, i],
                recv_sem=o_recv.at[k, i],
                device_id={"segment": after},
                device_id_type=MESH,
            )
            for i in range(PAIR)
        ]

    def relay(way, p, k, own, own_log, target):
        arrived(way, p, k)
        value, log = merged(own, own_log, buf[way, p, k], logs[way, p, k])
        buf[way, p, k] = value.astype(buf.dtype)
        logs[way, p, k] = log
        send(way, p, k, target)

    def near(u):
        p, k = u // chunks, lax.rem(u, chunks)
        relay(forth, p, k, stash[p - 1, k], stash_logs[p - 1, k], me + ahead)

    def mid_final(k):
        arrived(forth, 0, k)
        arrived(back, 1, k)
        value, log = merged(own_ref[k, :rows], own_ref[k, rows:], buf[forth, 0, k], logs[forth, 0, k])
        value, log = merged(value, log, buf[back, 1, k], logs[back, 1, k])
        buf[back, 1, k] = value.astype(buf.dtype)
        for copy in out_copies(back, 1, k):
            copy.start()

    def end_final(k):
        arrived(back, 2, k)
        value, log = merged(own_ref[k, :rows], own_ref[k, rows:], buf[back, 2, k], logs[back, 2, k])
        buf[back, 2, k] = value.astype(buf.dtype)
        for copy in out_copies(back, 2, k):
            copy.start()

    @pl.when(is_mid)
    def _():
        @pl.loop(0, last)
        def _(k):
            for copy in early_hops(k):
                copy.start()

            @pl.when(k == 1)
            def _():
                last_hop(0, me + ahead).start()
                last_hop(1, me - ahead).start()

    @pl.when(is_end)
    def _():
        last_hop(0, me + ahead).start()

    @pl.when(me > 0)
    def _():
        from_left.wait()

    @pl.when(me < 3)
    def _():
        from_right.wait()

    steps, lead = 3 * chunks, chunks // 2

    @pl.loop(0, steps)
    def _(t):
        late = t - lead
        place = jnp.where(
            is_mid,
            lax.rem(t // chunks + 2, 4),
            jnp.where((late < 0) | (late >= 2 * chunks), 1, 2 + late // chunks),
        )
        k = jnp.where(
            is_mid,
            lax.rem(t, chunks),
            jnp.where(late < 0, t, jnp.where(late < 2 * chunks, lax.rem(late + chunks, chunks), t - 2 * chunks)),
        )
        g = k // halves
        b = seen(place)

        @pl.when((t < chunks) & is_mid & (lax.rem(t, halves) == 0))
        def _():
            for copy in head_loads(g):
                copy.wait()

        @pl.when(is_end & (lax.rem(t, halves) == 0) & ((t < lead) | ((t >= 2 * lead) & (t < chunks + lead))))
        def _():
            for copy in head_loads(g):
                copy.wait()

        @pl.when(is_end & (late >= 0) & ((late < 2 * chunks) | (t == steps - 1)))
        def _():
            q_copy(q_buf.at[b, k], b, k, me + ahead).wait_recv()

        @pl.when(is_mid & (t >= 3) & (t < chunks + 3))
        def _():
            copy = third_hop(t - 3)
            copy.wait_recv()
            copy.start()

        @pl.when(t == chunks)
        def _():
            own_load.wait()

        @pl.when(is_mid & (t == 3))
        def _():
            left, right = late_hops()
            q_copy(q_ref.at[0], lax.min(me + 1, 3), last, me + ahead).wait_recv()
            q_copy(q_ref.at[0], lax.max(me - 1, 0), last, me + ahead).wait_recv()
            left.start()
            right.start()

        query = q_buf[b, k]
        for j in range(blocks_here):
            lines = slice(j * BLOCK_TOKENS, (j + 1) * BLOCK_TOKENS)
            fold(
                query, k_buf[g, lines], v_buf[g, lines],
                hidden(b, g, j), None, j == 0, acc, top,
            )
        context, log = closed(acc[...], top[...])

        @pl.when(is_end)
        def _():
            buf[forth, place - 1, k] = context.astype(buf.dtype)
            logs[forth, place - 1, k] = log
            send(forth, place - 1, k, me + ahead)

        @pl.when(is_mid & (t < 2 * chunks))
        def _():
            stash[t // chunks, k] = context
            stash_logs[t // chunks, k] = log

        @pl.when(is_mid & (t >= 2 * chunks))
        def _():
            relay(back, 2, k, context, log, me - ahead)

        @pl.when(is_mid & (t + 2 >= chunks) & (t + 2 < 3 * chunks))
        def _():
            near(t + 2)

        @pl.when(is_mid & (t >= chunks + 2) & (t < chunks + 2 + lead))
        def _():
            mid_final(t - chunks - 2)

        @pl.when(is_mid & (t >= 2 * chunks + 3 + lead))
        def _():
            mid_final(t - 2 * chunks - 3)

        @pl.when(is_end & (t >= 2 * chunks + 3))
        def _():
            end_final(t - 2 * chunks - 3)

    @pl.when(is_mid)
    def _():
        @pl.loop(chunks - 3, chunks)
        def _(k):
            mid_final(k)

    @pl.when(is_end)
    def _():
        @pl.loop(chunks - 3, chunks)
        def _(k):
            end_final(k)

    last_hop(0, me + ahead).wait_send()

    @pl.when(is_mid)
    def _():
        last_hop(1, me - ahead).wait_send()

    @pl.when(is_mid)
    def _():
        @pl.loop(0, chunks)
        def _(k):
            for copy in second_hops(k, q_ref.at[0], q_ref.at[0]) + (third_hop(k),):
                copy.wait_send()
            for copy in part_copies(forth, 1, k, me + ahead) + part_copies(forth, 2, k, me + ahead):
                copy.wait_send()
            for copy in part_copies(back, 2, k, me - ahead):
                copy.wait_send()
            for copy in out_copies(back, 1, k):
                copy.wait()

    @pl.when(is_end)
    def _():
        @pl.loop(0, chunks)
        def _(k):
            for p in range(3):
                for copy in part_copies(forth, p, k, me + ahead):
                    copy.wait_send()
            for copy in out_copies(back, 2, k):
                copy.wait()


def local(queries, span_key_values, key_value_cache, chosen, offset):
    n_ctx = lax.axis_size("ctx")
    n_seg = lax.axis_size("segment")
    me = lax.axis_index("ctx")
    tokens = queries.shape[1]
    kv_heads = key_value_cache.shape[3] // HEAD_SIZE
    q_heads = queries.shape[2] // HEAD_SIZE
    per_head = q_heads // kv_heads
    slots = key_value_cache.shape[1]
    blocks_here = slots // BLOCK_TOKENS
    if not (
        n_ctx == 4
        and tokens == BLOCK_TOKENS
        and n_seg > 1
        and per_head % PAIR == 0
        and slots * kv_heads <= 16384
        and q_heads == 8 * PAIR
        and kv_heads == 4
    ):
        return general(queries, span_key_values, key_value_cache, chosen, offset)
    bf16, f32 = jnp.bfloat16, jnp.float32
    dma = pltpu.SemaphoreType.DMA
    chunks, rows = q_heads // PAIR, PAIR * tokens
    lines = rows // HEAD_SIZE
    vmem = pl.BlockSpec(memory_space=pltpu.VMEM)
    smem = pl.BlockSpec(memory_space=pltpu.SMEM)
    anywhere = pl.BlockSpec(memory_space=pl.ANY)

    positions = (offset[0] + me * tokens + jnp.arange(tokens, dtype=jnp.int32)).astype(f32)
    half = HEAD_SIZE // 2
    frequencies = ROPE_BASE ** (-(2.0 * jnp.arange(half, dtype=f32)) / HEAD_SIZE)
    angles = positions[:, None] * frequencies[None, :]
    cosine, sine = jnp.cos(angles), jnp.sin(angles)
    cos_table = jnp.concatenate([cosine, cosine], axis=1)
    sin_table = jnp.concatenate([-sine, sine], axis=1)
    q_early, q_last = pl.pallas_call(
        turn_kernel,
        out_shape=(
            jax.ShapeDtypeStruct((chunks - 1, rows, HEAD_SIZE), bf16),
            jax.ShapeDtypeStruct((1, rows, HEAD_SIZE), bf16),
        ),
        in_specs=[vmem] * 3,
        out_specs=(vmem, vmem),
        cost_estimate=pl.CostEstimate(
            flops=6 * queries.size, bytes_accessed=4 * queries.size, transcendentals=0
        ),
        compiler_params=pltpu.CompilerParams(vmem_limit_bytes=24 * 2**20),
    )(queries, cos_table, sin_table)
    q_left = lax.ppermute(q_early, "ctx", [(i, i + 1) for i in range(n_ctx - 1)])
    q_right = lax.ppermute(q_early, "ctx", [(i + 1, i) for i in range(n_ctx - 1)])

    cache = key_value_cache[0].transpose(1, 0, 2)
    span = span_key_values[0].transpose(1, 0, 2)
    picks = chosen.reshape(-1)
    work = 4 * q_heads * tokens * BLOCK_TOKENS * HEAD_SIZE
    own = pl.pallas_call(
        home_kernel,
        out_shape=jax.ShapeDtypeStruct((chunks, rows + lines, HEAD_SIZE), f32),
        in_specs=[smem] + [vmem] * 3 + [anywhere] * 3,
        out_specs=anywhere,
        scratch_shapes=[
            pltpu.VMEM((chunks // kv_heads, rows, 2 * HEAD_SIZE), f32),
            pltpu.VMEM((chunks // kv_heads, rows, HEAD_SIZE), f32),
            pltpu.VMEM((tokens, 2 * HEAD_SIZE), bf16),
            pltpu.VMEM((kv_heads, 2, slots, HEAD_SIZE), bf16),
            pltpu.VMEM((chunks, rows + lines, HEAD_SIZE), f32),
            pltpu.VMEM((chunks, rows, HEAD_SIZE), bf16),
            dma((kv_heads,)),
            dma((kv_heads,)),
            dma((2,)),
        ],
        cost_estimate=pl.CostEstimate(
            flops=6 * work, bytes_accessed=16 * 2**20, transcendentals=work // 128
        ),
        compiler_params=pltpu.CompilerParams(vmem_limit_bytes=48 * 2**20),
    )(picks, span, cos_table, sin_table, q_early, q_last, cache)

    return pl.pallas_call(
        functools.partial(relay_kernel, n_seg),
        out_shape=jax.ShapeDtypeStruct(queries.shape, bf16),
        in_specs=[smem] + [anywhere] * 5,
        out_specs=anywhere,
        scratch_shapes=[
            pltpu.VMEM((n_ctx, chunks, rows, HEAD_SIZE), bf16),
            pltpu.VMEM((kv_heads, slots, HEAD_SIZE), bf16),
            pltpu.VMEM((kv_heads, slots, 2 * HEAD_SIZE), bf16),
            pltpu.VMEM((2, 3, chunks, rows, HEAD_SIZE), bf16),
            pltpu.VMEM((2, 3, chunks, lines, HEAD_SIZE), f32),
            pltpu.VMEM((2, chunks, rows, HEAD_SIZE), f32),
            pltpu.VMEM((2, chunks, lines, HEAD_SIZE), f32),
            pltpu.VMEM((chunks, rows + lines, HEAD_SIZE), f32),
            pltpu.VMEM((rows, 2 * HEAD_SIZE), f32),
            pltpu.VMEM((rows, HEAD_SIZE), f32),
            dma((2 * kv_heads + 3,)),
            dma((n_ctx, chunks)),
            dma((n_ctx, chunks)),
            dma((2,)),
            dma((2, 3, chunks)),
            dma((2, 3, chunks)),
            dma((2, 3, chunks)),
            dma((2, 3, chunks)),
            dma((chunks, PAIR)),
            dma((chunks, PAIR)),
        ],
        cost_estimate=pl.CostEstimate(
            flops=24 * work, bytes_accessed=32 * 2**20, transcendentals=work // 16
        ),
        compiler_params=pltpu.CompilerParams(
            collective_id=0, has_side_effects=True, vmem_limit_bytes=60 * 2**20
        ),
    )(picks, own, cache, q_last, q_left, q_right)


def solution(mesh):
    return jax.shard_map(
        local,
        mesh=mesh,
        in_specs=(
            P(("groups", "segment"), "ctx", "head"),
            P(("groups", "segment"), "ctx", None, "head"),
            P(("groups", "segment"), "ctx", None, "head"),
            P(("groups", "segment"), None, "head", None),
            P(("groups", "segment")),
        ),
        out_specs=P(("groups", "segment"), "ctx", "head"),
        check_vma=False,
    )
```
